128 devices in a mesh: rep: 32 (over y, z, core), shard: 4 (over x).
Axes of the slice: x: 4, y: 4, z: 4, core: 2. Of those that a mesh axis runs over, the one named last changes fastest.
Arguments:
- hidden: bfloat16 [128, 256, 768], P('rep', 'shard'), may hold values from -6 to 6
- grad_out: bfloat16 [128, 256, 768], P('rep', 'shard'), may hold values from -6 to 6
- lengths: int32 [128], P('rep'), may hold values from 1 to 256, 20480 in all
- bucket: int32 [511], replicated, may hold values from 1 to 511, as said below
- w_query: bfloat16 [768, 768], P('shard'), may hold values from -0.21875 to 0.21875
- w_key: bfloat16 [768, 768], P('shard'), may hold values from -0.21875 to 0.21875
- w_value: bfloat16 [768, 768], P('shard'), may hold values from -0.21875 to 0.21875
- w_out: bfloat16 [768, 768], P('shard'), may hold values from -1.25 to 1.25
- w_inner: bfloat16 [768, 3072], P('shard'), may hold values from -0.21875 to 0.21875
- w_outer: bfloat16 [3072, 768], P('shard'), may hold values from -0.109375 to 0.109375
- rel_table: bfloat16 [512, 768], P('shard'), may hold values from -6 to 6
- ln1_gain: bfloat16 [768], P('shard'), may hold values from 0.5 to 1.5
- ln1_bias: bfloat16 [768], P('shard'), may hold values from -1.5 to 1.5
- ln2_gain: bfloat16 [768], P('shard'), may hold values from 0.5 to 1.5
- ln2_bias: bfloat16 [768], P('shard'), may hold values from -1.5 to 1.5
Outputs:
- layer_output: bfloat16 [128, 256, 768], P('rep', 'shard')
- grad_hidden: bfloat16 [128, 256, 768], P('rep', 'shard')
- grad_w_query: float32 [768, 768], P('shard')
- grad_w_key: float32 [768, 768], P('shard')
- grad_w_value: float32 [768, 768], P('shard')
- grad_w_out: float32 [768, 768], P('shard')
- grad_w_inner: float32 [768, 3072], P('shard')
- grad_w_outer: float32 [3072, 768], P('shard')
- grad_rel_table: float32 [512, 768], P('shard')
- grad_ln1_gain: float32 [768], P('shard')
- grad_ln1_bias: float32 [768], P('shard')
- grad_ln2_gain: float32 [768], P('shard')
- grad_ln2_bias: float32 [768], P('shard')
- rms_values: float32 [4], replicated
The draws below stay inside these ranges and needn't reach their ends.
Inputs may be any that keep to these rules, and one draw needn't show every extreme that they name: bucket[255 + d] = 256 + d for |d| < 128; beyond that it moves away from 256 monotonically with |d|, symmetric in the sign of d, several offsets sharing a row.
All inputs are finite; a program needn't handle non-finite values. No bound on the sum of `lengths` on one device may be relied on, other than what follows from the above.
Results may differ from the reference program's by a relative error of at most 0.028.
Values may be sent and summed in bfloat16 or wider, within the bound.
No kernel may reach another device: no remote copies, remote signals or barrier semaphores. Data moves between devices by JAX's collectives and lax.ppermute only.
A program may use at most 192 MiB of HBM per device.

```python
import math
from functools import partial
import jax
import jax.numpy as jnp
import numpy as np
from jax import lax

D = 768
HEADS = 12
HEAD_DIM = 64
FF = 3072
REL = 512
LMAX = 256
SEQS = 128


def draw_bucket(key, part):
    half_rows = REL // 2
    middle = min(REL // 4, LMAX // 2)
    target = min(LMAX - 1, half_rows - 1)
    distance = jnp.arange(LMAX, dtype=jnp.int32)
    picks = jax.random.randint(jax.random.fold_in(key, 17), (LMAX,), 0, 2).astype(jnp.int32)
    rises = jnp.where(distance >= middle, picks, 0).astype(jnp.int32)
    climb = jnp.minimum(jnp.cumsum(rises), target - middle)
    climb = jnp.where(distance == LMAX - 1, target - middle, climb)
    magnitude = jnp.where(distance < middle, distance, middle + climb).astype(jnp.int32)
    offsets = jnp.arange(2 * LMAX - 1, dtype=jnp.int32) - (LMAX - 1)
    signs = jnp.where(offsets < 0, -1, 1).astype(jnp.int32)
    return (half_rows + signs * jnp.take(magnitude, jnp.abs(offsets))).astype(jnp.int32)


def block_levels(rng, shape, shards, low, top_value):
    level, own = 1.0, jax.random.fold_in(rng, 6)
    for dim, shards_of in shards:
        steps = jnp.exp(jax.random.uniform(jax.random.fold_in(own, dim), (shards_of,), jnp.float32, low / len(shards), top_value / len(shards)))
        level = level * jnp.repeat(steps, shape[dim] // shards_of).reshape([-1 if axis == dim else 1 for axis in range(len(shape))])
    return level


def split_up(count, total, reach, lean):
    portions = [(1 << 20) // math.isqrt(rank ** lean) + 1 for rank in range(2, count + 1)]
    spare, holding = total - reach - (count - 1), [1] * (count - 1)
    while spare > 0:
        candidates = [i for i in range(count - 1) if holding[i] < reach]
        mass, remaining = sum([portions[i] for i in candidates]), spare
        for i in candidates:
            addition = min(reach - holding[i], max(1, remaining * portions[i] // mass), spare)
            holding[i] = holding[i] + addition
            spare = spare - addition
    return np.array([reach] + holding)


def ragged(rng, number_of, total, limit, slope):
    if number_of == 2:
        one = jax.random.randint(rng, (), max(1, total - limit), min(limit, total - 1) + 1)
        return jnp.stack([one, total - one])
    sizes = jnp.asarray(split_up(number_of, total, limit, slope), jnp.int32)
    couples = (number_of - 1) // 2
    source_of, taker = sizes[1:1 + 2 * couples:2], sizes[2:2 + 2 * couples:2]
    room = jnp.minimum(source_of - 1, limit - taker)
    moved = jax.random.randint(jax.random.fold_in(rng, 1), (couples,), 0, 1 << 20) % (room + 1)
    sizes = sizes.at[1:1 + 2 * couples:2].set(source_of - moved).at[2:2 + 2 * couples:2].set(taker + moved)
    return sizes[jax.random.permutation(jax.random.fold_in(rng, 2), number_of)]


def gaussian(stream_key, dims, width, bound, cuts=(), kind=jnp.bfloat16):
    drawn = jax.random.normal(stream_key, dims, jnp.float32) * width
    if len(cuts) > 0:
        drawn = block_levels(stream_key, dims, cuts, -0.22, 0.18) * drawn
    return jnp.clip(drawn, min=-bound, max=bound).astype(kind)


def setup_inputs(seed: int = 0) -> dict:
    key_list = jax.random.split(jax.random.key(seed), 16)
    hidden = gaussian(key_list[0], (SEQS, LMAX, D), 1.0, 6.0, ((0, 32), (1, 4)))
    grad_out = gaussian(key_list[1], (SEQS, LMAX, D), 1.0, 6.0, ((0, 32), (1, 4)))
    lengths = ragged(key_list[2], SEQS, SEQS * LMAX * 5 // 8, LMAX, 1).astype(jnp.int32)
    bucket = draw_bucket(jax.random.fold_in(key_list[15], 71), 0)
    w_query = gaussian(key_list[4], (D, D), D ** -0.5, 0.21875, ((0, 4),))
    w_key = gaussian(key_list[5], (D, D), D ** -0.5, 0.21875, ((0, 4),))
    w_value = gaussian(key_list[6], (D, D), D ** -0.5, 0.21875, ((0, 4),))
    w_out = gaussian(key_list[7], (D, D), (D // 32) ** -0.5, 1.25, ((0, 4),))
    w_inner = gaussian(key_list[8], (D, FF), D ** -0.5, 0.21875, ((0, 4),))
    w_outer = gaussian(key_list[9], (FF, D), FF ** -0.5, 0.109375, ((0, 4),))
    rel_table = gaussian(key_list[10], (REL, D), 1.0, 6.0, ((0, 4),))
    ln1_gain = jnp.clip(1.0 + 0.1 * jax.random.normal(key_list[11], (D,), jnp.float32), 0.5, 1.5).astype(jnp.bfloat16)
    ln1_bias = gaussian(key_list[12], (D,), 0.3, 1.5, ((0, 4),))
    ln2_gain = jnp.clip(1.0 + 0.1 * jax.random.normal(key_list[13], (D,), jnp.float32), 0.5, 1.5).astype(jnp.bfloat16)
    ln2_bias = gaussian(key_list[14], (D,), 0.3, 1.5, ((0, 4),))
    return {"hidden": hidden, "grad_out": grad_out, "lengths": lengths, "bucket": bucket, "w_query": w_query, "w_key": w_key, "w_value": w_value, "w_out": w_out, "w_inner": w_inner, "w_outer": w_outer, "rel_table": rel_table, "ln1_gain": ln1_gain, "ln1_bias": ln1_bias, "ln2_gain": ln2_gain, "ln2_bias": ln2_bias}


@jax.custom_vjp
def low(v):
    return lax.optimization_barrier(v.astype(jnp.bfloat16)).astype(jnp.float32)

@jax.custom_vjp
def low_back(v):
    return v

def low_keep(v):
    return (low(v), None)

def low_pass(kept, grad):
    return (grad,)

def back_keep(v):
    return (v, None)

def back_low(kept, grad):
    return (low(grad),)
low.defvjp(low_keep, low_pass)
low_back.defvjp(back_keep, back_low)
EPSILON = 1e-07
MASKED = -1e+30

def matmul_high(left, right):
    return jnp.dot(left, right, precision=lax.Precision.HIGHEST, preferred_element_type=jnp.float32)

def split_heads(matrix):
    number = matrix.shape[0]
    return matrix.reshape(number, HEADS, HEAD_DIM).transpose(1, 0, 2)

def join_heads(stacked):
    return stacked.transpose(1, 0, 2).reshape(stacked.shape[1], HEADS * HEAD_DIM)

def layer_norm(values, gain, shift):
    center = values - lax.optimization_barrier(jnp.mean(values, axis=1, keepdims=True))
    inverse = lax.rsqrt(lax.optimization_barrier(jnp.mean(center * center, axis=1, keepdims=True)) + EPSILON)
    return center * inverse * gain + shift

def positions_of(table, w_key, w_query):
    return (low(low_back(matmul_high(table, w_key))), low(low_back(matmul_high(table, w_query))))

def attend_head(pieces, index_table, key_valid):
    query_head, key_head, value_head, posk_head, posq_head = pieces
    scaling = (3.0 * HEAD_DIM) ** (-0.5)
    content = matmul_high(query_head, key_head.T)
    to_pos = low_back(matmul_high(query_head, posk_head.T))
    from_pos = low_back(matmul_high(key_head, posq_head.T))
    to_gather = jnp.take_along_axis(to_pos, index_table, axis=1)
    from_gather = jnp.take_along_axis(from_pos, index_table, axis=1).T
    scores = low_back((content + to_gather + from_gather) * scaling)
    scores = jnp.where(key_valid[None, :], scores, MASKED)
    row_top = lax.optimization_barrier(jnp.max(scores, axis=1, keepdims=True))
    shifted = jnp.exp(scores - row_top)
    probs = shifted / lax.optimization_barrier(jnp.sum(shifted, axis=1, keepdims=True))
    return matmul_high(low(probs), value_head)

def sequence_forward(tokens, weights, positions, length, index_table):
    w_query, w_key, w_value, w_out, w_inner, w_outer, ln1_gain, ln1_bias, ln2_gain, ln2_bias = weights
    pos_key, pos_query = positions
    key_valid = jnp.arange(LMAX, dtype=jnp.int32) < length
    row_mask = key_valid.astype(jnp.float32)[:, None]
    queries = low(low_back(matmul_high(tokens, w_query)))
    keys_all = low(low_back(matmul_high(tokens, w_key)))
    values_all = low(low_back(matmul_high(tokens, w_value)))
    head_fn = jax.checkpoint(partial(attend_head, index_table=index_table, key_valid=key_valid))
    contexts = lax.map(head_fn, (split_heads(queries), split_heads(keys_all), split_heads(values_all), split_heads(pos_key), split_heads(pos_query)))
    context = low(low_back(join_heads(contexts)))
    attn_out = low_back(matmul_high(context, w_out))
    hidden_one = layer_norm(tokens + attn_out, ln1_gain, ln1_bias)
    inner_pre = low_back(matmul_high(low(hidden_one), w_inner))
    ffn_out = low_back(matmul_high(low(jax.nn.gelu(inner_pre, approximate=False)), w_outer))
    layer_full = layer_norm(hidden_one + ffn_out, ln2_gain, ln2_bias) * row_mask
    squares = jnp.stack([jnp.sum(tokens * tokens * row_mask), jnp.sum(attn_out * attn_out * row_mask), jnp.sum(ffn_out * ffn_out * row_mask), jnp.sum(layer_full * layer_full)])
    return (layer_full, squares)

def reference(hidden, grad_out, lengths, bucket, w_query, w_key, w_value, w_out, w_inner, w_outer, rel_table, ln1_gain, ln1_bias, ln2_gain, ln2_bias):
    weights = tuple((weight.astype(jnp.float32) for weight in (w_query, w_key, w_value, w_out, w_inner, w_outer, ln1_gain, ln1_bias, ln2_gain, ln2_bias)))
    table = rel_table.astype(jnp.float32)
    positions, position_back = jax.vjp(positions_of, table, weights[1], weights[0])
    slot_rows = jnp.arange(LMAX, dtype=jnp.int32)
    offsets = slot_rows[:, None] - slot_rows[None, :] + LMAX - 1
    index_table = jnp.take(bucket, offsets).astype(jnp.int32)

    def one_sequence(carry, pieces):
        grad_sums, pos_sums, stat_sums = carry
        tokens, upstream, length = pieces

        def local(tok_in, weight_in, pos_in):
            return sequence_forward(tok_in, weight_in, pos_in, length, index_table)
        layer_full, back_fn, squares = jax.vjp(local, tokens, weights, positions, has_aux=True)
        grad_tokens, grad_weights, grad_pos = back_fn(upstream)
        grad_sums = jax.tree.map(lambda first, second: first + second, grad_sums, grad_weights)
        pos_sums = jax.tree.map(lambda first, second: first + second, pos_sums, grad_pos)
        return ((grad_sums, pos_sums, stat_sums + squares), (layer_full.astype(jnp.bfloat16), grad_tokens.astype(jnp.bfloat16)))
    start = (jax.tree.map(jnp.zeros_like, weights), jax.tree.map(jnp.zeros_like, positions), jnp.zeros((4,), jnp.float32))
    carried, produced = lax.scan(one_sequence, start, (hidden.astype(jnp.float32), grad_out.astype(jnp.float32), lengths))
    grad_sums, pos_sums, stat_sums = carried
    layer_output, grad_hidden = produced
    grad_table, key_extra, query_extra = position_back(pos_sums)
    total_tokens = jnp.sum(lengths).astype(jnp.float32)
    rms_values = jnp.sqrt(stat_sums / (total_tokens * D))
    return (layer_output, grad_hidden, grad_sums[0] + query_extra, grad_sums[1] + key_extra, grad_sums[2], grad_sums[3], grad_sums[4], grad_sums[5], grad_table, grad_sums[6], grad_sums[7], grad_sums[8], grad_sums[9], rms_values)
```

```python
import jax
import jax.numpy as jnp
from jax import lax
from jax.experimental import pallas as pl
from jax.experimental.pallas import tpu as pltpu
from jax.sharding import Mesh
from jax.sharding import PartitionSpec as P

D = 768
HEADS = 12
HEAD_DIM = 64
PAIRS = HEADS // 2
ROWS = 256
OFFS = 512
TOKENS = 20480
GROUP = 4
PIECE = D // GROUP
HALF = PIECE // 2
WIDE = GROUP * D
REL_HALF = OFFS // GROUP // 2
REL_AT = 3 * HALF
FIRST = 3 * HALF + REL_HALF
OUT_AT = D // 2
NORM_AT = D // 2 + HALF
SECOND = D // 2 + HALF + 16
META_LENGTH, META_CORE, META_SLOT, META_KEEP, META_SEND = 0, 1, 2, 6, 10
EPSILON = 1e-07
MASKED = -1e30
SCALING = (3.0 * HEAD_DIM) ** (-0.5)
F32 = jnp.float32
LOW = jnp.bfloat16
MIB = 1024 * 1024


def mm(a, b):
    return lax.dot_general(a, b, (((1,), (0,)), ((), ())), preferred_element_type=F32)


def mm_nt(a, b):
    return lax.dot_general(a, b, (((1,), (1,)), ((), ())), preferred_element_type=F32)


def mm_tn(a, b):
    return lax.dot_general(a, b, (((0,), (0,)), ((), ())), preferred_element_type=F32)


def iota(shape, dim):
    return lax.broadcasted_iota(jnp.int32, shape, dim)


def whole(ref, start, size):
    piece = ref[:, :, start : start + size, :]
    return piece.reshape(GROUP * 2 * size, piece.shape[3])


def run_copies(copies):
    for copy in copies:
        copy.start()
    for copy in copies:
        copy.wait()


def placed(meta_ref, pieces, target, sem, at):
    core = meta_ref[META_CORE]
    near, far, across = (meta_ref[META_SLOT + i] for i in range(3))
    slots = ((near, core), (far, core), (across, core), (far, 1 - core), (near, 1 - core), (across, 1 - core))
    return [
        pltpu.make_async_copy(piece, target(slot, half), sem.at[at + i])
        for i, (piece, (slot, half)) in enumerate(zip(pieces, slots))
    ]


def load_first(meta_ref, own, pieces, w_ref, sem):
    me = meta_ref[META_SLOT + 3]
    copies = placed(meta_ref, pieces, lambda slot, half: w_ref.at[slot, half], sem, 0)
    at = len(copies)
    for half in range(2):
        for i, ref in enumerate(own):
            size = REL_HALF if i == 3 else HALF
            copies.append(
                pltpu.make_async_copy(
                    ref.at[pl.ds(half * size, size)], w_ref.at[me, half, pl.ds(i * HALF, size)], sem.at[at]
                )
            )
            at += 1
    return copies


def split_halves(meta_ref, value, keep_ref, send_ref, shard, rows, cols=slice(None)):
    half = value.shape[0] // 2
    low, high = value[:half].astype(LOW), value[half:].astype(LOW)
    first_core = meta_ref[META_CORE] == 0
    keep_ref[meta_ref[META_KEEP + shard], rows, cols] = jnp.where(first_core, low, high)
    send_ref[meta_ref[META_SEND + shard], rows, cols] = jnp.where(first_core, high, low)


def attend_forward_body(
    meta_ref, tok_ref, bucket_ref, own_q, own_k, own_v, own_rel, p0, p1, p2, p3, p4, p5,
    q_ref, k_ref, v_ref, pk_ref, pq_ref, relw_ref, probs_ref, ctx_ref,
    w_ref, sem,
):
    run_copies(load_first(meta_ref, (own_q, own_k, own_v, own_rel), (p0, p1, p2, p3, p4, p5), w_ref, sem))
    tok = tok_ref[...]
    rel = whole(w_ref, REL_AT, REL_HALF)
    pick = (bucket_ref[...] == iota((OFFS, OFFS), 1)).astype(LOW)
    relw = mm(pick, rel).astype(LOW)
    relw_ref[...] = relw
    w_query = whole(w_ref, 0, HALF)
    q_ref[...] = mm(tok, w_query).astype(LOW)
    pq_ref[...] = mm(relw, w_query).astype(LOW)
    w_key = whole(w_ref, HALF, HALF)
    k_ref[...] = mm(tok, w_key).astype(LOW)
    pk_ref[...] = mm(relw, w_key).astype(LOW)
    v_ref[...] = mm(tok, whole(w_ref, 2 * HALF, HALF)).astype(LOW)
    length = meta_ref[META_LENGTH]
    valid = iota((ROWS, ROWS), 1) < length
    side = iota((ROWS, 2 * HEAD_DIM), 1) // HEAD_DIM

    def pair_step(pair, carry):
        cols = pl.ds(pl.multiple_of(pair * 2 * HEAD_DIM, 2 * HEAD_DIM), 2 * HEAD_DIM)
        q_pair, k_pair, v_pair = q_ref[:, cols], k_ref[:, cols], v_ref[:, cols]
        pk_pair, pq_pair = pk_ref[:, cols], pq_ref[:, cols]
        zero = jnp.zeros_like(q_pair)
        contexts = []
        for h in range(2):
            mine = side == h
            q_head = jnp.where(mine, q_pair, zero)
            k_head = jnp.where(mine, k_pair, zero)
            content = mm_nt(q_head, k_pair)
            to_off = mm_nt(q_head, pk_pair)
            from_off = mm_nt(k_head, pq_pair)
            to_rel = pltpu.roll(to_off, ROWS + 1, 1, stride=1, stride_axis=0)[:, :ROWS]
            from_rel = pltpu.roll(from_off, ROWS + 1, 1, stride=1, stride_axis=0)[:, :ROWS]
            scores = (content + to_rel + from_rel.T) * SCALING
            scores = jnp.where(valid, scores, MASKED)
            top = jnp.max(scores, axis=1, keepdims=True)
            shifted = jnp.exp(scores - top)
            summed = jnp.sum(shifted, axis=1, keepdims=True)
            probs = (shifted * (1.0 / summed)).astype(LOW)
            probs_ref[2 * pair + h] = probs
            contexts.append(mm(probs, v_pair))
        ctx_ref[:, cols] = jnp.where(side == 0, contexts[0], contexts[1]).astype(LOW)
        return carry

    lax.fori_loop(0, PAIRS, pair_step, 0)


def attend_forward(meta, tok, bucket_column, own, pieces):
    shape = jax.ShapeDtypeStruct
    full, anywhere = pl.BlockSpec(memory_space=pltpu.VMEM), pl.BlockSpec(memory_space=pl.ANY)
    return pl.pallas_call(
        attend_forward_body,
        out_shape=(
            shape((ROWS, D), LOW), shape((ROWS, D), LOW), shape((ROWS, D), LOW),
            shape((OFFS, D), LOW), shape((OFFS, D), LOW), shape((OFFS, D), LOW),
            shape((HEADS, ROWS, ROWS), LOW), shape((ROWS, D), LOW),
        ),
        in_specs=[pl.BlockSpec(memory_space=pltpu.SMEM), full, full] + [anywhere] * 10,
        out_specs=(full,) * 8,
        scratch_shapes=[pltpu.VMEM((GROUP, 2, FIRST, D), LOW), pltpu.SemaphoreType.DMA((14,))],
        compiler_params=pltpu.CompilerParams(vmem_limit_bytes=28 * MIB),
        cost_estimate=pl.CostEstimate(flops=8_000_000_000, bytes_accessed=40_000_000, transcendentals=800_000),
        name="attend_forward",
    )(meta, tok, bucket_column, *own, *pieces)


def attend_backward_body(
    meta_ref, q_ref, k_ref, v_ref, pk_ref, pq_ref, relw_ref, probs_ref, gctx_ref, tok_ref, gres_ref, bucket_ref,
    own_q, own_k, own_v, own_rel, p0, p1, p2, p3, p4, p5,
    gtok_ref, keep_ref, send_ref,
    gq_ref, gk_ref, gv_ref, gpk_ref, gpq_ref, qr_ref, kr_ref, w_ref, sem,
):
    copies = load_first(meta_ref, (own_q, own_k, own_v, own_rel), (p0, p1, p2, p3, p4, p5), w_ref, sem)
    for copy in copies:
        copy.start()
    flip = (iota((ROWS, ROWS), 0) + iota((ROWS, ROWS), 1) == ROWS - 1).astype(LOW)
    qr_ref[...] = mm(flip, q_ref[...]).astype(LOW)
    kr_ref[...] = mm(flip, k_ref[...]).astype(LOW)
    side = iota((ROWS, 2 * HEAD_DIM), 1) // HEAD_DIM
    side_off = iota((OFFS, 2 * HEAD_DIM), 1) // HEAD_DIM
    blank = jnp.zeros((ROWS, OFFS - ROWS), F32)

    def pair_step(pair, carry):
        cols = pl.ds(pl.multiple_of(pair * 2 * HEAD_DIM, 2 * HEAD_DIM), 2 * HEAD_DIM)
        q_pair, k_pair, v_pair = q_ref[:, cols], k_ref[:, cols], v_ref[:, cols]
        pk_pair, pq_pair, gctx_pair = pk_ref[:, cols], pq_ref[:, cols], gctx_ref[:, cols]
        qr_pair, kr_pair = qr_ref[:, cols], kr_ref[:, cols]
        zero = jnp.zeros_like(q_pair)
        parts = []
        for h in range(2):
            gctx_head = jnp.where(side == h, gctx_pair, zero)
            grad_probs = mm_nt(gctx_head, v_pair)
            probs_low = probs_ref[2 * pair + h]
            probs = probs_low.astype(F32)
            inner = jnp.sum(probs * grad_probs, axis=1, keepdims=True)
            grad_scores = (probs * (grad_probs - inner)).astype(LOW)
            g_value = mm_tn(probs_low, gctx_pair)
            rows_back = mm(flip, grad_scores)
            cols_back = mm_nt(flip, grad_scores)
            to_off = pltpu.roll(jnp.concatenate([rows_back, blank], axis=1), 0, 1, stride=1, stride_axis=0).astype(LOW)
            from_off = pltpu.roll(jnp.concatenate([cols_back, blank], axis=1), 0, 1, stride=1, stride_axis=0).astype(LOW)
            g_query = mm(rows_back.astype(LOW), k_pair) + mm(to_off, pk_pair)
            g_key = mm(cols_back.astype(LOW), q_pair) + mm(from_off, pq_pair)
            g_pk = mm_tn(to_off, qr_pair)
            g_pq = mm_tn(from_off, kr_pair)
            parts.append((g_value, g_query, g_key, g_pk, g_pq))
        first, second = parts
        gv_ref[:, cols] = jnp.where(side == 0, first[0], second[0]).astype(LOW)
        gq_ref[:, cols] = (jnp.where(side == 0, first[1], second[1]) * SCALING).astype(LOW)
        gk_ref[:, cols] = (jnp.where(side == 0, first[2], second[2]) * SCALING).astype(LOW)
        gpk_ref[:, cols] = (jnp.where(side_off == 0, first[3], second[3]) * SCALING).astype(LOW)
        gpq_ref[:, cols] = (jnp.where(side_off == 0, first[4], second[4]) * SCALING).astype(LOW)
        return carry

    lax.fori_loop(0, PAIRS, pair_step, 0)
    for copy in copies:
        copy.wait()
    tok, relw = tok_ref[...], relw_ref[...]
    g_query = mm(flip, gq_ref[...]).astype(LOW)
    w_query = whole(w_ref, 0, HALF)
    g_tok = gres_ref[...] + mm_nt(g_query, w_query)
    g_rel = mm_nt(gpq_ref[...], w_query)

    def put(start, size, value):
        for shard in range(GROUP):
            rows = value[shard * 2 * size : (shard + 1) * 2 * size]
            split_halves(meta_ref, rows, keep_ref, send_ref, shard, slice(start, start + size))

    put(0, HALF, mm_tn(tok, g_query) + mm_tn(relw, gpq_ref[...]))
    g_key = mm(flip, gk_ref[...]).astype(LOW)
    w_key = whole(w_ref, HALF, HALF)
    g_tok = g_tok + mm_nt(g_key, w_key)
    g_rel = (g_rel + mm_nt(gpk_ref[...], w_key)).astype(LOW)
    put(HALF, HALF, mm_tn(tok, g_key) + mm_tn(relw, gpk_ref[...]))
    g_value = gv_ref[...]
    gtok_ref[...] = (g_tok + mm_nt(g_value, whole(w_ref, 2 * HALF, HALF))).astype(LOW)
    put(2 * HALF, HALF, mm_tn(tok, g_value))
    pick = (bucket_ref[...] == iota((OFFS, OFFS), 1)).astype(LOW)
    put(REL_AT, REL_HALF, mm_tn(pick, g_rel))


def attend_backward(meta, saved, gctx, tok, gres, bucket_column, own, pieces):
    shape = jax.ShapeDtypeStruct
    full, anywhere = pl.BlockSpec(memory_space=pltpu.VMEM), pl.BlockSpec(memory_space=pl.ANY)
    return pl.pallas_call(
        attend_backward_body,
        out_shape=(shape((ROWS, D), LOW), shape((GROUP, FIRST, D), LOW), shape((GROUP, FIRST, D), LOW)),
        in_specs=[pl.BlockSpec(memory_space=pltpu.SMEM)] + [full] * 11 + [anywhere] * 10,
        out_specs=(full,) * 3,
        scratch_shapes=[
            pltpu.VMEM((ROWS, D), LOW), pltpu.VMEM((ROWS, D), LOW), pltpu.VMEM((ROWS, D), LOW),
            pltpu.VMEM((OFFS, D), LOW), pltpu.VMEM((OFFS, D), LOW),
            pltpu.VMEM((ROWS, D), LOW), pltpu.VMEM((ROWS, D), LOW),
            pltpu.VMEM((GROUP, 2, FIRST, D), LOW), pltpu.SemaphoreType.DMA((14,)),
        ],
        compiler_params=pltpu.CompilerParams(vmem_limit_bytes=36 * MIB),
        cost_estimate=pl.CostEstimate(flops=12_000_000_000, bytes_accessed=60_000_000, transcendentals=0),
        name="attend_backward",
    )(meta, *saved, gctx, tok, gres, bucket_column, *own, *pieces)


def feed_body(
    meta_ref, tok_ref, ctx_ref, up_ref, own_outer, own_out, own_norm, own_inner,
    a0, a1, a2, a3, a4, a5, b0, b1, b2, b3, b4, b5,
    out_ref, gctx_ref, gres_ref, keep_ref, send_ref, keep_in_ref, send_in_ref,
    low_ref, act_ref, slope_ref, w_ref, in_ref, sem,
):
    me = meta_ref[META_SLOT + 3]
    copies = placed(meta_ref, (a0, a1, a2, a3, a4, a5), lambda slot, half: w_ref.at[slot, half], sem, 0)
    copies += placed(
        meta_ref, (b0, b1, b2, b3, b4, b5), lambda slot, half: in_ref.at[pl.ds(slot * PIECE + half * HALF, HALF)], sem, 6
    )
    copies.append(pltpu.make_async_copy(own_inner, in_ref.at[pl.ds(me * PIECE, PIECE)], sem.at[12]))
    copies.append(pltpu.make_async_copy(own_norm, w_ref.at[me, 0, pl.ds(NORM_AT, 16)], sem.at[13]))
    for half in range(2):
        copies.append(
            pltpu.make_async_copy(
                own_outer.at[pl.ds(half * (D // 2), D // 2)], w_ref.at[me, half, pl.ds(0, D // 2)], sem.at[14 + half]
            )
        )
        copies.append(
            pltpu.make_async_copy(
                own_out.at[pl.ds(half * HALF, HALF)], w_ref.at[me, half, pl.ds(OUT_AT, HALF)], sem.at[16 + half]
            )
        )
    run_copies(copies)
    length = meta_ref[META_LENGTH]
    mask = (iota((ROWS, 1), 0) < length).astype(F32)
    norm_rows = [w_ref[s, 0, NORM_AT : NORM_AT + 16, :].astype(F32)[:1] for s in range(GROUP)]
    gain_one, bias_one, gain_two, bias_two = (
        jnp.concatenate([row[:, i * PIECE : (i + 1) * PIECE] for row in norm_rows], axis=1) for i in range(4)
    )
    token = tok_ref[...].astype(F32)
    ctx = ctx_ref[...]
    w_out = whole(w_ref, OUT_AT, HALF)
    attn = mm(ctx, w_out)

    def norm(values):
        center = values - jnp.mean(values, axis=1, keepdims=True)
        inverse = lax.rsqrt(jnp.mean(center * center, axis=1, keepdims=True) + EPSILON)
        return center * inverse, inverse

    def norm_back(upstream, normed, inverse, gain):
        scaled = upstream * gain
        plain = jnp.mean(scaled, axis=1, keepdims=True)
        cross = jnp.mean(scaled * normed, axis=1, keepdims=True)
        return inverse * (scaled - plain - normed * cross)

    def total(values):
        return jnp.sum(values, axis=0, keepdims=True)

    normed_one, inverse_one = norm(token + attn)
    hidden_one = normed_one * gain_one + bias_one
    low_ref[...] = hidden_one.astype(LOW)

    def columns(c):
        return pl.ds(pl.multiple_of(c * D, D), D)

    def outer_rows(c):
        return w_ref[c, :, 0 : D // 2, :].reshape(D, D)

    def forward_step(c, ffn):
        inner = mm(low_ref[...], in_ref[:, columns(c)])
        cumulative = 0.5 * (1.0 + lax.erf(inner * 0.5**0.5))
        density = jnp.exp(-0.5 * inner * inner) * 0.3989422804014327
        act = (inner * cumulative).astype(LOW)
        act_ref[c] = act
        slope_ref[c] = cumulative + inner * density
        return ffn + mm(act, outer_rows(c))

    ffn = lax.fori_loop(0, GROUP, forward_step, jnp.zeros((ROWS, D), F32))
    normed_two, inverse_two = norm(hidden_one + ffn)
    layer = (normed_two * gain_two + bias_two) * mask
    out_ref[...] = layer.astype(LOW)
    squares = [token * token * mask, attn * attn * mask, ffn * ffn * mask, layer * layer]
    sums = [jnp.sum(total(s), axis=1, keepdims=True) for s in squares]
    grad_y = up_ref[...].astype(F32) * mask
    grad_gain_two = total(grad_y * normed_two)
    grad_bias_two = total(grad_y)
    grad_two = norm_back(grad_y, normed_two, inverse_two, gain_two)
    grad_ffn = grad_two.astype(LOW)

    def back_step(c, grad_hidden):
        grad_act = mm_nt(grad_ffn, outer_rows(c))
        grad_inner = (grad_act * slope_ref[c]).astype(LOW)
        split_halves(meta_ref, mm_tn(act_ref[c], grad_ffn), keep_ref, send_ref, c, slice(0, D // 2))
        grad_w = mm_tn(low_ref[...], grad_inner)
        for s in range(GROUP):
            rows = grad_w[s * PIECE : (s + 1) * PIECE]
            split_halves(meta_ref, rows, keep_in_ref, send_in_ref, s, slice(None), columns(c))
        return grad_hidden + mm_nt(grad_inner, in_ref[:, columns(c)])

    grad_hidden = lax.fori_loop(0, GROUP, back_step, grad_two)
    grad_gain_one = total(grad_hidden * normed_one)
    grad_bias_one = total(grad_hidden)
    grad_one = norm_back(grad_hidden, normed_one, inverse_one, gain_one)
    gres_ref[...] = grad_one
    grad_attn = grad_one.astype(LOW)
    grad_out = mm_tn(ctx, grad_attn)
    for s in range(GROUP):
        rows = grad_out[s * PIECE : (s + 1) * PIECE]
        split_halves(meta_ref, rows, keep_ref, send_ref, s, slice(OUT_AT, OUT_AT + HALF))
    gctx_ref[...] = mm_nt(grad_attn, w_out).astype(LOW)
    lane = iota((1, D), 1)
    stats = jnp.zeros((1, D), F32)
    for i, value in enumerate(sums):
        stats = jnp.where(lane == i, value, stats)
    low = stats - stats.astype(LOW).astype(F32)
    zeros = jnp.zeros((1, D), F32)
    norm_rows = (grad_gain_one, grad_bias_one, grad_gain_two, grad_bias_two)
    for s in range(GROUP):
        row = jnp.concatenate([r[:, s * PIECE : (s + 1) * PIECE] for r in norm_rows], axis=1)
        block = jnp.concatenate([row] + [zeros] * 15 + [stats, low] + [zeros] * 14, axis=0)
        split_halves(meta_ref, block, keep_ref, send_ref, s, slice(NORM_AT, NORM_AT + 16))


def feed(meta, tok, ctx, up, own, outer_pieces, inner_pieces):
    shape = jax.ShapeDtypeStruct
    full, anywhere = pl.BlockSpec(memory_space=pltpu.VMEM), pl.BlockSpec(memory_space=pl.ANY)
    block, wide = shape((GROUP, SECOND, D), LOW), shape((GROUP, HALF, WIDE), LOW)
    return pl.pallas_call(
        feed_body,
        out_shape=(shape((ROWS, D), LOW), shape((ROWS, D), LOW), shape((ROWS, D), F32), block, block, wide, wide),
        in_specs=[pl.BlockSpec(memory_space=pltpu.SMEM)] + [full] * 3 + [anywhere] * 16,
        out_specs=(full,) * 7,
        scratch_shapes=[
            pltpu.VMEM((ROWS, D), LOW), pltpu.VMEM((GROUP, ROWS, D), LOW), pltpu.VMEM((GROUP, ROWS, D), F32),
            pltpu.VMEM((GROUP, 2, SECOND, D), LOW), pltpu.VMEM((D, WIDE), LOW), pltpu.SemaphoreType.DMA((18,)),
        ],
        compiler_params=pltpu.CompilerParams(vmem_limit_bytes=48 * MIB),
        cost_estimate=pl.CostEstimate(flops=12_000_000_000, bytes_accessed=60_000_000, transcendentals=1_600_000),
        name="feed",
    )(meta, tok, ctx, up, *own, *outer_pieces, *inner_pieces)


def pairs_over(size, flips):
    return [(c, i, c, i ^ flips[c]) for c in range(2) for i in range(size)]


def hop(value, axis, flips):
    if axis == "shard":
        pairs = [(c * 4 + i, d * 4 + j) for c, i, d, j in pairs_over(4, flips)]
        return lax.ppermute(value, ("core", "shard"), pairs)
    pairs = [(i * 2 + c, j * 2 + d) for c, i, d, j in pairs_over(4, flips)]
    return lax.ppermute(value, (axis, "core"), pairs)


NEAR, FAR = (1, 3), (3, 1)


def swap(value):
    return lax.ppermute(value, "core", [(0, 1), (1, 0)])


def spread(half):
    near = hop(half, "shard", NEAR)
    far = hop(half, "shard", FAR)
    across = hop(near, "shard", FAR)
    return near, far, across, swap(near), swap(far), swap(across)


def add(*values):
    total = values[0].astype(F32)
    for value in values[1:]:
        total = total + value.astype(F32)
    return total.astype(LOW)


def reduce_over_all(keep, send):
    other = swap(send)
    first = hop(add(keep[:2], other[:2]), "shard", NEAR)
    second = hop(add(keep[2], other[2], first[0]), "shard", FAR)
    mine = add(keep[3], other[3], first[1], second)
    rows = mine.shape[0] // 2
    parts = []
    for part, order in ((mine[:rows], ("y", "z")), (mine[rows:], ("z", "y"))):
        for axis in order:
            for flips in (NEAR, FAR):
                part = add(part, hop(part, axis, flips))
        parts.append(part)
    mine = jnp.concatenate(parts, axis=0)
    return mine, swap(mine)


def arrange(lengths):
    slots = jnp.arange(GROUP, dtype=jnp.int32)
    longer = (lengths[None, :] > lengths[:, None]) | (lengths[None, :] == lengths[:, None]) & (
        slots[None, :] < slots[:, None]
    )
    dealing = jnp.sum(longer.astype(jnp.int32), axis=1)
    chosen = (dealing[None, :] == slots[:, None]).astype(jnp.int32)
    source_of = jnp.sum(chosen * slots[None, :], axis=1)
    return dealing, source_of


def shards(
    hidden, grad_out, lengths, bucket, w_query, w_key, w_value, w_out, w_inner, w_outer, rel_table,
    ln1_gain, ln1_bias, ln2_gain, ln2_bias,
):
    member = lax.axis_index("shard")
    dealing, source_of = arrange(lengths)
    both = jnp.concatenate([jnp.take(hidden, source_of, axis=0), jnp.take(grad_out, source_of, axis=0)], axis=2)
    arrived = lax.all_to_all(both, "shard", split_axis=0, concat_axis=1, tiled=True)[0]
    tok, up = arrived[:, :D], arrived[:, D:]
    core = lax.axis_index("core")
    length = jnp.sum(jnp.where(dealing == member, lengths, 0))
    near, far = jnp.where(core == 0, 1, 3), jnp.where(core == 0, 3, 1)
    slots = jnp.stack([member ^ near, member ^ far, member ^ 2, member])
    shard_ids = jnp.arange(GROUP, dtype=jnp.int32) ^ member
    table = jnp.array([[3, 1, 0, 2], [3, 2, 0, 1]], jnp.int32)
    keep_at = jnp.take(jnp.take(table, core, axis=0), shard_ids)
    send_at = jnp.take(jnp.take(table, 1 - core, axis=0), shard_ids)
    meta = jnp.concatenate([jnp.stack([length, core]), slots, keep_at, send_at]).astype(jnp.int32)

    def half_of(matrix):
        size = matrix.shape[0] // 2
        return lax.dynamic_slice_in_dim(matrix, core * size, size, 0)

    norm_block = jnp.concatenate(
        [jnp.concatenate([ln1_gain, ln1_bias, ln2_gain, ln2_bias])[None], jnp.zeros((15, D), LOW)], axis=0
    )
    own_first = (w_query, w_key, w_value, rel_table)
    first = spread(jnp.concatenate([half_of(matrix) for matrix in own_first], axis=0))
    outer = spread(jnp.concatenate([half_of(w_outer), half_of(w_out), norm_block], axis=0))
    inner = spread(half_of(w_inner))
    bucket_column = jnp.concatenate([bucket[::-1], jnp.full((1,), -1, jnp.int32)])[:, None]
    *saved, ctx = attend_forward(meta, tok, bucket_column, own_first, first)
    out, gctx, gres, keep, send, keep_in, send_in = feed(
        meta, tok, ctx, up, (w_outer, w_out, norm_block, w_inner), outer, inner
    )
    gtok, keep_first, send_first = attend_backward(meta, saved, gctx, tok, gres, bucket_column, own_first, first)

    def whole_shard(halves):
        mine, other = (half.astype(F32) for half in halves)
        return jnp.where(core == 0, mine, other), jnp.where(core == 0, other, mine)

    def rows(halves, start, size):
        return jnp.concatenate([half[start : start + size] for half in halves], axis=0)

    two = whole_shard(reduce_over_all(keep, send))
    wide = whole_shard(reduce_over_all(keep_in, send_in))
    one = whole_shard(reduce_over_all(keep_first, send_first))
    returned = lax.all_to_all(
        jnp.concatenate([out, gtok], axis=1)[None], "shard", split_axis=1, concat_axis=0, tiled=True
    )
    returned = jnp.take(returned, dealing, axis=0)
    norm_sums = two[0][NORM_AT].reshape(GROUP, PIECE)
    stats = two[1][NORM_AT, :GROUP] + two[1][NORM_AT + 1, :GROUP]
    return (
        returned[:, :, :D],
        returned[:, :, D:],
        rows(one, 0, HALF),
        rows(one, HALF, HALF),
        rows(one, 2 * HALF, HALF),
        rows(two, OUT_AT, HALF),
        rows(wide, 0, HALF),
        rows(two, 0, D // 2),
        rows(one, REL_AT, REL_HALF),
        norm_sums[0],
        norm_sums[1],
        norm_sums[2],
        norm_sums[3],
        jnp.sqrt(stats / (TOKENS * D)),
    )


def solution(mesh):
    split = Mesh(mesh.devices.reshape(4, 4, 2, 4), ("y", "z", "core", "shard"))
    rep = ("y", "z", "core")
    rows, vector = P("shard", None), P("shard")
    batch = P(rep, "shard", None)
    return jax.shard_map(
        shards,
        mesh=split,
        in_specs=(batch, batch, P(rep), P(), *(rows,) * 7, *(vector,) * 4),
        out_specs=(batch, batch, *(rows,) * 7, *(vector,) * 4, P()),
        check_vma=False,
    )
```

```python
import jax
import jax.numpy as jnp
from jax import lax
from jax.experimental import pallas as pl
from jax.experimental.pallas import tpu as pltpu
from jax.sharding import Mesh
from jax.sharding import PartitionSpec as P

D = 768
HEADS = 12
HEAD_DIM = 64
PAIRS = HEADS // 2
ROWS = 256
OFFS = 512
TOKENS = 20480
GROUP = 4
PIECE = D // GROUP
HALF = PIECE // 2
WIDE = GROUP * D
REL_HALF = OFFS // GROUP // 2
REL_AT = 3 * HALF
FIRST = 3 * HALF + REL_HALF
OUT_AT = D // 2
NORM_AT = D // 2 + HALF
QUARTER = 128
SECOND = GROUP * QUARTER
SPAN = QUARTER + HALF
PART = ROWS // GROUP
X, Y, Z, CORE, LENGTH, SEQ = 0, 1, 2, 3, 4, 5
META = 16
EPSILON = 1e-07
MASKED = -1e30
SCALING = (3.0 * HEAD_DIM) ** (-0.5)
F32 = jnp.float32
LOW = jnp.bfloat16
MIB = 1024 * 1024


def mm(a, b):
    return lax.dot_general(a, b, (((1,), (0,)), ((), ())), preferred_element_type=F32)


def mm_nt(a, b):
    return lax.dot_general(a, b, (((1,), (1,)), ((), ())), preferred_element_type=F32)


def mm_tn(a, b):
    return lax.dot_general(a, b, (((0,), (0,)), ((), ())), preferred_element_type=F32)


def iota(shape, dim):
    return lax.broadcasted_iota(jnp.int32, shape, dim)


def whole(ref, start, size):
    piece = ref[:, :, start : start + size, :]
    return piece.reshape(GROUP * 2 * size, piece.shape[3])


def run_copies(copies):
    for copy in copies:
        copy.start()
    for copy in copies:
        copy.wait()


class Copies:
    def __init__(self, sem):
        self.sem, self.made = sem, []

    def add(self, source, target):
        self.made.append(pltpu.make_async_copy(source, target, self.sem.at[len(self.made)]))

    def start(self):
        for copy in self.made:
            copy.start()

    def wait(self):
        for copy in self.made:
            copy.wait()


def near_of(core):
    return 1 + 2 * core


def far_of(core):
    return 3 - 2 * core


def assist_of(meta_ref, core):
    return jnp.where(core == 0, meta_ref[Y], meta_ref[Z])


def position(distance, near):
    far = 4 - near
    place = jnp.where(distance == near, 1, jnp.where(distance == far, 2, 0))
    return jnp.where(distance == 0, 3, place)


def pack_body(
    coord_ref, length_ref, hidden_ref, grad_ref, own_q, own_k, own_v, own_rel, own_outer, own_out, own_inner, norm_ref,
    meta_ref, block_ref, *rest,
):
    rows_out, sem, tail_sem = rest
    first_ref, second_ref = block_ref.at[pl.ds(0, FIRST)], block_ref.at[pl.ds(FIRST, SPAN)]
    x, y, z, core = (coord_ref[i] for i in range(4))
    for i in range(4):
        meta_ref[i] = coord_ref[i]
    lengths = [length_ref[i] for i in range(GROUP)]
    dealing = []
    for i in range(GROUP):
        rank = jnp.int32(0)
        for j in range(GROUP):
            if j != i:
                ahead = lengths[j] >= lengths[i] if j < i else lengths[j] > lengths[i]
                rank = rank + ahead.astype(jnp.int32)
        dealing.append(rank)
    length = jnp.int32(0)
    for i in range(GROUP):
        length = length + jnp.where(dealing[i] == x, lengths[i], 0)
    meta_ref[LENGTH] = length
    copies = Copies(sem)
    for k in range(GROUP):
        source = jnp.int32(0)
        for i in range(GROUP):
            source = source + jnp.where(dealing[i] == (x ^ k), i, 0)
        meta_ref[SEQ + k] = source
        copies.add(hidden_ref.at[source], rows_out.at[x ^ k, 0])
        copies.add(grad_ref.at[source], rows_out.at[x ^ k, 1])
    for i in range(SEQ + GROUP, META):
        meta_ref[i] = jnp.int32(0)
    for i, ref in enumerate((own_q, own_k, own_v, own_rel)):
        size = REL_HALF if i == 3 else HALF
        copies.add(ref.at[pl.ds(core * size, size)], first_ref.at[pl.ds(i * HALF, size)])
    quarter = jnp.where(core == 0, y, z)
    copies.add(
        own_inner.at[pl.ds(core * HALF, HALF), pl.ds(pl.multiple_of(quarter * D, D), D)],
        second_ref.at[pl.ds(QUARTER, HALF)],
    )
    copies.start()
    tail = Copies(tail_sem)

    @pl.when(quarter < 3)
    def _():
        copy = pltpu.make_async_copy(
            own_outer.at[pl.ds(core * 3 * QUARTER + quarter * QUARTER, QUARTER)], second_ref.at[pl.ds(0, QUARTER)],
            tail_sem.at[0],
        )
        copy.start()
        copy.wait()

    @pl.when(quarter == 3)
    def _():
        tail.add(own_out.at[pl.ds(core * HALF, HALF)], second_ref.at[pl.ds(0, HALF)])
        tail.add(norm_ref, second_ref.at[pl.ds(HALF, QUARTER - HALF)])
        tail.start()
        tail.wait()

    copies.wait()


def pack(coords, lengths, hidden, grad_out, own_first, own_second, norm_block):
    shape = jax.ShapeDtypeStruct
    scalars, anywhere = pl.BlockSpec(memory_space=pltpu.SMEM), pl.BlockSpec(memory_space=pltpu.HBM)
    full = pl.BlockSpec(memory_space=pltpu.VMEM)
    return pl.pallas_call(
        pack_body,
        out_shape=(
            shape((META,), jnp.int32), shape((FIRST + SPAN, D), LOW), shape((GROUP, 2, PART, D), LOW),
        ),
        in_specs=[scalars, scalars] + [anywhere] * 10,
        out_specs=(scalars, full, full),
        scratch_shapes=[pltpu.SemaphoreType.DMA((13,)), pltpu.SemaphoreType.DMA((2,))],
        compiler_params=pltpu.CompilerParams(vmem_limit_bytes=60 * MIB),
        name="pack",
    )(coords, lengths, hidden, grad_out, *own_first, *own_second, norm_block)


def load_rows(copies, rows_ref, which, target):
    for member in range(GROUP):
        copies.add(rows_ref.at[member, which], target.at[pl.ds(member * PART, PART)])


def load_first(meta_ref, copies, own, pieces, w_ref):
    x, core = meta_ref[X], meta_ref[CORE]
    near, far = x ^ near_of(core), x ^ far_of(core)
    slots = ((near, core), (far, core), (x ^ 2, core), (far, 1 - core), (near, 1 - core), (x ^ 2, 1 - core))
    for piece, (slot, half) in zip(pieces, slots):
        copies.add(piece.at[pl.ds(0, FIRST)], w_ref.at[slot, half])
    for half in range(2):
        for i, ref in enumerate(own):
            size = REL_HALF if i == 3 else HALF
            copies.add(ref.at[pl.ds(half * size, size)], w_ref.at[x, half, pl.ds(i * HALF, size)])


def load_second(meta_ref, copies, own, pieces, w_ref, in_ref):
    own_outer, own_out, own_norm, own_inner = own
    x = meta_ref[X]
    for side in range(2):
        core = meta_ref[CORE] if side == 0 else 1 - meta_ref[CORE]
        assist = assist_of(meta_ref, core)
        arrived, (near, far, across_outer, across_inner) = pieces[7 * side : 7 * side + 3], pieces[7 * side + 3 : 7 * side + 7]
        for i, slot in enumerate((x ^ near_of(core), x ^ far_of(core), x ^ 2)):
            base = arrived[i]
            for outer, inner, quarter in (
                (base.at[pl.ds(FIRST, QUARTER)], base.at[pl.ds(FIRST + QUARTER, HALF)], assist),
                (near.at[i, pl.ds(0, QUARTER)], near.at[i, pl.ds(QUARTER, HALF)], assist ^ 1),
                (far.at[i, pl.ds(0, QUARTER)], far.at[i, pl.ds(QUARTER, HALF)], assist ^ 3),
                (across_outer.at[i], across_inner.at[i], assist ^ 2),
            ):
                copies.add(outer, w_ref.at[slot, core, pl.ds(quarter * QUARTER, QUARTER)])
                copies.add(
                    inner, in_ref.at[pl.ds(slot * PIECE + core * HALF, HALF), pl.ds(pl.multiple_of(quarter * D, D), D)]
                )
    for half in range(2):
        copies.add(own_outer.at[pl.ds(half * 3 * QUARTER, 3 * QUARTER)], w_ref.at[x, half, pl.ds(0, 3 * QUARTER)])
        copies.add(own_out.at[pl.ds(half * HALF, HALF)], w_ref.at[x, half, pl.ds(OUT_AT, HALF)])
    copies.add(own_norm, w_ref.at[x, 0, pl.ds(NORM_AT, QUARTER - HALF)])
    copies.add(own_inner, in_ref.at[pl.ds(x * PIECE, PIECE)])


def select_halves(meta_ref, value):
    half = value.shape[0] // 2
    low, high = value[:half].astype(LOW), value[half:].astype(LOW)
    first_core = meta_ref[CORE] == 0
    return jnp.where(first_core, low, high), jnp.where(first_core, high, low)


def heads_forward(meta_ref, first_pair, refs, probs_ref, ctx_ref):
    q_ref, k_ref, v_ref, pk_ref, pq_ref = refs
    length = meta_ref[LENGTH]
    valid = iota((ROWS, ROWS), 1) < length
    side = iota((ROWS, 2 * HEAD_DIM), 1) // HEAD_DIM

    def pair_step(pair, carry):
        out_cols = pl.ds(pl.multiple_of((pair - first_pair) * 2 * HEAD_DIM, 2 * HEAD_DIM), 2 * HEAD_DIM)
        cols = pl.ds(pl.multiple_of(pair * 2 * HEAD_DIM, 2 * HEAD_DIM), 2 * HEAD_DIM)
        q_pair, k_pair, v_pair = q_ref[:, cols], k_ref[:, cols], v_ref[:, cols]
        pk_pair, pq_pair = pk_ref[:, cols], pq_ref[:, cols]
        zero = jnp.zeros_like(q_pair)
        contexts = []
        for h in range(2):
            mine = side == h
            q_head = jnp.where(mine, q_pair, zero)
            k_head = jnp.where(mine, k_pair, zero)
            content = mm_nt(q_head, k_pair)
            to_off = mm_nt(q_head, pk_pair)
            from_off = mm_nt(k_head, pq_pair)
            to_rel = pltpu.roll(to_off, ROWS + 1, 1, stride=1, stride_axis=0)[:, :ROWS]
            from_rel = pltpu.roll(from_off, ROWS + 1, 1, stride=1, stride_axis=0)[:, :ROWS]
            scores = (content + to_rel + from_rel.T) * SCALING
            scores = jnp.where(valid, scores, MASKED)
            top = jnp.max(scores, axis=1, keepdims=True)
            shifted = jnp.exp(scores - top)
            summed = jnp.sum(shifted, axis=1, keepdims=True)
            probs = (shifted * (1.0 / summed)).astype(LOW)
            probs_ref[2 * (pair - first_pair) + h] = probs
            contexts.append(mm(probs, v_pair))
        ctx_ref[:, out_cols] = jnp.where(side == 0, contexts[0], contexts[1]).astype(LOW)
        return carry

    lax.fori_loop(first_pair, first_pair + PAIRS // 2, pair_step, 0)


def attend_forward_body(
    meta_ref, bucket_ref, rows_ref, own_q, own_k, own_v, own_rel, p0, p1, p2, p3, p4, p5,
    tok_ref, q_ref, k_ref, v_ref, pk_ref, pq_ref, relw_ref, probs_ref, ctx_ref,
    w_ref, sem,
):
    copies = Copies(sem)
    load_rows(copies, rows_ref, 0, tok_ref)
    load_first(meta_ref, copies, (own_q, own_k, own_v, own_rel), (p0, p1, p2, p3, p4, p5), w_ref)
    copies.start()
    copies.wait()
    tok = tok_ref[...]
    rel = whole(w_ref, REL_AT, REL_HALF)
    pick = (bucket_ref[...] == iota((OFFS, OFFS), 1)).astype(LOW)
    relw = mm(pick, rel).astype(LOW)
    relw_ref[...] = relw
    w_query = whole(w_ref, 0, HALF)
    q_ref[...] = mm(tok, w_query).astype(LOW)
    pq_ref[...] = mm(relw, w_query).astype(LOW)
    w_key = whole(w_ref, HALF, HALF)
    k_ref[...] = mm(tok, w_key).astype(LOW)
    pk_ref[...] = mm(relw, w_key).astype(LOW)
    v_ref[...] = mm(tok, whole(w_ref, 2 * HALF, HALF)).astype(LOW)
    heads_forward(meta_ref, 0, (q_ref, k_ref, v_ref, pk_ref, pq_ref), probs_ref, ctx_ref)


def attend_forward_two_body(meta_ref, q_ref, k_ref, v_ref, pk_ref, pq_ref, probs_ref, ctx_ref):
    heads_forward(meta_ref, PAIRS // 2, (q_ref, k_ref, v_ref, pk_ref, pq_ref), probs_ref, ctx_ref)


def attend_forward(meta, bucket_column, rows, own, pieces):
    shape = jax.ShapeDtypeStruct
    full, anywhere = pl.BlockSpec(memory_space=pltpu.VMEM), pl.BlockSpec(memory_space=pltpu.HBM)
    return pl.pallas_call(
        attend_forward_body,
        out_shape=(
            *(shape((ROWS, D), LOW),) * 4,
            shape((OFFS, D), LOW), shape((OFFS, D), LOW), shape((OFFS, D), LOW),
            shape((HEADS // 2, ROWS, ROWS), LOW), shape((ROWS, D // 2), LOW),
        ),
        in_specs=[pl.BlockSpec(memory_space=pltpu.SMEM), full] + [anywhere] * 11,
        out_specs=(full,) * 9,
        scratch_shapes=[pltpu.VMEM((GROUP, 2, FIRST, D), LOW), pltpu.SemaphoreType.DMA((18,))],
        compiler_params=pltpu.CompilerParams(vmem_limit_bytes=28 * MIB),
        cost_estimate=pl.CostEstimate(flops=12_000_000_000, bytes_accessed=40_000_000, transcendentals=800_000),
        name="attend_forward",
    )(meta, bucket_column, rows, *own, *pieces)


def attend_forward_two(meta, saved):
    shape = jax.ShapeDtypeStruct
    full = pl.BlockSpec(memory_space=pltpu.VMEM)
    return pl.pallas_call(
        attend_forward_two_body,
        out_shape=(shape((HEADS // 2, ROWS, ROWS), LOW), shape((ROWS, D // 2), LOW)),
        in_specs=[pl.BlockSpec(memory_space=pltpu.SMEM)] + [full] * 5,
        out_specs=(full,) * 2,
        compiler_params=pltpu.CompilerParams(vmem_limit_bytes=24 * MIB),
        cost_estimate=pl.CostEstimate(flops=8_000_000_000, bytes_accessed=20_000_000, transcendentals=400_000),
        name="attend_forward_two",
    )(meta, *saved)


def heads_back(first_pair, count, refs, outs):
    q_ref, k_ref, v_ref, pk_ref, pq_ref, probs_ref, gctx_ref = refs
    gq_ref, gk_ref, gv_ref, gpk_ref, gpq_ref, qr_ref, kr_ref = outs
    flip = (iota((ROWS, ROWS), 0) + iota((ROWS, ROWS), 1) == ROWS - 1).astype(LOW)
    qr_ref[...] = mm(flip, q_ref[...]).astype(LOW)
    kr_ref[...] = mm(flip, k_ref[...]).astype(LOW)
    side = iota((ROWS, 2 * HEAD_DIM), 1) // HEAD_DIM
    side_off = iota((OFFS, 2 * HEAD_DIM), 1) // HEAD_DIM
    blank = jnp.zeros((ROWS, OFFS - ROWS), F32)

    def pair_step(pair, carry):
        cols = pl.ds(pl.multiple_of(pair * 2 * HEAD_DIM, 2 * HEAD_DIM), 2 * HEAD_DIM)
        q_pair, k_pair, v_pair = q_ref[:, cols], k_ref[:, cols], v_ref[:, cols]
        pk_pair, pq_pair, gctx_pair = pk_ref[:, cols], pq_ref[:, cols], gctx_ref[:, cols]
        qr_pair, kr_pair = qr_ref[:, cols], kr_ref[:, cols]
        zero = jnp.zeros_like(q_pair)
        parts = []
        for h in range(2):
            gctx_head = jnp.where(side == h, gctx_pair, zero)
            grad_probs = mm_nt(gctx_head, v_pair)
            probs_low = probs_ref[2 * (pair - first_pair) + h]
            probs = probs_low.astype(F32)
            inner = jnp.sum(probs * grad_probs, axis=1, keepdims=True)
            grad_scores = (probs * (grad_probs - inner)).astype(LOW)
            g_value = mm_tn(probs_low, gctx_pair)
            rows_back = mm(flip, grad_scores)
            cols_back = mm_nt(flip, grad_scores)
            to_off = pltpu.roll(jnp.concatenate([rows_back, blank], axis=1), 0, 1, stride=1, stride_axis=0).astype(LOW)
            from_off = pltpu.roll(jnp.concatenate([cols_back, blank], axis=1), 0, 1, stride=1, stride_axis=0).astype(LOW)
            g_query = mm(rows_back.astype(LOW), k_pair) + mm(to_off, pk_pair)
            g_key = mm(cols_back.astype(LOW), q_pair) + mm(from_off, pq_pair)
            g_pk = mm_tn(to_off, qr_pair)
            g_pq = mm_tn(from_off, kr_pair)
            parts.append((g_value, g_query, g_key, g_pk, g_pq))
        first, second = parts
        gv_ref[:, cols] = jnp.where(side == 0, first[0], second[0]).astype(LOW)
        gq_ref[:, cols] = (jnp.where(side == 0, first[1], second[1]) * SCALING).astype(LOW)
        gk_ref[:, cols] = (jnp.where(side == 0, first[2], second[2]) * SCALING).astype(LOW)
        gpk_ref[:, cols] = (jnp.where(side_off == 0, first[3], second[3]) * SCALING).astype(LOW)
        gpq_ref[:, cols] = (jnp.where(side_off == 0, first[4], second[4]) * SCALING).astype(LOW)
        return carry

    lax.fori_loop(first_pair, first_pair + count, pair_step, 0)
    return flip


def attend_back_one_body(
    q_ref, k_ref, v_ref, pk_ref, pq_ref, probs_ref, gctx_ref,
    gq_ref, gk_ref, gv_ref, gpk_ref, gpq_ref, qr_ref, kr_ref,
):
    heads_back(
        0, PAIRS // 2, (q_ref, k_ref, v_ref, pk_ref, pq_ref, probs_ref, gctx_ref),
        (gq_ref, gk_ref, gv_ref, gpk_ref, gpq_ref, qr_ref, kr_ref),
    )


def attend_back_two_body(
    meta_ref, q_ref, k_ref, v_ref, pk_ref, pq_ref, probs_ref, gctx_ref, hq, hk, hv, hpk, hpq,
    tok_ref, relw_ref, gres_ref, bucket_ref,
    own_q, own_k, own_v, own_rel, p0, p1, p2, p3, p4, p5,
    out_ref,
    home_ref, keep_ref, send_ref,
    gq_ref, gk_ref, gv_ref, gpk_ref, gpq_ref, qr_ref, kr_ref, gtok_ref, w_ref, sem,
):
    copies = Copies(sem)
    load_first(meta_ref, copies, (own_q, own_k, own_v, own_rel), (p0, p1, p2, p3, p4, p5), w_ref)
    copies.start()
    for target, done in ((gq_ref, hq), (gk_ref, hk), (gv_ref, hv), (gpk_ref, hpk), (gpq_ref, hpq)):
        target[:, : D // 2] = done[...]
    flip = heads_back(
        PAIRS // 2, PAIRS // 2, (q_ref, k_ref, v_ref, pk_ref, pq_ref, probs_ref, gctx_ref),
        (gq_ref, gk_ref, gv_ref, gpk_ref, gpq_ref, qr_ref, kr_ref),
    )
    copies.wait()
    tok, relw = tok_ref[...], relw_ref[...]
    g_query = mm(flip, gq_ref[...]).astype(LOW)
    w_query = whole(w_ref, 0, HALF)
    g_tok = gres_ref[...] + mm_nt(g_query, w_query)
    g_rel = mm_nt(gpq_ref[...], w_query)

    x, core = meta_ref[X], meta_ref[CORE]

    def put(start, size, value):
        for shard in range(GROUP):
            keep, send = select_halves(meta_ref, value[shard * 2 * size : (shard + 1) * 2 * size])
            keep_ref[position(x ^ shard, near_of(core)), start : start + size] = keep
            send_ref[position(x ^ shard, far_of(core)), start : start + size] = send

    put(0, HALF, mm_tn(tok, g_query) + mm_tn(relw, gpq_ref[...]))
    g_key = mm(flip, gk_ref[...]).astype(LOW)
    w_key = whole(w_ref, HALF, HALF)
    g_tok = g_tok + mm_nt(g_key, w_key)
    g_rel = (g_rel + mm_nt(gpk_ref[...], w_key)).astype(LOW)
    put(HALF, HALF, mm_tn(tok, g_key) + mm_tn(relw, gpk_ref[...]))
    g_value = gv_ref[...]
    gtok_ref[...] = (g_tok + mm_nt(g_value, whole(w_ref, 2 * HALF, HALF))).astype(LOW)
    put(2 * HALF, HALF, mm_tn(tok, g_value))
    pick = (bucket_ref[...] == iota((OFFS, OFFS), 1)).astype(LOW)
    put(REL_AT, REL_HALF, mm_tn(pick, g_rel))
    for member in range(GROUP):
        home_ref[member, 0] = out_ref[member * PART : (member + 1) * PART, :]
        home_ref[member, 1] = gtok_ref[member * PART : (member + 1) * PART, :]


def attend_back_one(saved, gctx):
    shape = jax.ShapeDtypeStruct
    full = pl.BlockSpec(memory_space=pltpu.VMEM)
    return pl.pallas_call(
        attend_back_one_body,
        out_shape=(*(shape((ROWS, D // 2), LOW),) * 3, *(shape((OFFS, D // 2), LOW),) * 2),
        in_specs=[full] * 7,
        out_specs=(full,) * 5,
        scratch_shapes=[pltpu.VMEM((ROWS, D), LOW), pltpu.VMEM((ROWS, D), LOW)],
        compiler_params=pltpu.CompilerParams(vmem_limit_bytes=24 * MIB),
        cost_estimate=pl.CostEstimate(flops=8_000_000_000, bytes_accessed=20_000_000, transcendentals=0),
        name="attend_back_one",
    )(*saved, gctx)


def attend_back_two(meta, saved, gctx, half_done, tok, relw, gres, bucket_column, own, pieces, out):
    shape = jax.ShapeDtypeStruct
    full, anywhere = pl.BlockSpec(memory_space=pltpu.VMEM), pl.BlockSpec(memory_space=pltpu.HBM)
    return pl.pallas_call(
        attend_back_two_body,
        out_shape=(shape((GROUP, 2, PART, D), LOW), shape((GROUP, FIRST, D), LOW), shape((GROUP, FIRST, D), LOW)),
        in_specs=[pl.BlockSpec(memory_space=pltpu.SMEM)] + [full] * 16 + [anywhere] * 10 + [full],
        out_specs=(full,) * 3,
        scratch_shapes=[
            *(pltpu.VMEM((ROWS, D), LOW),) * 3, *(pltpu.VMEM((OFFS, D), LOW),) * 2, *(pltpu.VMEM((ROWS, D), LOW),) * 3,
            pltpu.VMEM((GROUP, 2, FIRST, D), LOW), pltpu.SemaphoreType.DMA((14,)),
        ],
        compiler_params=pltpu.CompilerParams(vmem_limit_bytes=36 * MIB),
        cost_estimate=pl.CostEstimate(flops=14_000_000_000, bytes_accessed=40_000_000, transcendentals=0),
        name="attend_back_two",
    )(meta, *saved, gctx, *half_done, tok, relw, gres, bucket_column, *own, *pieces, out)


def feed_body(
    meta_ref, tok_ref, ctx_one_ref, ctx_two_ref, rows_ref, own_outer, own_out, own_norm, own_inner, *rest,
):
    pieces, rest = rest[:14], rest[14:]
    out_ref, gctx_ref, gres_ref, keep_ref, send_ref, keep_in_ref, send_in_ref = rest[:7]
    up_ref, low_ref, act_ref, slope_ref, w_ref, in_ref, sem = rest[7:]
    copies = Copies(sem)
    load_rows(copies, rows_ref, 1, up_ref)
    load_second(meta_ref, copies, (own_outer, own_out, own_norm, own_inner), pieces, w_ref, in_ref)
    copies.start()
    copies.wait()
    x, core = meta_ref[X], meta_ref[CORE]
    assist, assist_peer = assist_of(meta_ref, core), assist_of(meta_ref, 1 - core)

    def put_outer(shard, quarter, keep, send, start):
        rows = slice(start, start + keep.shape[0])
        keep_ref[position(assist ^ quarter, 1), position(x ^ shard, near_of(core)), rows] = keep
        send_ref[position(assist_peer ^ quarter, 1), position(x ^ shard, far_of(core)), rows] = send

    def put_inner(shard, quarter, keep, send):
        keep_in_ref[position(assist ^ quarter, 3), position(x ^ shard, near_of(core))] = keep
        send_in_ref[position(assist_peer ^ quarter, 3), position(x ^ shard, far_of(core))] = send

    length = meta_ref[LENGTH]
    mask = (iota((ROWS, 1), 0) < length).astype(F32)
    norm_rows = [w_ref[s, 0, NORM_AT : NORM_AT + QUARTER - HALF, :].astype(F32)[:1] for s in range(GROUP)]
    gain_one, bias_one, gain_two, bias_two = (
        jnp.concatenate([row[:, i * PIECE : (i + 1) * PIECE] for row in norm_rows], axis=1) for i in range(4)
    )
    token = tok_ref[...].astype(F32)
    ctx = jnp.concatenate([ctx_one_ref[...], ctx_two_ref[...]], axis=1)
    w_out = whole(w_ref, OUT_AT, HALF)
    attn = mm(ctx, w_out)

    def norm(values):
        center = values - jnp.mean(values, axis=1, keepdims=True)
        inverse = lax.rsqrt(jnp.mean(center * center, axis=1, keepdims=True) + EPSILON)
        return center * inverse, inverse

    def norm_back(upstream, normed, inverse, gain):
        scaled = upstream * gain
        plain = jnp.mean(scaled, axis=1, keepdims=True)
        cross = jnp.mean(scaled * normed, axis=1, keepdims=True)
        return inverse * (scaled - plain - normed * cross)

    def total(values):
        return jnp.sum(values, axis=0, keepdims=True)

    normed_one, inverse_one = norm(token + attn)
    hidden_one = normed_one * gain_one + bias_one
    low_ref[...] = hidden_one.astype(LOW)

    def columns(c):
        return pl.ds(pl.multiple_of(c * D, D), D)

    def outer_rows(c):
        return w_ref[c, :, 0 : D // 2, :].reshape(D, D)

    def forward_step(c, ffn):
        inner = mm(low_ref[...], in_ref[:, columns(c)])
        cumulative = 0.5 * (1.0 + lax.erf(inner * 0.5**0.5))
        density = jnp.exp(-0.5 * inner * inner) * 0.3989422804014327
        act = (inner * cumulative).astype(LOW)
        act_ref[c] = act
        slope_ref[c] = cumulative + inner * density
        return ffn + mm(act, outer_rows(c))

    ffn = lax.fori_loop(0, GROUP, forward_step, jnp.zeros((ROWS, D), F32))
    normed_two, inverse_two = norm(hidden_one + ffn)
    layer = (normed_two * gain_two + bias_two) * mask
    out_ref[...] = layer.astype(LOW)
    squares = [token * token * mask, attn * attn * mask, ffn * ffn * mask, layer * layer]
    sums = [jnp.sum(total(s), axis=1, keepdims=True) for s in squares]
    grad_y = up_ref[...].astype(F32) * mask
    grad_gain_two = total(grad_y * normed_two)
    grad_bias_two = total(grad_y)
    grad_two = norm_back(grad_y, normed_two, inverse_two, gain_two)
    grad_ffn = grad_two.astype(LOW)

    def back_step(c, grad_hidden):
        grad_act = mm_nt(grad_ffn, outer_rows(c))
        grad_inner = (grad_act * slope_ref[c]).astype(LOW)
        keep, send = select_halves(meta_ref, mm_tn(act_ref[c], grad_ffn))
        for quarter in range(3):
            rows = slice(quarter * QUARTER, (quarter + 1) * QUARTER)
            put_outer(c, quarter, keep[rows], send[rows], 0)
        grad_w = mm_tn(low_ref[...], grad_inner)
        for s in range(GROUP):
            put_inner(s, c, *select_halves(meta_ref, grad_w[s * PIECE : (s + 1) * PIECE]))
        return grad_hidden + mm_nt(grad_inner, in_ref[:, columns(c)])

    grad_hidden = lax.fori_loop(0, GROUP, back_step, grad_two)
    grad_gain_one = total(grad_hidden * normed_one)
    grad_bias_one = total(grad_hidden)
    grad_one = norm_back(grad_hidden, normed_one, inverse_one, gain_one)
    gres_ref[...] = grad_one
    grad_attn = grad_one.astype(LOW)
    grad_out = mm_tn(ctx, grad_attn)
    for s in range(GROUP):
        put_outer(s, 3, *select_halves(meta_ref, grad_out[s * PIECE : (s + 1) * PIECE]), 0)
    gctx_ref[...] = mm_nt(grad_attn, w_out).astype(LOW)
    lane = iota((1, D), 1)
    stats = jnp.zeros((1, D), F32)
    for i, value in enumerate(sums):
        stats = jnp.where(lane == i, value, stats)
    low = stats - stats.astype(LOW).astype(F32)
    zeros = jnp.zeros((1, D), F32)
    norm_rows = (grad_gain_one, grad_bias_one, grad_gain_two, grad_bias_two)
    for s in range(GROUP):
        row = jnp.concatenate([r[:, s * PIECE : (s + 1) * PIECE] for r in norm_rows], axis=1)
        block = jnp.concatenate([row] + [zeros] * 31 + [stats, low] + [zeros] * 30, axis=0)
        put_outer(s, 3, *select_halves(meta_ref, block), HALF)


def feed(meta, tok, ctx_one, ctx_two, rows, own, pieces):
    shape = jax.ShapeDtypeStruct
    full, anywhere = pl.BlockSpec(memory_space=pltpu.VMEM), pl.BlockSpec(memory_space=pltpu.HBM)
    block, wide = shape((GROUP, GROUP, QUARTER, D), LOW), shape((GROUP, GROUP, HALF, D), LOW)
    return pl.pallas_call(
        feed_body,
        out_shape=(
            shape((ROWS, D), LOW), shape((ROWS, D), LOW), shape((ROWS, D), F32), block, block, wide, wide
        ),
        in_specs=[pl.BlockSpec(memory_space=pltpu.SMEM)] + [full] * 3 + [anywhere] * 19,
        out_specs=(full,) * 7,
        scratch_shapes=[
            *(pltpu.VMEM((ROWS, D), LOW),) * 2, pltpu.VMEM((GROUP, ROWS, D), LOW), pltpu.VMEM((GROUP, ROWS, D), F32),
            pltpu.VMEM((GROUP, 2, SECOND, D), LOW), pltpu.VMEM((D, WIDE), LOW), pltpu.SemaphoreType.DMA((58,)),
        ],
        compiler_params=pltpu.CompilerParams(vmem_limit_bytes=48 * MIB),
        cost_estimate=pl.CostEstimate(flops=16_000_000_000, bytes_accessed=60_000_000, transcendentals=1_600_000),
        name="feed",
    )(meta, tok, ctx_one, ctx_two, rows, *own, *pieces)


def finish_body(
    meta_ref, mine, other, rows_ref,
    q_ref, k_ref, v_ref, rel_ref, outer_ref, wout_ref, inner_ref, extra_ref, out_ref, gtok_ref,
):
    for piece, side in ((mine, 0), (other, 1)):
        core = meta_ref[CORE] if side == 0 else 1 - meta_ref[CORE]
        assist = assist_of(meta_ref, core)
        for i, ref in enumerate((q_ref, k_ref, v_ref, rel_ref)):
            size = REL_HALF if i == 3 else HALF
            ref[pl.ds(pl.multiple_of(core * size, size), size), :] = piece[i * HALF : i * HALF + size, :].astype(F32)
        for distance in range(GROUP):
            quarter = assist ^ distance
            at = FIRST + distance * SPAN
            block = piece[at : at + QUARTER, :].astype(F32)

            @pl.when(quarter < 3)
            def _():
                outer_ref[pl.ds(pl.multiple_of(core * 3 * QUARTER + quarter * QUARTER, QUARTER), QUARTER), :] = block

            @pl.when(quarter == 3)
            def _():
                wout_ref[pl.ds(pl.multiple_of(core * HALF, HALF), HALF), :] = block[:HALF]
                extra_ref[core] = block[HALF:]

            inner_ref[
                pl.ds(pl.multiple_of(core * HALF, HALF), HALF), pl.ds(pl.multiple_of(quarter * D, D), D)
            ] = piece[at + QUARTER : at + SPAN, :].astype(F32)
    for k in range(GROUP):
        member = meta_ref[X] ^ k
        out_ref[meta_ref[SEQ + k]] = rows_ref[member, 0]
        gtok_ref[meta_ref[SEQ + k]] = rows_ref[member, 1]


def finish(meta, mine, other, rows):
    shape = jax.ShapeDtypeStruct
    full = pl.BlockSpec(memory_space=pltpu.VMEM)
    return pl.pallas_call(
        finish_body,
        out_shape=(
            *(shape((PIECE, D), F32),) * 3, shape((OFFS // GROUP, D), F32),
            shape((D, D), F32), shape((PIECE, D), F32), shape((PIECE, WIDE), F32), shape((2, QUARTER - HALF, D), F32),
            *(shape((GROUP, PART, D), LOW),) * 2,
        ),
        in_specs=[pl.BlockSpec(memory_space=pltpu.SMEM)] + [full] * 3,
        out_specs=(full,) * 10,
        compiler_params=pltpu.CompilerParams(vmem_limit_bytes=24 * MIB),
        name="finish",
    )(meta, mine, other, rows)


NEAR, FAR = (1, 3), (3, 1)


def hop_x(value, flips):
    pairs = [(c * 4 + i, c * 4 + (i ^ flips[c])) for c in range(2) for i in range(4)]
    return lax.ppermute(value, ("core", "shard"), pairs)


def hop_yz(value, flip, swapped=False):
    pairs = []
    for y in range(4):
        for z in range(4):
            for c in range(2):
                along_y = (c == 0) != swapped
                ty, tz = (y ^ flip, z) if along_y else (y, z ^ flip)
                pairs.append(((y * 4 + z) * 2 + c, (ty * 4 + tz) * 2 + c))
    return lax.ppermute(value, ("y", "z", "core"), pairs)


def swap(value):
    return lax.ppermute(value, "core", [(0, 1), (1, 0)])


def after(value, *others):
    return lax.optimization_barrier((value, *others))[0]


def add(*values):
    total = values[0].astype(F32)
    for value in values[1:]:
        total = total + value.astype(F32)
    return total.astype(LOW)


def exchange_rows(rows):
    return lax.all_to_all(rows, "shard", split_axis=0, concat_axis=0, tiled=True)


def shards(
    hidden, grad_out, lengths, bucket, w_query, w_key, w_value, w_out, w_inner, w_outer, rel_table,
    ln1_gain, ln1_bias, ln2_gain, ln2_bias,
):
    coords = jnp.stack([lax.axis_index(name) for name in ("shard", "y", "z", "core")]).astype(jnp.int32)
    norm_block = jnp.concatenate(
        [jnp.concatenate([ln1_gain, ln1_bias, ln2_gain, ln2_bias])[None], jnp.zeros((31, D), LOW)], axis=0
    )
    bucket_column = jnp.concatenate([bucket[::-1], jnp.full((1,), -1, jnp.int32)])[:, None]
    own_first = (w_query, w_key, w_value, rel_table)
    meta, block, rows = pack(
        coords, lengths, hidden, grad_out, own_first, (w_outer, w_out, w_inner), norm_block
    )
    near, far = hop_x(block, NEAR), hop_x(block, FAR)
    rows = exchange_rows(rows)
    across = hop_x(near, FAR)
    swapped_near, swapped_far = swap(near), swap(far)
    base = jnp.stack([piece[FIRST:] for piece in (near, far, across)])
    base_near, base_far = hop_yz(base, 1), hop_yz(base, 3)
    pieces = (near, far, across, swapped_near, swapped_far, swap(across))
    tok, *saved, relw, probs, ctx = attend_forward(meta, bucket_column, rows, own_first, pieces)
    base_near, base_far, _ = lax.optimization_barrier((base_near, base_far, ctx))
    across_outer = hop_yz(base_near[:, :QUARTER], 3)
    across_inner = hop_yz(base_far[:, QUARTER:], 1)
    swapped = swap(base_near), swap(base_far)
    probs_two, ctx_two = attend_forward_two(meta, saved)
    swapped, across_outer, across_inner, _ = lax.optimization_barrier((swapped, across_outer, across_inner, ctx_two))
    arrived = (
        *pieces[:3], base_near, base_far, across_outer, across_inner,
        *pieces[3:], *swapped, swap(across_outer), swap(across_inner),
    )
    out, gctx, gres, keep, send, keep_in, send_in = feed(
        meta, tok, ctx, ctx_two, rows, (w_outer, w_out, norm_block, w_inner), arrived
    )
    other, other_in = swap(send), swap(send_in)
    half_done = attend_back_one((*saved, probs), gctx)
    leave = add(keep[:2], other[:2])
    leave_in = add(keep_in[:2], other_in[:2])
    came, came_in = hop_yz(leave, 1), hop_yz(leave_in, 3)
    half_done = after(tuple(half_done), leave, leave_in)
    leaving, keep_one, send_one = attend_back_two(
        meta, (*saved, probs_two), gctx, half_done, tok, relw, gres, bucket_column, own_first, pieces, out
    )
    other_one = swap(after(send_one, came, came_in))
    last = hop_yz(add(keep[2], other[2], came[0]), 3)
    last_in = hop_yz(add(keep_in[2], other_in[2], came_in[0]), 1)
    leave_one = add(keep_one[:2], other_one[:2])
    came_one = hop_x(leave_one, NEAR)
    came_one = after(came_one, last, last_in)
    leave_two = add(keep_one[2], other_one[2], came_one[0])
    last_one = hop_x(leave_two, FAR)
    last, last_in, _ = lax.optimization_barrier((last, last_in, leave_two))
    mine = add(keep[3], other[3], came[1], last)
    mine_in = add(keep_in[3], other_in[3], came_in[1], last_in)
    both = jnp.concatenate([mine, mine_in], axis=1)
    came_x = hop_x(both[:2], NEAR)
    home = exchange_rows(leaving)
    last_one = after(last_one, came_x)
    mine_one = add(keep_one[3], other_one[3], came_one[1], last_one)
    come_one = hop_yz(mine_one, 1, swapped=True)
    last_x = hop_x(after(add(both[2], came_x[0]), mine_one), FAR)
    mine_one = add(mine_one, after(come_one, last_x))
    come_one = hop_yz(mine_one, 3, swapped=True)
    both = after(add(both[3], came_x[1], last_x), mine_one)
    step = hop_yz(both, 1, swapped=True)
    mine_one = add(mine_one, after(come_one, step))
    come_one = hop_yz(mine_one, 1)
    both = after(add(both, step), mine_one)
    step = hop_yz(both, 3, swapped=True)
    mine_one = add(mine_one, after(come_one, step))
    come_one = hop_yz(mine_one, 3)
    both = after(add(both, step), mine_one)
    both = [both, *(hop_yz(both, flip) for flip in (1, 3, 2))]
    both[1], both[2], both[3] = both[1], both[3], both[2]
    mine_one = add(mine_one, come_one)
    packed = after(jnp.concatenate([mine_one, *both], axis=0), home)
    q_grad, k_grad, v_grad, rel_grad, outer_grad, out_grad, inner_grad, extra, layer_output, grad_hidden = finish(
        meta, packed, swap(packed), home
    )
    norm_sums = extra[0, 0].reshape(GROUP, PIECE)
    stats = extra[1, 0, :GROUP] + extra[1, 1, :GROUP]
    return (
        layer_output, grad_hidden, q_grad, k_grad, v_grad, out_grad, inner_grad, outer_grad, rel_grad,
        norm_sums[0], norm_sums[1], norm_sums[2], norm_sums[3],
        jnp.sqrt(stats / (TOKENS * D)),
    )


def solution(mesh):
    split = Mesh(mesh.devices.reshape(4, 4, 2, 4), ("y", "z", "core", "shard"))
    rep = ("y", "z", "core")
    rows, vector = P("shard", None), P("shard")
    batch = P(rep, "shard", None)
    return jax.shard_map(
        shards,
        mesh=split,
        in_specs=(batch, batch, P(rep), P(), *(rows,) * 7, *(vector,) * 4),
        out_specs=(batch, batch, *(rows,) * 7, *(vector,) * 4, P()),
        check_vma=False,
    )
```

```python
import jax
import jax.numpy as jnp
from jax import lax
from jax.experimental import pallas as pl
from jax.experimental.pallas import tpu as pltpu
from jax.sharding import Mesh
from jax.sharding import PartitionSpec as P

D = 768
HEADS = 12
HEAD_DIM = 64
PAIRS = HEADS // 2
ROWS = 256
OFFS = 512
TOKENS = 20480
GROUP = 4
PIECE = D // GROUP
HALF = PIECE // 2
WIDE = GROUP * D
REL_HALF = OFFS // GROUP // 2
REL_AT = 3 * HALF
FIRST = 3 * HALF + REL_HALF
OUT_AT = D // 2
NORM_AT = D // 2 + HALF
QUARTER = 128
SECOND = GROUP * QUARTER
SPAN = QUARTER + HALF
PART = ROWS // GROUP
X, Y, Z, CORE, LENGTH, SEQ = 0, 1, 2, 3, 4, 5
META = 16
EPSILON = 1e-07
MASKED = -1e30
SCALING = (3.0 * HEAD_DIM) ** (-0.5)
F32 = jnp.float32
LOW = jnp.bfloat16
MIB = 1024 * 1024


def mm(a, b):
    return lax.dot_general(a, b, (((1,), (0,)), ((), ())), preferred_element_type=F32)


def mm_nt(a, b):
    return lax.dot_general(a, b, (((1,), (1,)), ((), ())), preferred_element_type=F32)


def mm_tn(a, b):
    return lax.dot_general(a, b, (((0,), (0,)), ((), ())), preferred_element_type=F32)


def iota(shape, dim):
    return lax.broadcasted_iota(jnp.int32, shape, dim)


def whole(ref, start, size):
    piece = ref[:, :, start : start + size, :]
    return piece.reshape(GROUP * 2 * size, piece.shape[3])


def run_copies(copies):
    for copy in copies:
        copy.start()
    for copy in copies:
        copy.wait()


class Copies:
    def __init__(self, sem):
        self.sem, self.made = sem, []

    def add(self, source, target):
        self.made.append(pltpu.make_async_copy(source, target, self.sem.at[len(self.made)]))

    def start(self):
        for copy in self.made:
            copy.start()

    def wait(self):
        for copy in self.made:
            copy.wait()


def near_of(core):
    return 1 + 2 * core


def far_of(core):
    return 3 - 2 * core


def assist_of(meta_ref, core):
    return jnp.where(core == 0, meta_ref[Y], meta_ref[Z])


def position(distance, near):
    far = 4 - near
    place = jnp.where(distance == near, 1, jnp.where(distance == far, 2, 0))
    return jnp.where(distance == 0, 3, place)


def pack_body(
    coord_ref, length_ref, hidden_ref, grad_ref, own_q, own_k, own_v, own_rel, own_outer, own_out, own_inner, norm_ref,
    meta_ref, first_ref, second_ref, *rest,
):
    rows_out, sem, tail_sem = rest
    x, y, z, core = (coord_ref[i] for i in range(4))
    for i in range(4):
        meta_ref[i] = coord_ref[i]
    lengths = [length_ref[i] for i in range(GROUP)]
    dealing = []
    for i in range(GROUP):
        rank = jnp.int32(0)
        for j in range(GROUP):
            if j != i:
                ahead = lengths[j] >= lengths[i] if j < i else lengths[j] > lengths[i]
                rank = rank + ahead.astype(jnp.int32)
        dealing.append(rank)
    length = jnp.int32(0)
    for i in range(GROUP):
        length = length + jnp.where(dealing[i] == x, lengths[i], 0)
    meta_ref[LENGTH] = length
    copies = Copies(sem)
    for k in range(GROUP):
        source = jnp.int32(0)
        for i in range(GROUP):
            source = source + jnp.where(dealing[i] == (x ^ k), i, 0)
        meta_ref[SEQ + k] = source
        copies.add(hidden_ref.at[source], rows_out.at[x ^ k, 0])
        copies.add(grad_ref.at[source], rows_out.at[x ^ k, 1])
    for i in range(SEQ + GROUP, META):
        meta_ref[i] = jnp.int32(0)
    for i, ref in enumerate((own_q, own_k, own_v, own_rel)):
        size = REL_HALF if i == 3 else HALF
        copies.add(ref.at[pl.ds(core * size, size)], first_ref.at[pl.ds(i * HALF, size)])
    quarter = jnp.where(core == 0, y, z)
    copies.add(
        own_inner.at[pl.ds(core * HALF, HALF), pl.ds(pl.multiple_of(quarter * D, D), D)],
        second_ref.at[pl.ds(QUARTER, HALF)],
    )
    copies.start()
    tail = Copies(tail_sem)

    @pl.when(quarter < 3)
    def _():
        copy = pltpu.make_async_copy(
            own_outer.at[pl.ds(core * 3 * QUARTER + quarter * QUARTER, QUARTER)], second_ref.at[pl.ds(0, QUARTER)],
            tail_sem.at[0],
        )
        copy.start()
        copy.wait()

    @pl.when(quarter == 3)
    def _():
        tail.add(own_out.at[pl.ds(core * HALF, HALF)], second_ref.at[pl.ds(0, HALF)])
        tail.add(norm_ref, second_ref.at[pl.ds(HALF, QUARTER - HALF)])
        tail.start()
        tail.wait()

    copies.wait()


def pack(coords, lengths, hidden, grad_out, own_first, own_second, norm_block):
    shape = jax.ShapeDtypeStruct
    scalars, anywhere = pl.BlockSpec(memory_space=pltpu.SMEM), pl.BlockSpec(memory_space=pltpu.HBM)
    full = pl.BlockSpec(memory_space=pltpu.VMEM)
    return pl.pallas_call(
        pack_body,
        out_shape=(
            shape((META,), jnp.int32), shape((FIRST, D), LOW), shape((SPAN, D), LOW), shape((GROUP, 2, PART, D), LOW),
        ),
        in_specs=[scalars, scalars] + [anywhere] * 10,
        out_specs=(scalars, full, full, full),
        scratch_shapes=[pltpu.SemaphoreType.DMA((13,)), pltpu.SemaphoreType.DMA((2,))],
        compiler_params=pltpu.CompilerParams(vmem_limit_bytes=60 * MIB),
        name="pack",
    )(coords, lengths, hidden, grad_out, *own_first, *own_second, norm_block)


def load_first(meta_ref, copies, own, pieces, w_ref):
    x, core = meta_ref[X], meta_ref[CORE]
    near, far = x ^ near_of(core), x ^ far_of(core)
    slots = ((near, core), (far, core), (x ^ 2, core), (far, 1 - core), (near, 1 - core), (x ^ 2, 1 - core))
    for piece, (slot, half) in zip(pieces, slots):
        copies.add(piece, w_ref.at[slot, half])
    for i, ref in enumerate(own):
        size = REL_HALF if i == 3 else HALF
        copies.add(ref, w_ref.at[x, :, pl.ds(i * HALF, size)])


def load_second(meta_ref, copies, own, pieces, w_ref, in_ref):
    own_outer, own_out, own_norm, own_inner = own
    for side in range(2):
        assist = assist_of(meta_ref, meta_ref[CORE] if side == 0 else 1 - meta_ref[CORE])
        base, near, far, across_outer, across_inner = pieces[5 * side : 5 * side + 5]
        for distance, outer, inner in (
            (0, base.at[:, pl.ds(0, QUARTER)], base.at[:, pl.ds(QUARTER, HALF)]),
            (1, near.at[:, pl.ds(0, QUARTER)], near.at[:, pl.ds(QUARTER, HALF)]),
            (3, far.at[:, pl.ds(0, QUARTER)], far.at[:, pl.ds(QUARTER, HALF)]),
            (2, across_outer, across_inner),
        ):
            quarter = assist ^ distance
            copies.add(outer, w_ref.at[side, pl.ds(0, 3), pl.ds(quarter * QUARTER, QUARTER)])
            copies.add(inner, in_ref.at[side, pl.ds(0, 3), :, pl.ds(pl.multiple_of(quarter * D, D), D)])
    for half in range(2):
        side = half ^ meta_ref[CORE]
        copies.add(own_outer.at[pl.ds(half * 3 * QUARTER, 3 * QUARTER)], w_ref.at[side, 3, pl.ds(0, 3 * QUARTER)])
        copies.add(own_out.at[pl.ds(half * HALF, HALF)], w_ref.at[side, 3, pl.ds(OUT_AT, HALF)])
        copies.add(own_inner.at[pl.ds(half * HALF, HALF)], in_ref.at[side, 3])
    copies.add(own_norm, w_ref.at[meta_ref[CORE], 3, pl.ds(NORM_AT, QUARTER - HALF)])


def second_block(meta_ref, shard, half):
    apart = meta_ref[X] ^ shard
    place = jnp.where(apart == near_of(half), 0, jnp.where(apart == far_of(half), 1, 2))
    return half ^ meta_ref[CORE], jnp.where(apart == 0, 3, place)


def select_halves(meta_ref, value):
    half = value.shape[0] // 2
    low, high = value[:half].astype(LOW), value[half:].astype(LOW)
    first_core = meta_ref[CORE] == 0
    return jnp.where(first_core, low, high), jnp.where(first_core, high, low)


def heads_forward(meta_ref, first_pair, refs, probs_ref, ctx_ref):
    q_ref, k_ref, v_ref, pk_ref, pq_ref = refs
    length = meta_ref[LENGTH]
    valid = iota((ROWS, ROWS), 1) < length
    side = iota((ROWS, 2 * HEAD_DIM), 1) // HEAD_DIM

    def pair_step(pair, carry):
        out_cols = pl.ds(pl.multiple_of((pair - first_pair) * 2 * HEAD_DIM, 2 * HEAD_DIM), 2 * HEAD_DIM)
        cols = pl.ds(pl.multiple_of(pair * 2 * HEAD_DIM, 2 * HEAD_DIM), 2 * HEAD_DIM)
        q_pair, k_pair, v_pair = q_ref[:, cols], k_ref[:, cols], v_ref[:, cols]
        pk_pair, pq_pair = pk_ref[:, cols], pq_ref[:, cols]
        zero = jnp.zeros_like(q_pair)
        contexts = []
        for h in range(2):
            mine = side == h
            q_head = jnp.where(mine, q_pair, zero)
            k_head = jnp.where(mine, k_pair, zero)
            content = mm_nt(q_head, k_pair)
            to_off = mm_nt(q_head, pk_pair)
            from_off = mm_nt(k_head, pq_pair)
            to_rel = pltpu.roll(to_off, ROWS + 1, 1, stride=1, stride_axis=0)[:, :ROWS]
            from_rel = pltpu.roll(from_off, ROWS + 1, 1, stride=1, stride_axis=0)[:, :ROWS]
            scores = (content + to_rel + from_rel.T) * SCALING
            scores = jnp.where(valid, scores, MASKED)
            top = jnp.max(scores, axis=1, keepdims=True)
            shifted = jnp.exp(scores - top)
            summed = jnp.sum(shifted, axis=1, keepdims=True)
            probs = (shifted * (1.0 / summed)).astype(LOW)
            probs_ref[2 * (pair - first_pair) + h] = probs
            contexts.append(mm(probs, v_pair))
        ctx_ref[:, out_cols] = jnp.where(side == 0, contexts[0], contexts[1]).astype(LOW)
        return carry

    lax.fori_loop(first_pair, first_pair + PAIRS // 2, pair_step, 0)


def attend_forward_body(
    meta_ref, bucket_ref, rows_ref, own_q, own_k, own_v, own_rel, p0, p1, p2, p3, p4, p5,
    tok_ref, q_ref, k_ref, v_ref, pk_ref, pq_ref, relw_ref, probs_ref, ctx_ref,
    w_ref, rows_in, sem,
):
    copies = Copies(sem)
    copies.add(rows_ref.at[:, 0], rows_in)
    load_first(meta_ref, copies, (own_q, own_k, own_v, own_rel), (p0, p1, p2, p3, p4, p5), w_ref)
    copies.start()
    copies.wait()
    tok = rows_in[...].reshape(ROWS, D)
    tok_ref[...] = tok
    rel = whole(w_ref, REL_AT, REL_HALF)
    pick = (bucket_ref[...] == iota((OFFS, OFFS), 1)).astype(LOW)
    relw = mm(pick, rel).astype(LOW)
    relw_ref[...] = relw
    w_query = whole(w_ref, 0, HALF)
    q_ref[...] = mm(tok, w_query).astype(LOW)
    pq_ref[...] = mm(relw, w_query).astype(LOW)
    w_key = whole(w_ref, HALF, HALF)
    k_ref[...] = mm(tok, w_key).astype(LOW)
    pk_ref[...] = mm(relw, w_key).astype(LOW)
    v_ref[...] = mm(tok, whole(w_ref, 2 * HALF, HALF)).astype(LOW)
    heads_forward(meta_ref, 0, (q_ref, k_ref, v_ref, pk_ref, pq_ref), probs_ref, ctx_ref)


def attend_forward_two_body(meta_ref, q_ref, k_ref, v_ref, pk_ref, pq_ref, probs_ref, ctx_ref):
    heads_forward(meta_ref, PAIRS // 2, (q_ref, k_ref, v_ref, pk_ref, pq_ref), probs_ref, ctx_ref)


def attend_forward(meta, bucket_column, rows, own, pieces):
    shape = jax.ShapeDtypeStruct
    full, anywhere = pl.BlockSpec(memory_space=pltpu.VMEM), pl.BlockSpec(memory_space=pltpu.HBM)
    return pl.pallas_call(
        attend_forward_body,
        out_shape=(
            *(shape((ROWS, D), LOW),) * 4,
            shape((OFFS, D), LOW), shape((OFFS, D), LOW), shape((OFFS, D), LOW),
            shape((HEADS // 2, ROWS, ROWS), LOW), shape((ROWS, D // 2), LOW),
        ),
        in_specs=[pl.BlockSpec(memory_space=pltpu.SMEM), full] + [anywhere] * 11,
        out_specs=(full,) * 9,
        scratch_shapes=[
            pltpu.VMEM((GROUP, 2, FIRST, D), LOW), pltpu.VMEM((GROUP, PART, D), LOW), pltpu.SemaphoreType.DMA((11,)),
        ],
        compiler_params=pltpu.CompilerParams(vmem_limit_bytes=28 * MIB),
        cost_estimate=pl.CostEstimate(flops=12_000_000_000, bytes_accessed=40_000_000, transcendentals=800_000),
        name="attend_forward",
    )(meta, bucket_column, rows, *own, *pieces)


def attend_forward_two(meta, saved):
    shape = jax.ShapeDtypeStruct
    full = pl.BlockSpec(memory_space=pltpu.VMEM)
    return pl.pallas_call(
        attend_forward_two_body,
        out_shape=(shape((HEADS // 2, ROWS, ROWS), LOW), shape((ROWS, D // 2), LOW)),
        in_specs=[pl.BlockSpec(memory_space=pltpu.SMEM)] + [full] * 5,
        out_specs=(full,) * 2,
        compiler_params=pltpu.CompilerParams(vmem_limit_bytes=24 * MIB),
        cost_estimate=pl.CostEstimate(flops=8_000_000_000, bytes_accessed=20_000_000, transcendentals=400_000),
        name="attend_forward_two",
    )(meta, *saved)


def heads_back(first_pair, count, refs, outs):
    q_ref, k_ref, v_ref, pk_ref, pq_ref, probs_ref, gctx_ref = refs
    gq_ref, gk_ref, gv_ref, gpk_ref, gpq_ref, qr_ref, kr_ref = outs
    flip = (iota((ROWS, ROWS), 0) + iota((ROWS, ROWS), 1) == ROWS - 1).astype(LOW)
    qr_ref[...] = mm(flip, q_ref[...]).astype(LOW)
    kr_ref[...] = mm(flip, k_ref[...]).astype(LOW)
    side = iota((ROWS, 2 * HEAD_DIM), 1) // HEAD_DIM
    side_off = iota((OFFS, 2 * HEAD_DIM), 1) // HEAD_DIM
    blank = jnp.zeros((ROWS, OFFS - ROWS), F32)

    def pair_step(pair, carry):
        cols = pl.ds(pl.multiple_of(pair * 2 * HEAD_DIM, 2 * HEAD_DIM), 2 * HEAD_DIM)
        q_pair, k_pair, v_pair = q_ref[:, cols], k_ref[:, cols], v_ref[:, cols]
        pk_pair, pq_pair, gctx_pair = pk_ref[:, cols], pq_ref[:, cols], gctx_ref[:, cols]
        qr_pair, kr_pair = qr_ref[:, cols], kr_ref[:, cols]
        zero = jnp.zeros_like(q_pair)
        parts = []
        for h in range(2):
            gctx_head = jnp.where(side == h, gctx_pair, zero)
            grad_probs = mm_nt(gctx_head, v_pair)
            probs_low = probs_ref[2 * (pair - first_pair) + h]
            probs = probs_low.astype(F32)
            inner = jnp.sum(probs * grad_probs, axis=1, keepdims=True)
            grad_scores = (probs * (grad_probs - inner)).astype(LOW)
            g_value = mm_tn(probs_low, gctx_pair)
            rows_back = mm(flip, grad_scores)
            cols_back = mm_nt(flip, grad_scores)
            to_off = pltpu.roll(jnp.concatenate([rows_back, blank], axis=1), 0, 1, stride=1, stride_axis=0).astype(LOW)
            from_off = pltpu.roll(jnp.concatenate([cols_back, blank], axis=1), 0, 1, stride=1, stride_axis=0).astype(LOW)
            g_query = mm(rows_back.astype(LOW), k_pair) + mm(to_off, pk_pair)
            g_key = mm(cols_back.astype(LOW), q_pair) + mm(from_off, pq_pair)
            g_pk = mm_tn(to_off, qr_pair)
            g_pq = mm_tn(from_off, kr_pair)
            parts.append((g_value, g_query, g_key, g_pk, g_pq))
        first, second = parts
        gv_ref[:, cols] = jnp.where(side == 0, first[0], second[0]).astype(LOW)
        gq_ref[:, cols] = (jnp.where(side == 0, first[1], second[1]) * SCALING).astype(LOW)
        gk_ref[:, cols] = (jnp.where(side == 0, first[2], second[2]) * SCALING).astype(LOW)
        gpk_ref[:, cols] = (jnp.where(side_off == 0, first[3], second[3]) * SCALING).astype(LOW)
        gpq_ref[:, cols] = (jnp.where(side_off == 0, first[4], second[4]) * SCALING).astype(LOW)
        return carry

    lax.fori_loop(first_pair, first_pair + count, pair_step, 0)
    return flip


def attend_back_one_body(
    q_ref, k_ref, v_ref, pk_ref, pq_ref, probs_ref, gctx_ref,
    gq_ref, gk_ref, gv_ref, gpk_ref, gpq_ref, qr_ref, kr_ref,
):
    heads_back(
        0, PAIRS // 2, (q_ref, k_ref, v_ref, pk_ref, pq_ref, probs_ref, gctx_ref),
        (gq_ref, gk_ref, gv_ref, gpk_ref, gpq_ref, qr_ref, kr_ref),
    )


def attend_back_two_body(
    meta_ref, q_ref, k_ref, v_ref, pk_ref, pq_ref, probs_ref, gctx_ref, hq, hk, hv, hpk, hpq,
    tok_ref, relw_ref, gres_ref, bucket_ref,
    own_q, own_k, own_v, own_rel, p0, p1, p2, p3, p4, p5,
    out_ref,
    home_ref, keep_ref, send_ref,
    gq_ref, gk_ref, gv_ref, gpk_ref, gpq_ref, qr_ref, kr_ref, gtok_ref, w_ref, sem,
):
    copies = Copies(sem)
    load_first(meta_ref, copies, (own_q, own_k, own_v, own_rel), (p0, p1, p2, p3, p4, p5), w_ref)
    copies.start()
    for target, done in ((gq_ref, hq), (gk_ref, hk), (gv_ref, hv), (gpk_ref, hpk), (gpq_ref, hpq)):
        target[:, : D // 2] = done[...]
    flip = heads_back(
        PAIRS // 2, PAIRS // 2, (q_ref, k_ref, v_ref, pk_ref, pq_ref, probs_ref, gctx_ref),
        (gq_ref, gk_ref, gv_ref, gpk_ref, gpq_ref, qr_ref, kr_ref),
    )
    copies.wait()
    tok, relw = tok_ref[...], relw_ref[...]
    g_query = mm(flip, gq_ref[...]).astype(LOW)
    w_query = whole(w_ref, 0, HALF)
    g_tok = gres_ref[...] + mm_nt(g_query, w_query)
    g_rel = mm_nt(gpq_ref[...], w_query)

    x, core = meta_ref[X], meta_ref[CORE]

    def put(start, size, value):
        for shard in range(GROUP):
            keep, send = select_halves(meta_ref, value[shard * 2 * size : (shard + 1) * 2 * size])
            keep_ref[position(x ^ shard, near_of(core)), start : start + size] = keep
            send_ref[position(x ^ shard, far_of(core)), start : start + size] = send

    put(0, HALF, mm_tn(tok, g_query) + mm_tn(relw, gpq_ref[...]))
    g_key = mm(flip, gk_ref[...]).astype(LOW)
    w_key = whole(w_ref, HALF, HALF)
    g_tok = g_tok + mm_nt(g_key, w_key)
    g_rel = (g_rel + mm_nt(gpk_ref[...], w_key)).astype(LOW)
    put(HALF, HALF, mm_tn(tok, g_key) + mm_tn(relw, gpk_ref[...]))
    g_value = gv_ref[...]
    gtok_ref[...] = (g_tok + mm_nt(g_value, whole(w_ref, 2 * HALF, HALF))).astype(LOW)
    put(2 * HALF, HALF, mm_tn(tok, g_value))
    pick = (bucket_ref[...] == iota((OFFS, OFFS), 1)).astype(LOW)
    put(REL_AT, REL_HALF, mm_tn(pick, g_rel))
    for member in range(GROUP):
        home_ref[member, 0] = out_ref[member * PART : (member + 1) * PART, :]
        home_ref[member, 1] = gtok_ref[member * PART : (member + 1) * PART, :]


def attend_back_one(saved, gctx):
    shape = jax.ShapeDtypeStruct
    full = pl.BlockSpec(memory_space=pltpu.VMEM)
    return pl.pallas_call(
        attend_back_one_body,
        out_shape=(*(shape((ROWS, D // 2), LOW),) * 3, *(shape((OFFS, D // 2), LOW),) * 2),
        in_specs=[full] * 7,
        out_specs=(full,) * 5,
        scratch_shapes=[pltpu.VMEM((ROWS, D), LOW), pltpu.VMEM((ROWS, D), LOW)],
        compiler_params=pltpu.CompilerParams(vmem_limit_bytes=24 * MIB),
        cost_estimate=pl.CostEstimate(flops=8_000_000_000, bytes_accessed=20_000_000, transcendentals=0),
        name="attend_back_one",
    )(*saved, gctx)


def attend_back_two(meta, saved, gctx, half_done, tok, relw, gres, bucket_column, own, pieces, out):
    shape = jax.ShapeDtypeStruct
    full, anywhere = pl.BlockSpec(memory_space=pltpu.VMEM), pl.BlockSpec(memory_space=pltpu.HBM)
    return pl.pallas_call(
        attend_back_two_body,
        out_shape=(shape((GROUP, 2, PART, D), LOW), shape((GROUP, FIRST, D), LOW), shape((GROUP, FIRST, D), LOW)),
        in_specs=[pl.BlockSpec(memory_space=pltpu.SMEM)] + [full] * 16 + [anywhere] * 10 + [full],
        out_specs=(full,) * 3,
        scratch_shapes=[
            *(pltpu.VMEM((ROWS, D), LOW),) * 3, *(pltpu.VMEM((OFFS, D), LOW),) * 2, *(pltpu.VMEM((ROWS, D), LOW),) * 3,
            pltpu.VMEM((GROUP, 2, FIRST, D), LOW), pltpu.SemaphoreType.DMA((10,)),
        ],
        compiler_params=pltpu.CompilerParams(vmem_limit_bytes=36 * MIB),
        cost_estimate=pl.CostEstimate(flops=14_000_000_000, bytes_accessed=40_000_000, transcendentals=0),
        name="attend_back_two",
    )(meta, *saved, gctx, *half_done, tok, relw, gres, bucket_column, *own, *pieces, out)


def feed_body(
    meta_ref, tok_ref, ctx_one_ref, ctx_two_ref, rows_ref, own_outer, own_out, own_norm, own_inner, *rest,
):
    pieces, rest = rest[:10], rest[10:]
    out_ref, gctx_ref, gres_ref, keep_ref, send_ref, keep_in_ref, send_in_ref = rest[:7]
    up_ref, low_ref, act_ref, slope_ref, w_ref, in_ref, sem = rest[7:]
    copies = Copies(sem)
    copies.add(rows_ref.at[:, 1], up_ref)
    load_second(meta_ref, copies, (own_outer, own_out, own_norm, own_inner), pieces, w_ref, in_ref)
    copies.start()
    copies.wait()
    x, core = meta_ref[X], meta_ref[CORE]
    assist, assist_peer = assist_of(meta_ref, core), assist_of(meta_ref, 1 - core)

    def put_outer(shard, quarter, keep, send, start):
        rows = slice(start, start + keep.shape[0])
        keep_ref[position(assist ^ quarter, 1), position(x ^ shard, near_of(core)), rows] = keep
        send_ref[position(assist_peer ^ quarter, 1), position(x ^ shard, far_of(core)), rows] = send

    def put_inner(shard, quarter, keep, send):
        keep_in_ref[position(assist ^ quarter, 3), position(x ^ shard, near_of(core))] = keep
        send_in_ref[position(assist_peer ^ quarter, 3), position(x ^ shard, far_of(core))] = send

    length = meta_ref[LENGTH]
    mask = (iota((ROWS, 1), 0) < length).astype(F32)
    norm_rows = []
    for s in range(GROUP):
        side, place = second_block(meta_ref, s, 0)
        norm_rows.append(w_ref[side, place, NORM_AT : NORM_AT + QUARTER - HALF, :].astype(F32)[:1])
    gain_one, bias_one, gain_two, bias_two = (
        jnp.concatenate([row[:, i * PIECE : (i + 1) * PIECE] for row in norm_rows], axis=1) for i in range(4)
    )
    token = tok_ref[...].astype(F32)
    ctx = jnp.concatenate([ctx_one_ref[...], ctx_two_ref[...]], axis=1)
    blocks = [second_block(meta_ref, shard, half) for shard in range(GROUP) for half in range(2)]
    w_out = jnp.concatenate([w_ref[side, place, OUT_AT : OUT_AT + HALF, :] for side, place in blocks], axis=0)
    attn = mm(ctx, w_out)

    def norm(values):
        center = values - jnp.mean(values, axis=1, keepdims=True)
        inverse = lax.rsqrt(jnp.mean(center * center, axis=1, keepdims=True) + EPSILON)
        return center * inverse, inverse

    def norm_back(upstream, normed, inverse, gain):
        scaled = upstream * gain
        plain = jnp.mean(scaled, axis=1, keepdims=True)
        cross = jnp.mean(scaled * normed, axis=1, keepdims=True)
        return inverse * (scaled - plain - normed * cross)

    def total(values):
        return jnp.sum(values, axis=0, keepdims=True)

    normed_one, inverse_one = norm(token + attn)
    hidden_one = normed_one * gain_one + bias_one
    low_ref[...] = hidden_one.astype(LOW)

    def columns(c):
        return pl.ds(pl.multiple_of(c * D, D), D)

    def outer_rows(c):
        halves = [second_block(meta_ref, c, half) for half in range(2)]
        return jnp.concatenate([w_ref[side, place, 0 : D // 2, :] for side, place in halves], axis=0)

    def inner_columns(c):
        return jnp.concatenate([in_ref[side, place, :, columns(c)] for side, place in blocks], axis=0)

    def forward_step(c, ffn):
        inner = mm(low_ref[...], inner_columns(c))
        cumulative = 0.5 * (1.0 + lax.erf(inner * 0.5**0.5))
        density = jnp.exp(-0.5 * inner * inner) * 0.3989422804014327
        act = (inner * cumulative).astype(LOW)
        act_ref[c] = act
        slope_ref[c] = cumulative + inner * density
        return ffn + mm(act, outer_rows(c))

    ffn = lax.fori_loop(0, GROUP, forward_step, jnp.zeros((ROWS, D), F32))
    normed_two, inverse_two = norm(hidden_one + ffn)
    layer = (normed_two * gain_two + bias_two) * mask
    out_ref[...] = layer.astype(LOW)
    squares = [token * token * mask, attn * attn * mask, ffn * ffn * mask, layer * layer]
    sums = [jnp.sum(total(s), axis=1, keepdims=True) for s in squares]
    grad_y = up_ref[...].reshape(ROWS, D).astype(F32) * mask
    grad_gain_two = total(grad_y * normed_two)
    grad_bias_two = total(grad_y)
    grad_two = norm_back(grad_y, normed_two, inverse_two, gain_two)
    grad_ffn = grad_two.astype(LOW)

    def back_step(c, grad_hidden):
        grad_act = mm_nt(grad_ffn, outer_rows(c))
        grad_inner = (grad_act * slope_ref[c]).astype(LOW)
        keep, send = select_halves(meta_ref, mm_tn(act_ref[c], grad_ffn))
        for quarter in range(3):
            rows = slice(quarter * QUARTER, (quarter + 1) * QUARTER)
            put_outer(c, quarter, keep[rows], send[rows], 0)
        grad_w = mm_tn(low_ref[...], grad_inner)
        for s in range(GROUP):
            put_inner(s, c, *select_halves(meta_ref, grad_w[s * PIECE : (s + 1) * PIECE]))
        return grad_hidden + mm_nt(grad_inner, inner_columns(c))

    grad_hidden = lax.fori_loop(0, GROUP, back_step, grad_two)
    grad_gain_one = total(grad_hidden * normed_one)
    grad_bias_one = total(grad_hidden)
    grad_one = norm_back(grad_hidden, normed_one, inverse_one, gain_one)
    gres_ref[...] = grad_one
    grad_attn = grad_one.astype(LOW)
    grad_out = mm_tn(ctx, grad_attn)
    for s in range(GROUP):
        put_outer(s, 3, *select_halves(meta_ref, grad_out[s * PIECE : (s + 1) * PIECE]), 0)
    gctx_ref[...] = mm_nt(grad_attn, w_out).astype(LOW)
    lane = iota((1, D), 1)
    stats = jnp.zeros((1, D), F32)
    for i, value in enumerate(sums):
        stats = jnp.where(lane == i, value, stats)
    low = stats - stats.astype(LOW).astype(F32)
    zeros = jnp.zeros((1, D), F32)
    norm_rows = (grad_gain_one, grad_bias_one, grad_gain_two, grad_bias_two)
    for s in range(GROUP):
        row = jnp.concatenate([r[:, s * PIECE : (s + 1) * PIECE] for r in norm_rows], axis=1)
        block = jnp.concatenate([row] + [zeros] * 31 + [stats, low] + [zeros] * 30, axis=0)
        put_outer(s, 3, *select_halves(meta_ref, block), HALF)


def feed(meta, tok, ctx_one, ctx_two, rows, own, pieces):
    shape = jax.ShapeDtypeStruct
    full, anywhere = pl.BlockSpec(memory_space=pltpu.VMEM), pl.BlockSpec(memory_space=pltpu.HBM)
    block, wide = shape((GROUP, GROUP, QUARTER, D), LOW), shape((GROUP, GROUP, HALF, D), LOW)
    return pl.pallas_call(
        feed_body,
        out_shape=(
            shape((ROWS, D), LOW), shape((ROWS, D), LOW), shape((ROWS, D), F32), block, block, wide, wide
        ),
        in_specs=[pl.BlockSpec(memory_space=pltpu.SMEM)] + [full] * 3 + [anywhere] * 15,
        out_specs=(full,) * 7,
        scratch_shapes=[
            pltpu.VMEM((GROUP, PART, D), LOW), pltpu.VMEM((ROWS, D), LOW), pltpu.VMEM((GROUP, ROWS, D), LOW),
            pltpu.VMEM((GROUP, ROWS, D), F32), pltpu.VMEM((2, GROUP, SECOND, D), LOW),
            pltpu.VMEM((2, GROUP, HALF, WIDE), LOW), pltpu.SemaphoreType.DMA((24,)),
        ],
        compiler_params=pltpu.CompilerParams(vmem_limit_bytes=48 * MIB),
        cost_estimate=pl.CostEstimate(flops=16_000_000_000, bytes_accessed=60_000_000, transcendentals=1_600_000),
        name="feed",
    )(meta, tok, ctx_one, ctx_two, rows, *own, *pieces)


def finish_body(
    meta_ref, mine, other, rows_ref,
    q_ref, k_ref, v_ref, rel_ref, outer_ref, wout_ref, inner_ref, extra_ref, out_ref, gtok_ref,
):
    for piece, side in ((mine, 0), (other, 1)):
        core = meta_ref[CORE] if side == 0 else 1 - meta_ref[CORE]
        assist = assist_of(meta_ref, core)
        for i, ref in enumerate((q_ref, k_ref, v_ref, rel_ref)):
            size = REL_HALF if i == 3 else HALF
            ref[pl.ds(pl.multiple_of(core * size, size), size), :] = piece[i * HALF : i * HALF + size, :].astype(F32)
        for distance in range(GROUP):
            quarter = assist ^ distance
            at = FIRST + distance * SPAN
            block = piece[at : at + QUARTER, :].astype(F32)

            @pl.when(quarter < 3)
            def _():
                outer_ref[pl.ds(pl.multiple_of(core * 3 * QUARTER + quarter * QUARTER, QUARTER), QUARTER), :] = block

            @pl.when(quarter == 3)
            def _():
                wout_ref[pl.ds(pl.multiple_of(core * HALF, HALF), HALF), :] = block[:HALF]
                extra_ref[core] = block[HALF:]

            inner_ref[
                pl.ds(pl.multiple_of(core * HALF, HALF), HALF), pl.ds(pl.multiple_of(quarter * D, D), D)
            ] = piece[at + QUARTER : at + SPAN, :].astype(F32)
    for k in range(GROUP):
        member = meta_ref[X] ^ k
        out_ref[meta_ref[SEQ + k]] = rows_ref[member, 0]
        gtok_ref[meta_ref[SEQ + k]] = rows_ref[member, 1]


def finish(meta, mine, other, rows):
    shape = jax.ShapeDtypeStruct
    full = pl.BlockSpec(memory_space=pltpu.VMEM)
    return pl.pallas_call(
        finish_body,
        out_shape=(
            *(shape((PIECE, D), F32),) * 3, shape((OFFS // GROUP, D), F32),
            shape((D, D), F32), shape((PIECE, D), F32), shape((PIECE, WIDE), F32), shape((2, QUARTER - HALF, D), F32),
            *(shape((GROUP, PART, D), LOW),) * 2,
        ),
        in_specs=[pl.BlockSpec(memory_space=pltpu.SMEM)] + [full] * 3,
        out_specs=(full,) * 10,
        compiler_params=pltpu.CompilerParams(vmem_limit_bytes=24 * MIB),
        name="finish",
    )(meta, mine, other, rows)


NEAR, FAR = (1, 3), (3, 1)


def hop_x(value, flips):
    pairs = [(c * 4 + i, c * 4 + (i ^ flips[c])) for c in range(2) for i in range(4)]
    return lax.ppermute(value, ("core", "shard"), pairs)


def hop_yz(value, flip, swapped=False):
    pairs = []
    for y in range(4):
        for z in range(4):
            for c in range(2):
                along_y = (c == 0) != swapped
                ty, tz = (y ^ flip, z) if along_y else (y, z ^ flip)
                pairs.append(((y * 4 + z) * 2 + c, (ty * 4 + tz) * 2 + c))
    return lax.ppermute(value, ("y", "z", "core"), pairs)


def swap(value):
    return lax.ppermute(value, "core", [(0, 1), (1, 0)])


def after(value, *others):
    return lax.optimization_barrier((value, *others))[0]


def add(*values):
    total = values[0].astype(F32)
    for value in values[1:]:
        total = total + value.astype(F32)
    return total.astype(LOW)


def exchange_rows(rows):
    return lax.all_to_all(rows, "shard", split_axis=0, concat_axis=0, tiled=True)


def shards(
    hidden, grad_out, lengths, bucket, w_query, w_key, w_value, w_out, w_inner, w_outer, rel_table,
    ln1_gain, ln1_bias, ln2_gain, ln2_bias,
):
    coords = jnp.stack([lax.axis_index(name) for name in ("shard", "y", "z", "core")]).astype(jnp.int32)
    norm_block = jnp.concatenate(
        [jnp.concatenate([ln1_gain, ln1_bias, ln2_gain, ln2_bias])[None], jnp.zeros((31, D), LOW)], axis=0
    )
    bucket_column = jnp.concatenate([bucket[::-1], jnp.full((1,), -1, jnp.int32)])[:, None]
    own_first = (w_query, w_key, w_value, rel_table)
    own_halves = tuple(ref.reshape(2, ref.shape[0] // 2, D) for ref in own_first)
    meta, first, second, rows = pack(
        coords, lengths, hidden, grad_out, own_first, (w_outer, w_out, w_inner), norm_block
    )
    near_two, far_two = hop_x(second, NEAR), hop_x(second, FAR)
    near, far = hop_x(first, NEAR), hop_x(first, FAR)
    rows = exchange_rows(rows)
    across_two = hop_x(near_two, FAR)
    base = after(jnp.stack([near_two, far_two, across_two]), near, far)
    base_near, base_far = hop_yz(base, 1), hop_yz(base, 3)
    across = hop_x(near, FAR)
    pieces = (near, far, across, swap(near), swap(far), swap(across))
    part_outer, part_inner = base_near[:, :QUARTER], base_far[:, QUARTER:]
    rows = after(rows, part_outer, part_inner)
    across_outer, across_inner = hop_yz(part_outer, 3), hop_yz(part_inner, 1)
    tok, *saved, relw, probs, ctx = attend_forward(meta, bucket_column, rows, own_halves, pieces)
    across_outer, across_inner, base, base_near, base_far, _ = lax.optimization_barrier(
        (across_outer, across_inner, base, base_near, base_far, ctx)
    )
    arrived = (base, base_near, base_far, across_outer, across_inner)
    swapped = tuple(swap(piece) for piece in arrived)
    probs_two, ctx_two = attend_forward_two(meta, saved)
    swapped = after(swapped, ctx_two)
    out, gctx, gres, keep, send, keep_in, send_in = feed(
        meta, tok, ctx, ctx_two, rows, (w_outer, w_out, norm_block, w_inner), (*arrived, *swapped)
    )
    other, other_in = swap(send), swap(send_in)
    half_done = attend_back_one((*saved, probs), gctx)
    leave = add(keep[:2], other[:2])
    leave_in = add(keep_in[:2], other_in[:2])
    came, came_in = hop_yz(leave, 1), hop_yz(leave_in, 3)
    half_done = after(tuple(half_done), leave, leave_in)
    leaving, keep_one, send_one = attend_back_two(
        meta, (*saved, probs_two), gctx, half_done, tok, relw, gres, bucket_column, own_halves, pieces, out
    )
    other_one = swap(after(send_one, came, came_in))
    last = hop_yz(add(keep[2], other[2], came[0]), 3)
    last_in = hop_yz(add(keep_in[2], other_in[2], came_in[0]), 1)
    leave_one = add(keep_one[:2], other_one[:2])
    came_one = hop_x(leave_one, NEAR)
    came_one = after(came_one, last, last_in)
    leave_two = add(keep_one[2], other_one[2], came_one[0])
    last_one = hop_x(leave_two, FAR)
    last, last_in, _ = lax.optimization_barrier((last, last_in, leave_two))
    mine = add(keep[3], other[3], came[1], last)
    mine_in = add(keep_in[3], other_in[3], came_in[1], last_in)
    both = jnp.concatenate([mine, mine_in], axis=1)
    came_x = hop_x(both[:2], NEAR)
    home = exchange_rows(leaving)
    last_one = after(last_one, came_x)
    mine_one = add(keep_one[3], other_one[3], came_one[1], last_one)
    come_one = hop_yz(mine_one, 1, swapped=True)
    last_x = hop_x(after(add(both[2], came_x[0]), mine_one), FAR)
    mine_one = add(mine_one, after(come_one, last_x))
    come_one = hop_yz(mine_one, 3, swapped=True)
    both = after(add(both[3], came_x[1], last_x), mine_one)
    step = hop_yz(both, 1, swapped=True)
    mine_one = add(mine_one, after(come_one, step))
    come_one = hop_yz(mine_one, 1)
    both = after(add(both, step), mine_one)
    step = hop_yz(both, 3, swapped=True)
    mine_one = add(mine_one, after(come_one, step))
    come_one = hop_yz(mine_one, 3)
    both = after(add(both, step), mine_one)
    both = [both, *(hop_yz(both, flip) for flip in (1, 3, 2))]
    both[1], both[2], both[3] = both[1], both[3], both[2]
    mine_one = add(mine_one, come_one)
    packed = after(jnp.concatenate([mine_one, *both], axis=0), home)
    q_grad, k_grad, v_grad, rel_grad, outer_grad, out_grad, inner_grad, extra, layer_output, grad_hidden = finish(
        meta, packed, swap(packed), home
    )
    norm_sums = extra[0, 0].reshape(GROUP, PIECE)
    stats = extra[1, 0, :GROUP] + extra[1, 1, :GROUP]
    return (
        layer_output, grad_hidden, q_grad, k_grad, v_grad, out_grad, inner_grad, outer_grad, rel_grad,
        norm_sums[0], norm_sums[1], norm_sums[2], norm_sums[3],
        jnp.sqrt(stats / (TOKENS * D)),
    )


def solution(mesh):
    split = Mesh(mesh.devices.reshape(4, 4, 2, 4), ("y", "z", "core", "shard"))
    rep = ("y", "z", "core")
    rows, vector = P("shard", None), P("shard")
    batch = P(rep, "shard", None)
    return jax.shard_map(
        shards,
        mesh=split,
        in_specs=(batch, batch, P(rep), P(), *(rows,) * 7, *(vector,) * 4),
        out_specs=(batch, batch, *(rows,) * 7, *(vector,) * 4, P()),
        check_vma=False,
    )
```

```python
import jax
import jax.numpy as jnp
from jax import lax
from jax.experimental import pallas as pl
from jax.experimental.pallas import tpu as pltpu
from jax.sharding import Mesh
from jax.sharding import PartitionSpec as P

D = 768
HEADS = 12
HEAD_DIM = 64
PAIRS = HEADS // 2
ROWS = 256
OFFS = 512
TOKENS = 20480
GROUP = 4
PIECE = D // GROUP
HALF = PIECE // 2
WIDE = GROUP * D
REL_HALF = OFFS // GROUP // 2
REL_AT = 3 * HALF
FIRST = 3 * HALF + REL_HALF
OUT_AT = D // 2
NORM_AT = D // 2 + HALF
QUARTER = 128
SECOND = GROUP * QUARTER
SPAN = QUARTER + HALF
PART = ROWS // GROUP
X, Y, Z, CORE, LENGTH, SEQ = 0, 1, 2, 3, 4, 5
META = 16
EPSILON = 1e-07
MASKED = -1e30
SCALING = (3.0 * HEAD_DIM) ** (-0.5)
F32 = jnp.float32
LOW = jnp.bfloat16
MIB = 1024 * 1024


def mm(a, b):
    return lax.dot_general(a, b, (((1,), (0,)), ((), ())), preferred_element_type=F32)


def mm_nt(a, b):
    return lax.dot_general(a, b, (((1,), (1,)), ((), ())), preferred_element_type=F32)


def mm_tn(a, b):
    return lax.dot_general(a, b, (((0,), (0,)), ((), ())), preferred_element_type=F32)


def iota(shape, dim):
    return lax.broadcasted_iota(jnp.int32, shape, dim)


def whole(ref, start, size):
    piece = ref[:, :, start : start + size, :]
    return piece.reshape(GROUP * 2 * size, piece.shape[3])


def run_copies(copies):
    for copy in copies:
        copy.start()
    for copy in copies:
        copy.wait()


class Copies:
    def __init__(self, sem):
        self.sem, self.made = sem, []

    def add(self, source, target):
        self.made.append(pltpu.make_async_copy(source, target, self.sem.at[len(self.made)]))

    def start(self):
        for copy in self.made:
            copy.start()

    def wait(self):
        for copy in self.made:
            copy.wait()


def near_of(core):
    return 1 + 2 * core


def far_of(core):
    return 3 - 2 * core


def assist_of(meta_ref, core):
    return jnp.where(core == 0, meta_ref[Y], meta_ref[Z])


def position(distance, near):
    far = 4 - near
    place = jnp.where(distance == near, 1, jnp.where(distance == far, 2, 0))
    return jnp.where(distance == 0, 3, place)


def pack_body(
    coord_ref, length_ref, hidden_ref, grad_ref, own_q, own_k, own_v, own_rel, own_outer, own_out, own_inner, norm_ref,
    meta_ref, first_ref, second_ref, *rest,
):
    rows_out, sem, tail_sem = rest
    x, y, z, core = (coord_ref[i] for i in range(4))
    for i in range(4):
        meta_ref[i] = coord_ref[i]
    lengths = [length_ref[i] for i in range(GROUP)]
    dealing = []
    for i in range(GROUP):
        rank = jnp.int32(0)
        for j in range(GROUP):
            if j != i:
                ahead = lengths[j] >= lengths[i] if j < i else lengths[j] > lengths[i]
                rank = rank + ahead.astype(jnp.int32)
        dealing.append(rank)
    length = jnp.int32(0)
    for i in range(GROUP):
        length = length + jnp.where(dealing[i] == x, lengths[i], 0)
    meta_ref[LENGTH] = length
    copies = Copies(sem)
    for k in range(GROUP):
        source = jnp.int32(0)
        for i in range(GROUP):
            source = source + jnp.where(dealing[i] == (x ^ k), i, 0)
        meta_ref[SEQ + k] = source
        copies.add(hidden_ref.at[source], rows_out.at[x ^ k, 0])
        copies.add(grad_ref.at[source], rows_out.at[x ^ k, 1])
    for i in range(SEQ + GROUP, META):
        meta_ref[i] = jnp.int32(0)
    for i, ref in enumerate((own_q, own_k, own_v, own_rel)):
        size = REL_HALF if i == 3 else HALF
        copies.add(ref.at[pl.ds(core * size, size)], first_ref.at[pl.ds(i * HALF, size)])
    quarter = jnp.where(core == 0, y, z)
    copies.add(
        own_inner.at[pl.ds(core * HALF, HALF), pl.ds(pl.multiple_of(quarter * D, D), D)],
        second_ref.at[pl.ds(QUARTER, HALF)],
    )
    copies.start()
    tail = Copies(tail_sem)

    @pl.when(quarter < 3)
    def _():
        copy = pltpu.make_async_copy(
            own_outer.at[pl.ds(core * 3 * QUARTER + quarter * QUARTER, QUARTER)], second_ref.at[pl.ds(0, QUARTER)],
            tail_sem.at[0],
        )
        copy.start()
        copy.wait()

    @pl.when(quarter == 3)
    def _():
        tail.add(own_out.at[pl.ds(core * HALF, HALF)], second_ref.at[pl.ds(0, HALF)])
        tail.add(norm_ref, second_ref.at[pl.ds(HALF, QUARTER - HALF)])
        tail.start()
        tail.wait()

    copies.wait()


def pack(coords, lengths, hidden, grad_out, own_first, own_second, norm_block):
    shape = jax.ShapeDtypeStruct
    scalars, anywhere = pl.BlockSpec(memory_space=pltpu.SMEM), pl.BlockSpec(memory_space=pltpu.HBM)
    full = pl.BlockSpec(memory_space=pltpu.VMEM)
    return pl.pallas_call(
        pack_body,
        out_shape=(
            shape((META,), jnp.int32), shape((FIRST, D), LOW), shape((SPAN, D), LOW), shape((GROUP, 2, PART, D), LOW),
        ),
        in_specs=[scalars, scalars] + [anywhere] * 10,
        out_specs=(scalars, full, full, full),
        scratch_shapes=[pltpu.SemaphoreType.DMA((13,)), pltpu.SemaphoreType.DMA((2,))],
        compiler_params=pltpu.CompilerParams(vmem_limit_bytes=60 * MIB),
        name="pack",
    )(coords, lengths, hidden, grad_out, *own_first, *own_second, norm_block)


def load_first(meta_ref, copies, own, pieces, w_ref):
    x, core = meta_ref[X], meta_ref[CORE]
    near, far = x ^ near_of(core), x ^ far_of(core)
    slots = ((near, core), (far, core), (x ^ 2, core), (far, 1 - core), (near, 1 - core), (x ^ 2, 1 - core))
    for piece, (slot, half) in zip(pieces, slots):
        copies.add(piece, w_ref.at[slot, half])
    for i, ref in enumerate(own):
        size = REL_HALF if i == 3 else HALF
        copies.add(ref, w_ref.at[x, :, pl.ds(i * HALF, size)])


def load_second(meta_ref, copies, own, pieces, w_ref, in_ref):
    own_outer, own_out, own_norm, own_inner = own
    for side in range(2):
        assist = assist_of(meta_ref, meta_ref[CORE] if side == 0 else 1 - meta_ref[CORE])
        base, near, far, across_outer, across_inner = pieces[5 * side : 5 * side + 5]
        for distance, outer, inner in (
            (0, base.at[:, pl.ds(0, QUARTER)], base.at[:, pl.ds(QUARTER, HALF)]),
            (1, near.at[:, pl.ds(0, QUARTER)], near.at[:, pl.ds(QUARTER, HALF)]),
            (3, far.at[:, pl.ds(0, QUARTER)], far.at[:, pl.ds(QUARTER, HALF)]),
            (2, across_outer, across_inner),
        ):
            quarter = assist ^ distance
            copies.add(outer, w_ref.at[side, pl.ds(0, 3), pl.ds(quarter * QUARTER, QUARTER)])
            copies.add(inner, in_ref.at[side, pl.ds(0, 3), :, pl.ds(pl.multiple_of(quarter * D, D), D)])
    for half in range(2):
        side = half ^ meta_ref[CORE]
        copies.add(own_outer.at[pl.ds(half * 3 * QUARTER, 3 * QUARTER)], w_ref.at[side, 3, pl.ds(0, 3 * QUARTER)])
        copies.add(own_out.at[pl.ds(half * HALF, HALF)], w_ref.at[side, 3, pl.ds(OUT_AT, HALF)])
        copies.add(own_inner.at[pl.ds(half * HALF, HALF)], in_ref.at[side, 3])
    copies.add(own_norm, w_ref.at[meta_ref[CORE], 3, pl.ds(NORM_AT, QUARTER - HALF)])


def second_block(meta_ref, shard, half):
    apart = meta_ref[X] ^ shard
    place = jnp.where(apart == near_of(half), 0, jnp.where(apart == far_of(half), 1, 2))
    return half ^ meta_ref[CORE], jnp.where(apart == 0, 3, place)


def select_halves(meta_ref, value):
    half = value.shape[0] // 2
    low, high = value[:half].astype(LOW), value[half:].astype(LOW)
    first_core = meta_ref[CORE] == 0
    return jnp.where(first_core, low, high), jnp.where(first_core, high, low)


def heads_forward(meta_ref, first_pair, refs, probs_ref, ctx_ref):
    q_ref, k_ref, v_ref, pk_ref, pq_ref = refs
    length = meta_ref[LENGTH]
    valid = iota((ROWS, ROWS), 1) < length
    side = iota((ROWS, 2 * HEAD_DIM), 1) // HEAD_DIM

    def pair_step(pair, carry):
        out_cols = pl.ds(pl.multiple_of((pair - first_pair) * 2 * HEAD_DIM, 2 * HEAD_DIM), 2 * HEAD_DIM)
        cols = pl.ds(pl.multiple_of(pair * 2 * HEAD_DIM, 2 * HEAD_DIM), 2 * HEAD_DIM)
        q_pair, k_pair, v_pair = q_ref[:, cols], k_ref[:, cols], v_ref[:, cols]
        pk_pair, pq_pair = pk_ref[:, cols], pq_ref[:, cols]
        zero = jnp.zeros_like(q_pair)
        contexts = []
        for h in range(2):
            mine = side == h
            q_head = jnp.where(mine, q_pair, zero)
            k_head = jnp.where(mine, k_pair, zero)
            content = mm_nt(q_head, k_pair)
            to_off = mm_nt(q_head, pk_pair)
            from_off = mm_nt(k_head, pq_pair)
            to_rel = pltpu.roll(to_off, ROWS + 1, 1, stride=1, stride_axis=0)[:, :ROWS]
            from_rel = pltpu.roll(from_off, ROWS + 1, 1, stride=1, stride_axis=0)[:, :ROWS]
            scores = (content + to_rel + from_rel.T) * SCALING
            scores = jnp.where(valid, scores, MASKED)
            top = jnp.max(scores, axis=1, keepdims=True)
            shifted = jnp.exp(scores - top)
            summed = jnp.sum(shifted, axis=1, keepdims=True)
            probs = (shifted * (1.0 / summed)).astype(LOW)
            probs_ref[2 * (pair - first_pair) + h] = probs
            contexts.append(mm(probs, v_pair))
        ctx_ref[:, out_cols] = jnp.where(side == 0, contexts[0], contexts[1]).astype(LOW)
        return carry

    lax.fori_loop(first_pair, first_pair + PAIRS // 2, pair_step, 0)


def attend_forward_body(
    meta_ref, bucket_ref, rows_ref, own_q, own_k, own_v, own_rel, p0, p1, p2, p3, p4, p5,
    tok_ref, q_ref, k_ref, v_ref, pk_ref, pq_ref, relw_ref, probs_ref, ctx_ref,
    w_ref, rows_in, sem,
):
    copies = Copies(sem)
    copies.add(rows_ref.at[:, 0], rows_in)
    load_first(meta_ref, copies, (own_q, own_k, own_v, own_rel), (p0, p1, p2, p3, p4, p5), w_ref)
    copies.start()
    copies.wait()
    tok = rows_in[...].reshape(ROWS, D)
    tok_ref[...] = tok
    rel = whole(w_ref, REL_AT, REL_HALF)
    pick = (bucket_ref[...] == iota((OFFS, OFFS), 1)).astype(LOW)
    relw = mm(pick, rel).astype(LOW)
    relw_ref[...] = relw
    w_query = whole(w_ref, 0, HALF)
    q_ref[...] = mm(tok, w_query).astype(LOW)
    pq_ref[...] = mm(relw, w_query).astype(LOW)
    w_key = whole(w_ref, HALF, HALF)
    k_ref[...] = mm(tok, w_key).astype(LOW)
    pk_ref[...] = mm(relw, w_key).astype(LOW)
    v_ref[...] = mm(tok, whole(w_ref, 2 * HALF, HALF)).astype(LOW)
    heads_forward(meta_ref, 0, (q_ref, k_ref, v_ref, pk_ref, pq_ref), probs_ref, ctx_ref)


def attend_forward_two_body(meta_ref, q_ref, k_ref, v_ref, pk_ref, pq_ref, probs_ref, ctx_ref):
    heads_forward(meta_ref, PAIRS // 2, (q_ref, k_ref, v_ref, pk_ref, pq_ref), probs_ref, ctx_ref)


def attend_forward(meta, bucket_column, rows, own, pieces):
    shape = jax.ShapeDtypeStruct
    full, anywhere = pl.BlockSpec(memory_space=pltpu.VMEM), pl.BlockSpec(memory_space=pltpu.HBM)
    return pl.pallas_call(
        attend_forward_body,
        out_shape=(
            *(shape((ROWS, D), LOW),) * 4,
            shape((OFFS, D), LOW), shape((OFFS, D), LOW), shape((OFFS, D), LOW),
            shape((HEADS // 2, ROWS, ROWS), LOW), shape((ROWS, D // 2), LOW),
        ),
        in_specs=[pl.BlockSpec(memory_space=pltpu.SMEM), full] + [anywhere] * 11,
        out_specs=(full,) * 9,
        scratch_shapes=[
            pltpu.VMEM((GROUP, 2, FIRST, D), LOW), pltpu.VMEM((GROUP, PART, D), LOW), pltpu.SemaphoreType.DMA((11,)),
        ],
        compiler_params=pltpu.CompilerParams(vmem_limit_bytes=28 * MIB),
        cost_estimate=pl.CostEstimate(flops=12_000_000_000, bytes_accessed=40_000_000, transcendentals=800_000),
        name="attend_forward",
    )(meta, bucket_column, rows, *own, *pieces)


def attend_forward_two(meta, saved):
    shape = jax.ShapeDtypeStruct
    full = pl.BlockSpec(memory_space=pltpu.VMEM)
    return pl.pallas_call(
        attend_forward_two_body,
        out_shape=(shape((HEADS // 2, ROWS, ROWS), LOW), shape((ROWS, D // 2), LOW)),
        in_specs=[pl.BlockSpec(memory_space=pltpu.SMEM)] + [full] * 5,
        out_specs=(full,) * 2,
        compiler_params=pltpu.CompilerParams(vmem_limit_bytes=24 * MIB),
        cost_estimate=pl.CostEstimate(flops=8_000_000_000, bytes_accessed=20_000_000, transcendentals=400_000),
        name="attend_forward_two",
    )(meta, *saved)


def heads_back(first_pair, count, refs, outs):
    q_ref, k_ref, v_ref, pk_ref, pq_ref, probs_ref, gctx_ref = refs
    gq_ref, gk_ref, gv_ref, gpk_ref, gpq_ref, qr_ref, kr_ref = outs
    flip = (iota((ROWS, ROWS), 0) + iota((ROWS, ROWS), 1) == ROWS - 1).astype(LOW)
    qr_ref[...] = mm(flip, q_ref[...]).astype(LOW)
    kr_ref[...] = mm(flip, k_ref[...]).astype(LOW)
    side = iota((ROWS, 2 * HEAD_DIM), 1) // HEAD_DIM
    side_off = iota((OFFS, 2 * HEAD_DIM), 1) // HEAD_DIM
    blank = jnp.zeros((ROWS, OFFS - ROWS), F32)

    def pair_step(pair, carry):
        cols = pl.ds(pl.multiple_of(pair * 2 * HEAD_DIM, 2 * HEAD_DIM), 2 * HEAD_DIM)
        q_pair, k_pair, v_pair = q_ref[:, cols], k_ref[:, cols], v_ref[:, cols]
        pk_pair, pq_pair, gctx_pair = pk_ref[:, cols], pq_ref[:, cols], gctx_ref[:, cols]
        qr_pair, kr_pair = qr_ref[:, cols], kr_ref[:, cols]
        zero = jnp.zeros_like(q_pair)
        parts = []
        for h in range(2):
            gctx_head = jnp.where(side == h, gctx_pair, zero)
            grad_probs = mm_nt(gctx_head, v_pair)
            probs_low = probs_ref[2 * (pair - first_pair) + h]
            probs = probs_low.astype(F32)
            inner = jnp.sum(probs * grad_probs, axis=1, keepdims=True)
            grad_scores = (probs * (grad_probs - inner)).astype(LOW)
            g_value = mm_tn(probs_low, gctx_pair)
            rows_back = mm(flip, grad_scores)
            cols_back = mm_nt(flip, grad_scores)
            to_off = pltpu.roll(jnp.concatenate([rows_back, blank], axis=1), 0, 1, stride=1, stride_axis=0).astype(LOW)
            from_off = pltpu.roll(jnp.concatenate([cols_back, blank], axis=1), 0, 1, stride=1, stride_axis=0).astype(LOW)
            g_query = mm(rows_back.astype(LOW), k_pair) + mm(to_off, pk_pair)
            g_key = mm(cols_back.astype(LOW), q_pair) + mm(from_off, pq_pair)
            g_pk = mm_tn(to_off, qr_pair)
            g_pq = mm_tn(from_off, kr_pair)
            parts.append((g_value, g_query, g_key, g_pk, g_pq))
        first, second = parts
        gv_ref[:, cols] = jnp.where(side == 0, first[0], second[0]).astype(LOW)
        gq_ref[:, cols] = (jnp.where(side == 0, first[1], second[1]) * SCALING).astype(LOW)
        gk_ref[:, cols] = (jnp.where(side == 0, first[2], second[2]) * SCALING).astype(LOW)
        gpk_ref[:, cols] = (jnp.where(side_off == 0, first[3], second[3]) * SCALING).astype(LOW)
        gpq_ref[:, cols] = (jnp.where(side_off == 0, first[4], second[4]) * SCALING).astype(LOW)
        return carry

    lax.fori_loop(first_pair, first_pair + count, pair_step, 0)
    return flip


def attend_back_one_body(
    q_ref, k_ref, v_ref, pk_ref, pq_ref, probs_ref, gctx_ref,
    gq_ref, gk_ref, gv_ref, gpk_ref, gpq_ref, qr_ref, kr_ref,
):
    heads_back(
        0, PAIRS // 2, (q_ref, k_ref, v_ref, pk_ref, pq_ref, probs_ref, gctx_ref),
        (gq_ref, gk_ref, gv_ref, gpk_ref, gpq_ref, qr_ref, kr_ref),
    )


def attend_back_two_body(
    meta_ref, q_ref, k_ref, v_ref, pk_ref, pq_ref, probs_ref, gctx_ref, hq, hk, hv, hpk, hpq,
    tok_ref, relw_ref, gres_ref, bucket_ref,
    own_q, own_k, own_v, own_rel, p0, p1, p2, p3, p4, p5,
    out_ref,
    home_ref, keep_ref, send_ref,
    grad_ref, gv_ref, pos_ref, qr_ref, kr_ref, gtok_ref, w_ref, sem,
):
    gq_ref, gk_ref, gpq_ref, gpk_ref = grad_ref.at[0], grad_ref.at[1], pos_ref.at[0], pos_ref.at[1]
    copies = Copies(sem)
    load_first(meta_ref, copies, (own_q, own_k, own_v, own_rel), (p0, p1, p2, p3, p4, p5), w_ref)
    copies.start()
    for target, done in ((gq_ref, hq), (gk_ref, hk), (gv_ref, hv), (gpk_ref, hpk), (gpq_ref, hpq)):
        target[:, : D // 2] = done[...]
    flip = heads_back(
        PAIRS // 2, PAIRS // 2, (q_ref, k_ref, v_ref, pk_ref, pq_ref, probs_ref, gctx_ref),
        (gq_ref, gk_ref, gv_ref, gpk_ref, gpq_ref, qr_ref, kr_ref),
    )
    copies.wait()
    tok, relw = tok_ref[...], relw_ref[...]
    x, core = meta_ref[X], meta_ref[CORE]

    def put(start, size, value):
        for shard in range(GROUP):
            keep, send = select_halves(meta_ref, value[shard * 2 * size : (shard + 1) * 2 * size])
            keep_ref[position(x ^ shard, near_of(core)), pl.ds(start, size)] = keep
            send_ref[position(x ^ shard, far_of(core)), pl.ds(start, size)] = send

    def weight_step(i, carry):
        g_tok, g_rel = carry
        start = pl.multiple_of(i * HALF, HALF)
        grads = mm(flip, grad_ref[i]).astype(LOW)
        weight = w_ref[:, :, pl.ds(start, HALF), :].reshape(D, D)
        put(start, HALF, mm_tn(tok, grads) + mm_tn(relw, pos_ref[i]))
        return g_tok + mm_nt(grads, weight), g_rel + mm_nt(pos_ref[i], weight)

    g_tok, g_rel = lax.fori_loop(0, 2, weight_step, (gres_ref[...], jnp.zeros((OFFS, D), F32)))
    g_value = gv_ref[...]
    gtok_ref[...] = (g_tok + mm_nt(g_value, whole(w_ref, 2 * HALF, HALF))).astype(LOW)
    put(2 * HALF, HALF, mm_tn(tok, g_value))
    pick = (bucket_ref[...] == iota((OFFS, OFFS), 1)).astype(LOW)
    put(REL_AT, REL_HALF, mm_tn(pick, g_rel.astype(LOW)))
    for member in range(GROUP):
        home_ref[member, 0] = out_ref[member * PART : (member + 1) * PART, :]
        home_ref[member, 1] = gtok_ref[member * PART : (member + 1) * PART, :]


def attend_back_one(saved, gctx):
    shape = jax.ShapeDtypeStruct
    full = pl.BlockSpec(memory_space=pltpu.VMEM)
    return pl.pallas_call(
        attend_back_one_body,
        out_shape=(*(shape((ROWS, D // 2), LOW),) * 3, *(shape((OFFS, D // 2), LOW),) * 2),
        in_specs=[full] * 7,
        out_specs=(full,) * 5,
        scratch_shapes=[pltpu.VMEM((ROWS, D), LOW), pltpu.VMEM((ROWS, D), LOW)],
        compiler_params=pltpu.CompilerParams(vmem_limit_bytes=24 * MIB),
        cost_estimate=pl.CostEstimate(flops=8_000_000_000, bytes_accessed=20_000_000, transcendentals=0),
        name="attend_back_one",
    )(*saved, gctx)


def attend_back_two(meta, saved, gctx, half_done, tok, relw, gres, bucket_column, own, pieces, out):
    shape = jax.ShapeDtypeStruct
    full, anywhere = pl.BlockSpec(memory_space=pltpu.VMEM), pl.BlockSpec(memory_space=pltpu.HBM)
    return pl.pallas_call(
        attend_back_two_body,
        out_shape=(shape((GROUP, 2, PART, D), LOW), shape((GROUP, FIRST, D), LOW), shape((GROUP, FIRST, D), LOW)),
        in_specs=[pl.BlockSpec(memory_space=pltpu.SMEM)] + [full] * 16 + [anywhere] * 10 + [full],
        out_specs=(full,) * 3,
        scratch_shapes=[
            pltpu.VMEM((2, ROWS, D), LOW), pltpu.VMEM((ROWS, D), LOW), pltpu.VMEM((2, OFFS, D), LOW),
            *(pltpu.VMEM((ROWS, D), LOW),) * 3,
            pltpu.VMEM((GROUP, 2, FIRST, D), LOW), pltpu.SemaphoreType.DMA((10,)),
        ],
        compiler_params=pltpu.CompilerParams(vmem_limit_bytes=22 * MIB),
        cost_estimate=pl.CostEstimate(flops=14_000_000_000, bytes_accessed=40_000_000, transcendentals=0),
        name="attend_back_two",
    )(meta, *saved, gctx, *half_done, tok, relw, gres, bucket_column, *own, *pieces, out)


def feed_body(
    meta_ref, tok_ref, ctx_one_ref, ctx_two_ref, rows_ref, own_outer, own_out, own_norm, own_inner, *rest,
):
    pieces, rest = rest[:10], rest[10:]
    out_ref, gctx_ref, gres_ref, keep_ref, send_ref, keep_in_ref, send_in_ref = rest[:7]
    up_ref, low_ref, act_ref, slope_ref, w_ref, in_ref, sem = rest[7:]
    copies = Copies(sem)
    copies.add(rows_ref.at[:, 1], up_ref)
    load_second(meta_ref, copies, (own_outer, own_out, own_norm, own_inner), pieces, w_ref, in_ref)
    copies.start()
    copies.wait()
    x, core = meta_ref[X], meta_ref[CORE]
    assist, assist_peer = assist_of(meta_ref, core), assist_of(meta_ref, 1 - core)

    def put_outer(shard, quarter, keep, send, start):
        rows = slice(start, start + keep.shape[0])
        keep_ref[position(assist ^ quarter, 1), position(x ^ shard, near_of(core)), rows] = keep
        send_ref[position(assist_peer ^ quarter, 1), position(x ^ shard, far_of(core)), rows] = send

    def put_inner(shard, quarter, keep, send):
        keep_in_ref[position(assist ^ quarter, 3), position(x ^ shard, near_of(core))] = keep
        send_in_ref[position(assist_peer ^ quarter, 3), position(x ^ shard, far_of(core))] = send

    length = meta_ref[LENGTH]
    mask = (iota((ROWS, 1), 0) < length).astype(F32)
    norm_rows = []
    for s in range(GROUP):
        side, place = second_block(meta_ref, s, 0)
        norm_rows.append(w_ref[side, place, NORM_AT : NORM_AT + QUARTER - HALF, :].astype(F32)[:1])
    gain_one, bias_one, gain_two, bias_two = (
        jnp.concatenate([row[:, i * PIECE : (i + 1) * PIECE] for row in norm_rows], axis=1) for i in range(4)
    )
    token = tok_ref[...].astype(F32)
    ctx = jnp.concatenate([ctx_one_ref[...], ctx_two_ref[...]], axis=1)
    blocks = [second_block(meta_ref, shard, half) for shard in range(GROUP) for half in range(2)]
    w_out = jnp.concatenate([w_ref[side, place, OUT_AT : OUT_AT + HALF, :] for side, place in blocks], axis=0)
    attn = mm(ctx, w_out)

    def norm(values):
        center = values - jnp.mean(values, axis=1, keepdims=True)
        inverse = lax.rsqrt(jnp.mean(center * center, axis=1, keepdims=True) + EPSILON)
        return center * inverse, inverse

    def norm_back(upstream, normed, inverse, gain):
        scaled = upstream * gain
        plain = jnp.mean(scaled, axis=1, keepdims=True)
        cross = jnp.mean(scaled * normed, axis=1, keepdims=True)
        return inverse * (scaled - plain - normed * cross)

    def total(values):
        return jnp.sum(values, axis=0, keepdims=True)

    normed_one, inverse_one = norm(token + attn)
    hidden_one = normed_one * gain_one + bias_one
    low_ref[...] = hidden_one.astype(LOW)

    def columns(c):
        return pl.ds(pl.multiple_of(c * D, D), D)

    def outer_rows(c):
        halves = [second_block(meta_ref, c, half) for half in range(2)]
        return jnp.concatenate([w_ref[side, place, 0 : D // 2, :] for side, place in halves], axis=0)

    def inner_columns(c):
        return jnp.concatenate([in_ref[side, place, :, columns(c)] for side, place in blocks], axis=0)

    def forward_step(c, ffn):
        inner = mm(low_ref[...], inner_columns(c))
        cumulative = 0.5 * (1.0 + lax.erf(inner * 0.5**0.5))
        density = jnp.exp(-0.5 * inner * inner) * 0.3989422804014327
        act = (inner * cumulative).astype(LOW)
        act_ref[c] = act
        slope_ref[c] = cumulative + inner * density
        return ffn + mm(act, outer_rows(c))

    ffn = lax.fori_loop(0, GROUP, forward_step, jnp.zeros((ROWS, D), F32))
    normed_two, inverse_two = norm(hidden_one + ffn)
    layer = (normed_two * gain_two + bias_two) * mask
    out_ref[...] = layer.astype(LOW)
    squares = [token * token * mask, attn * attn * mask, ffn * ffn * mask, layer * layer]
    sums = [jnp.sum(total(s), axis=1, keepdims=True) for s in squares]
    grad_y = up_ref[...].reshape(ROWS, D).astype(F32) * mask
    grad_gain_two = total(grad_y * normed_two)
    grad_bias_two = total(grad_y)
    grad_two = norm_back(grad_y, normed_two, inverse_two, gain_two)
    grad_ffn = grad_two.astype(LOW)

    def back_step(c, grad_hidden):
        grad_act = mm_nt(grad_ffn, outer_rows(c))
        grad_inner = (grad_act * slope_ref[c]).astype(LOW)
        keep, send = select_halves(meta_ref, mm_tn(act_ref[c], grad_ffn))
        for quarter in range(3):
            rows = slice(quarter * QUARTER, (quarter + 1) * QUARTER)
            put_outer(c, quarter, keep[rows], send[rows], 0)
        grad_w = mm_tn(low_ref[...], grad_inner)
        for s in range(GROUP):
            put_inner(s, c, *select_halves(meta_ref, grad_w[s * PIECE : (s + 1) * PIECE]))
        return grad_hidden + mm_nt(grad_inner, inner_columns(c))

    grad_hidden = lax.fori_loop(0, GROUP, back_step, grad_two)
    grad_gain_one = total(grad_hidden * normed_one)
    grad_bias_one = total(grad_hidden)
    grad_one = norm_back(grad_hidden, normed_one, inverse_one, gain_one)
    gres_ref[...] = grad_one
    grad_attn = grad_one.astype(LOW)
    grad_out = mm_tn(ctx, grad_attn)
    for s in range(GROUP):
        put_outer(s, 3, *select_halves(meta_ref, grad_out[s * PIECE : (s + 1) * PIECE]), 0)
    gctx_ref[...] = mm_nt(grad_attn, w_out).astype(LOW)
    lane = iota((1, D), 1)
    stats = jnp.zeros((1, D), F32)
    for i, value in enumerate(sums):
        stats = jnp.where(lane == i, value, stats)
    low = stats - stats.astype(LOW).astype(F32)
    zeros = jnp.zeros((1, D), F32)
    norm_rows = (grad_gain_one, grad_bias_one, grad_gain_two, grad_bias_two)
    for s in range(GROUP):
        row = jnp.concatenate([r[:, s * PIECE : (s + 1) * PIECE] for r in norm_rows], axis=1)
        block = jnp.concatenate([row] + [zeros] * 31 + [stats, low] + [zeros] * 30, axis=0)
        put_outer(s, 3, *select_halves(meta_ref, block), HALF)


def feed(meta, tok, ctx_one, ctx_two, rows, own, pieces):
    shape = jax.ShapeDtypeStruct
    full, anywhere = pl.BlockSpec(memory_space=pltpu.VMEM), pl.BlockSpec(memory_space=pltpu.HBM)
    block, wide = shape((GROUP, GROUP, QUARTER, D), LOW), shape((GROUP, GROUP, HALF, D), LOW)
    return pl.pallas_call(
        feed_body,
        out_shape=(
            shape((ROWS, D), LOW), shape((ROWS, D), LOW), shape((ROWS, D), F32), block, block, wide, wide
        ),
        in_specs=[pl.BlockSpec(memory_space=pltpu.SMEM)] + [full] * 3 + [anywhere] * 15,
        out_specs=(full,) * 7,
        scratch_shapes=[
            pltpu.VMEM((GROUP, PART, D), LOW), pltpu.VMEM((ROWS, D), LOW), pltpu.VMEM((GROUP, ROWS, D), LOW),
            pltpu.VMEM((GROUP, ROWS, D), F32), pltpu.VMEM((2, GROUP, SECOND, D), LOW),
            pltpu.VMEM((2, GROUP, HALF, WIDE), LOW), pltpu.SemaphoreType.DMA((24,)),
        ],
        compiler_params=pltpu.CompilerParams(vmem_limit_bytes=48 * MIB),
        cost_estimate=pl.CostEstimate(flops=16_000_000_000, bytes_accessed=60_000_000, transcendentals=1_600_000),
        name="feed",
    )(meta, tok, ctx_one, ctx_two, rows, *own, *pieces)


def finish_body(
    meta_ref, mine, other, rows_ref,
    q_ref, k_ref, v_ref, rel_ref, outer_ref, wout_ref, inner_ref, extra_ref, out_ref, gtok_ref,
):
    for piece, side in ((mine, 0), (other, 1)):
        core = meta_ref[CORE] if side == 0 else 1 - meta_ref[CORE]
        assist = assist_of(meta_ref, core)
        for i, ref in enumerate((q_ref, k_ref, v_ref, rel_ref)):
            size = REL_HALF if i == 3 else HALF
            ref[pl.ds(pl.multiple_of(core * size, size), size), :] = piece[i * HALF : i * HALF + size, :].astype(F32)

        def piece_step(distance, carry):
            quarter = assist ^ distance
            at = pl.multiple_of(FIRST + distance * SPAN, HALF // 3)
            block = piece[pl.ds(at, QUARTER), :].astype(F32)

            @pl.when(quarter < 3)
            def _():
                outer_ref[pl.ds(pl.multiple_of(core * 3 * QUARTER + quarter * QUARTER, QUARTER), QUARTER), :] = block

            @pl.when(quarter == 3)
            def _():
                wout_ref[pl.ds(pl.multiple_of(core * HALF, HALF), HALF), :] = block[:HALF]
                extra_ref[core] = block[HALF:]

            inner_ref[
                pl.ds(pl.multiple_of(core * HALF, HALF), HALF), pl.ds(pl.multiple_of(quarter * D, D), D)
            ] = piece[pl.ds(at + QUARTER, HALF), :].astype(F32)
            return carry

        lax.fori_loop(0, GROUP, piece_step, 0)
    for k in range(GROUP):
        member = meta_ref[X] ^ k
        out_ref[meta_ref[SEQ + k]] = rows_ref[member, 0]
        gtok_ref[meta_ref[SEQ + k]] = rows_ref[member, 1]


def finish(meta, mine, other, rows):
    shape = jax.ShapeDtypeStruct
    full = pl.BlockSpec(memory_space=pltpu.VMEM)
    return pl.pallas_call(
        finish_body,
        out_shape=(
            *(shape((PIECE, D), F32),) * 3, shape((OFFS // GROUP, D), F32),
            shape((D, D), F32), shape((PIECE, D), F32), shape((PIECE, WIDE), F32), shape((2, QUARTER - HALF, D), F32),
            *(shape((GROUP, PART, D), LOW),) * 2,
        ),
        in_specs=[pl.BlockSpec(memory_space=pltpu.SMEM)] + [full] * 3,
        out_specs=(full,) * 10,
        compiler_params=pltpu.CompilerParams(vmem_limit_bytes=24 * MIB),
        name="finish",
    )(meta, mine, other, rows)


NEAR, FAR = (1, 3), (3, 1)


def hop_x(value, flips):
    pairs = [(c * 4 + i, c * 4 + (i ^ flips[c])) for c in range(2) for i in range(4)]
    return lax.ppermute(value, ("core", "shard"), pairs)


def hop_yz(value, flip, swapped=False):
    pairs = []
    for y in range(4):
        for z in range(4):
            for c in range(2):
                along_y = (c == 0) != swapped
                ty, tz = (y ^ flip, z) if along_y else (y, z ^ flip)
                pairs.append(((y * 4 + z) * 2 + c, (ty * 4 + tz) * 2 + c))
    return lax.ppermute(value, ("y", "z", "core"), pairs)


def swap(value):
    return lax.ppermute(value, "core", [(0, 1), (1, 0)])


def after(value, *others):
    return lax.optimization_barrier((value, *others))[0]


def add(*values):
    total = values[0].astype(F32)
    for value in values[1:]:
        total = total + value.astype(F32)
    return total.astype(LOW)


def exchange_rows(rows):
    return lax.all_to_all(rows, "shard", split_axis=0, concat_axis=0, tiled=True)


def shards(
    hidden, grad_out, lengths, bucket, w_query, w_key, w_value, w_out, w_inner, w_outer, rel_table,
    ln1_gain, ln1_bias, ln2_gain, ln2_bias,
):
    coords = jnp.stack([lax.axis_index(name) for name in ("shard", "y", "z", "core")]).astype(jnp.int32)
    norm_block = jnp.concatenate(
        [jnp.concatenate([ln1_gain, ln1_bias, ln2_gain, ln2_bias])[None], jnp.zeros((31, D), LOW)], axis=0
    )
    bucket_column = jnp.concatenate([bucket[::-1], jnp.full((1,), -1, jnp.int32)])[:, None]
    own_first = (w_query, w_key, w_value, rel_table)
    own_halves = tuple(ref.reshape(2, ref.shape[0] // 2, D) for ref in own_first)
    meta, first, second, rows = pack(
        coords, lengths, hidden, grad_out, own_first, (w_outer, w_out, w_inner), norm_block
    )
    near_two, far_two = hop_x(second, NEAR), hop_x(second, FAR)
    near, far = hop_x(first, NEAR), hop_x(first, FAR)
    rows = exchange_rows(rows)
    across_two = hop_x(near_two, FAR)
    base = after(jnp.stack([near_two, far_two, across_two]), near, far)
    base_near, base_far = hop_yz(base, 1), hop_yz(base, 3)
    across = hop_x(near, FAR)
    pieces = (near, far, across, swap(near), swap(far), swap(across))
    part_outer, part_inner = base_near[:, :QUARTER], base_far[:, QUARTER:]
    rows = after(rows, part_outer, part_inner)
    across_outer, across_inner = hop_yz(part_outer, 3), hop_yz(part_inner, 1)
    tok, *saved, relw, probs, ctx = attend_forward(meta, bucket_column, rows, own_halves, pieces)
    across_outer, across_inner, base, base_near, base_far, _ = lax.optimization_barrier(
        (across_outer, across_inner, base, base_near, base_far, ctx)
    )
    arrived = (base, base_near, base_far, across_outer, across_inner)
    swapped = tuple(swap(piece) for piece in arrived)
    probs_two, ctx_two = attend_forward_two(meta, saved)
    swapped = after(swapped, ctx_two)
    out, gctx, gres, keep, send, keep_in, send_in = feed(
        meta, tok, ctx, ctx_two, rows, (w_outer, w_out, norm_block, w_inner), (*arrived, *swapped)
    )
    other, other_in = swap(send), swap(send_in)
    half_done = attend_back_one((*saved, probs), gctx)
    leave = add(keep[:2], other[:2])
    leave_in = add(keep_in[:2], other_in[:2])
    came, came_in = hop_yz(leave, 1), hop_yz(leave_in, 3)
    half_done = after(tuple(half_done), leave, leave_in)
    leaving, keep_one, send_one = attend_back_two(
        meta, (*saved, probs_two), gctx, half_done, tok, relw, gres, bucket_column, own_halves, pieces, out
    )
    other_one = swap(after(send_one, came, came_in))
    leave_one = add(keep_one[:2], other_one[:2])
    came, came_in = after((came, came_in), leave_one)
    last = hop_yz(add(keep[2], other[2], came[0]), 3)
    last_in = hop_yz(add(keep_in[2], other_in[2], came_in[0]), 1)
    came_one = hop_x(leave_one, NEAR)
    came_one = after(came_one, last, last_in)
    leave_two = add(keep_one[2], other_one[2], came_one[0])
    last_one = hop_x(leave_two, FAR)
    last, last_in, _ = lax.optimization_barrier((last, last_in, leave_two))
    mine = add(keep[3], other[3], came[1], last)
    mine_in = add(keep_in[3], other_in[3], came_in[1], last_in)
    both = jnp.concatenate([mine, mine_in], axis=1)
    came_x = hop_x(both[:2], NEAR)
    home = exchange_rows(leaving)
    last_one = after(last_one, came_x)
    mine_one = add(keep_one[3], other_one[3], came_one[1], last_one)
    come_one = hop_yz(mine_one, 1, swapped=True)
    last_x = hop_x(after(add(both[2], came_x[0]), mine_one), FAR)
    mine_one = add(mine_one, after(come_one, last_x))
    come_one = hop_yz(mine_one, 3, swapped=True)
    both = after(add(both[3], came_x[1], last_x), mine_one)
    step = hop_yz(both, 1, swapped=True)
    mine_one = add(mine_one, after(come_one, step))
    come_one = hop_yz(mine_one, 1)
    both = after(add(both, step), mine_one)
    step = hop_yz(both, 3, swapped=True)
    mine_one = add(mine_one, after(come_one, step))
    come_one = hop_yz(mine_one, 3)
    both = after(add(both, step), mine_one)
    both = [both, *(hop_yz(both, flip) for flip in (1, 3, 2))]
    both[1], both[2], both[3] = both[1], both[3], both[2]
    mine_one = add(mine_one, come_one)
    packed = after(jnp.concatenate([mine_one, *both], axis=0), home)
    q_grad, k_grad, v_grad, rel_grad, outer_grad, out_grad, inner_grad, extra, layer_output, grad_hidden = finish(
        meta, packed, swap(packed), home
    )
    norm_sums = extra[0, 0].reshape(GROUP, PIECE)
    stats = extra[1, 0, :GROUP] + extra[1, 1, :GROUP]
    return (
        layer_output, grad_hidden, q_grad, k_grad, v_grad, out_grad, inner_grad, outer_grad, rel_grad,
        norm_sums[0], norm_sums[1], norm_sums[2], norm_sums[3],
        jnp.sqrt(stats / (TOKENS * D)),
    )


def solution(mesh):
    split = Mesh(mesh.devices.reshape(4, 4, 2, 4), ("y", "z", "core", "shard"))
    rep = ("y", "z", "core")
    rows, vector = P("shard", None), P("shard")
    batch = P(rep, "shard", None)
    return jax.shard_map(
        shards,
        mesh=split,
        in_specs=(batch, batch, P(rep), P(), *(rows,) * 7, *(vector,) * 4),
        out_specs=(batch, batch, *(rows,) * 7, *(vector,) * 4, P()),
        check_vma=False,
    )
```

```python
import jax
import jax.numpy as jnp
from jax import lax
from jax.experimental import pallas as pl
from jax.experimental.pallas import tpu as pltpu
from jax.sharding import Mesh
from jax.sharding import PartitionSpec as P

D = 768
HEADS = 12
HEAD_DIM = 64
PAIRS = HEADS // 2
ROWS = 256
OFFS = 512
TOKENS = 20480
GROUP = 4
PIECE = D // GROUP
HALF = PIECE // 2
WIDE = GROUP * D
REL_HALF = OFFS // GROUP // 2
REL_AT = 3 * HALF
FIRST = 3 * HALF + REL_HALF
OUT_AT = D // 2
NORM_AT = D // 2 + HALF
QUARTER = 128
SECOND = GROUP * QUARTER
SPAN = QUARTER + HALF
PART = ROWS // GROUP
X, Y, Z, CORE, LENGTH, SEQ = 0, 1, 2, 3, 4, 5
META = 16
EPSILON = 1e-07
MASKED = -1e30
SCALING = (3.0 * HEAD_DIM) ** (-0.5)
F32 = jnp.float32
LOW = jnp.bfloat16
MIB = 1024 * 1024


def mm(a, b):
    return lax.dot_general(a, b, (((1,), (0,)), ((), ())), preferred_element_type=F32)


def mm_nt(a, b):
    return lax.dot_general(a, b, (((1,), (1,)), ((), ())), preferred_element_type=F32)


def mm_tn(a, b):
    return lax.dot_general(a, b, (((0,), (0,)), ((), ())), preferred_element_type=F32)


def iota(shape, dim):
    return lax.broadcasted_iota(jnp.int32, shape, dim)


def whole(ref, start, size):
    piece = ref[:, :, start : start + size, :]
    return piece.reshape(GROUP * 2 * size, piece.shape[3])


def run_copies(copies):
    for copy in copies:
        copy.start()
    for copy in copies:
        copy.wait()


class Copies:
    def __init__(self, sem):
        self.sem, self.made = sem, []

    def add(self, source, target):
        self.made.append(pltpu.make_async_copy(source, target, self.sem.at[len(self.made)]))

    def start(self):
        for copy in self.made:
            copy.start()

    def wait(self):
        for copy in self.made:
            copy.wait()


def near_of(core):
    return 1 + 2 * core


def far_of(core):
    return 3 - 2 * core


def assist_of(meta_ref, core):
    return jnp.where(core == 0, meta_ref[Y], meta_ref[Z])


def position(distance, near):
    far = 4 - near
    place = jnp.where(distance == near, 1, jnp.where(distance == far, 2, 0))
    return jnp.where(distance == 0, 3, place)


def pack_body(
    coord_ref, length_ref, hidden_ref, grad_ref, own_q, own_k, own_v, own_rel, own_outer, own_out, own_inner, norm_ref,
    meta_ref, first_ref, second_ref, *rest,
):
    rows_out, sem, tail_sem = rest
    x, y, z, core = (coord_ref[i] for i in range(4))
    for i in range(4):
        meta_ref[i] = coord_ref[i]
    lengths = [length_ref[i] for i in range(GROUP)]
    dealing = []
    for i in range(GROUP):
        rank = jnp.int32(0)
        for j in range(GROUP):
            if j != i:
                ahead = lengths[j] >= lengths[i] if j < i else lengths[j] > lengths[i]
                rank = rank + ahead.astype(jnp.int32)
        dealing.append(rank)
    length = jnp.int32(0)
    for i in range(GROUP):
        length = length + jnp.where(dealing[i] == x, lengths[i], 0)
    meta_ref[LENGTH] = length
    copies = Copies(sem)
    for k in range(GROUP):
        source = jnp.int32(0)
        for i in range(GROUP):
            source = source + jnp.where(dealing[i] == (x ^ k), i, 0)
        meta_ref[SEQ + k] = source
        copies.add(hidden_ref.at[source], rows_out.at[x ^ k, 0])
        copies.add(grad_ref.at[source], rows_out.at[x ^ k, 1])
    for i in range(SEQ + GROUP, META):
        meta_ref[i] = jnp.int32(0)
    for i, ref in enumerate((own_q, own_k, own_v, own_rel)):
        size = REL_HALF if i == 3 else HALF
        copies.add(ref.at[pl.ds(core * size, size)], first_ref.at[pl.ds(i * HALF, size)])
    quarter = jnp.where(core == 0, y, z)
    copies.add(
        own_inner.at[pl.ds(core * HALF, HALF), pl.ds(pl.multiple_of(quarter * D, D), D)],
        second_ref.at[pl.ds(QUARTER, HALF)],
    )
    copies.start()
    tail = Copies(tail_sem)

    @pl.when(quarter < 3)
    def _():
        copy = pltpu.make_async_copy(
            own_outer.at[pl.ds(core * 3 * QUARTER + quarter * QUARTER, QUARTER)], second_ref.at[pl.ds(0, QUARTER)],
            tail_sem.at[0],
        )
        copy.start()
        copy.wait()

    @pl.when(quarter == 3)
    def _():
        tail.add(own_out.at[pl.ds(core * HALF, HALF)], second_ref.at[pl.ds(0, HALF)])
        tail.add(norm_ref, second_ref.at[pl.ds(HALF, QUARTER - HALF)])
        tail.start()
        tail.wait()

    copies.wait()


def pack(coords, lengths, hidden, grad_out, own_first, own_second, norm_block):
    shape = jax.ShapeDtypeStruct
    scalars, anywhere = pl.BlockSpec(memory_space=pltpu.SMEM), pl.BlockSpec(memory_space=pltpu.HBM)
    full = pl.BlockSpec(memory_space=pltpu.VMEM)
    return pl.pallas_call(
        pack_body,
        out_shape=(
            shape((META,), jnp.int32), shape((FIRST, D), LOW), shape((SPAN, D), LOW), shape((GROUP, 2, PART, D), LOW),
        ),
        in_specs=[scalars, scalars] + [anywhere] * 10,
        out_specs=(scalars, full, full, full),
        scratch_shapes=[pltpu.SemaphoreType.DMA((13,)), pltpu.SemaphoreType.DMA((2,))],
        compiler_params=pltpu.CompilerParams(vmem_limit_bytes=60 * MIB),
        name="pack",
    )(coords, lengths, hidden, grad_out, *own_first, *own_second, norm_block)


def load_first(meta_ref, copies, own, pieces, w_ref):
    x, core = meta_ref[X], meta_ref[CORE]
    near, far = x ^ near_of(core), x ^ far_of(core)
    slots = ((near, core), (far, core), (x ^ 2, core), (far, 1 - core), (near, 1 - core), (x ^ 2, 1 - core))
    for piece, (slot, half) in zip(pieces, slots):
        copies.add(piece, w_ref.at[slot, half])
    for i, ref in enumerate(own):
        size = REL_HALF if i == 3 else HALF
        copies.add(ref, w_ref.at[x, :, pl.ds(i * HALF, size)])


def load_second(meta_ref, copies, own, pieces, w_ref, in_ref):
    own_outer, own_out, own_norm, own_inner = own
    for side in range(2):
        assist = assist_of(meta_ref, meta_ref[CORE] if side == 0 else 1 - meta_ref[CORE])
        base, near, far, across_outer, across_inner = pieces[5 * side : 5 * side + 5]
        for distance, outer, inner in (
            (0, base.at[:, pl.ds(0, QUARTER)], base.at[:, pl.ds(QUARTER, HALF)]),
            (1, near.at[:, pl.ds(0, QUARTER)], near.at[:, pl.ds(QUARTER, HALF)]),
            (3, far.at[:, pl.ds(0, QUARTER)], far.at[:, pl.ds(QUARTER, HALF)]),
            (2, across_outer, across_inner),
        ):
            quarter = assist ^ distance
            copies.add(outer, w_ref.at[side, pl.ds(0, 3), pl.ds(quarter * QUARTER, QUARTER)])
            copies.add(inner, in_ref.at[side, pl.ds(0, 3), :, pl.ds(pl.multiple_of(quarter * D, D), D)])
    for half in range(2):
        side = half ^ meta_ref[CORE]
        copies.add(own_outer.at[pl.ds(half * 3 * QUARTER, 3 * QUARTER)], w_ref.at[side, 3, pl.ds(0, 3 * QUARTER)])
        copies.add(own_out.at[pl.ds(half * HALF, HALF)], w_ref.at[side, 3, pl.ds(OUT_AT, HALF)])
        copies.add(own_inner.at[pl.ds(half * HALF, HALF)], in_ref.at[side, 3])
    copies.add(own_norm, w_ref.at[meta_ref[CORE], 3, pl.ds(NORM_AT, QUARTER - HALF)])


def second_block(meta_ref, shard, half):
    apart = meta_ref[X] ^ shard
    place = jnp.where(apart == near_of(half), 0, jnp.where(apart == far_of(half), 1, 2))
    return half ^ meta_ref[CORE], jnp.where(apart == 0, 3, place)


def select_halves(meta_ref, value):
    half = value.shape[0] // 2
    low, high = value[:half].astype(LOW), value[half:].astype(LOW)
    first_core = meta_ref[CORE] == 0
    return jnp.where(first_core, low, high), jnp.where(first_core, high, low)


def heads_forward(meta_ref, first_pair, refs, probs_ref, ctx_ref):
    q_ref, k_ref, v_ref, pk_ref, pq_ref = refs
    length = meta_ref[LENGTH]
    valid = iota((ROWS, ROWS), 1) < length
    side = iota((ROWS, 2 * HEAD_DIM), 1) // HEAD_DIM

    def pair_step(pair, carry):
        out_cols = pl.ds(pl.multiple_of((pair - first_pair) * 2 * HEAD_DIM, 2 * HEAD_DIM), 2 * HEAD_DIM)
        cols = pl.ds(pl.multiple_of(pair * 2 * HEAD_DIM, 2 * HEAD_DIM), 2 * HEAD_DIM)
        q_pair, k_pair, v_pair = q_ref[:, cols], k_ref[:, cols], v_ref[:, cols]
        pk_pair, pq_pair = pk_ref[:, cols], pq_ref[:, cols]
        zero = jnp.zeros_like(q_pair)
        contexts = []
        for h in range(2):
            mine = side == h
            q_head = jnp.where(mine, q_pair, zero)
            k_head = jnp.where(mine, k_pair, zero)
            content = mm_nt(q_head, k_pair)
            to_off = mm_nt(q_head, pk_pair)
            from_off = mm_nt(k_head, pq_pair)
            to_rel = pltpu.roll(to_off, ROWS + 1, 1, stride=1, stride_axis=0)[:, :ROWS]
            from_rel = pltpu.roll(from_off, ROWS + 1, 1, stride=1, stride_axis=0)[:, :ROWS]
            scores = (content + to_rel + from_rel.T) * SCALING
            scores = jnp.where(valid, scores, MASKED)
            top = jnp.max(scores, axis=1, keepdims=True)
            shifted = jnp.exp(scores - top)
            summed = jnp.sum(shifted, axis=1, keepdims=True)
            probs = (shifted * (1.0 / summed)).astype(LOW)
            probs_ref[2 * (pair - first_pair) + h] = probs
            contexts.append(mm(probs, v_pair))
        ctx_ref[:, out_cols] = jnp.where(side == 0, contexts[0], contexts[1]).astype(LOW)
        return carry

    lax.fori_loop(first_pair, first_pair + PAIRS // 2, pair_step, 0)


def attend_forward_body(
    meta_ref, bucket_ref, rows_ref, own_q, own_k, own_v, own_rel, p0, p1, p2, p3, p4, p5,
    tok_ref, q_ref, k_ref, v_ref, pk_ref, pq_ref, relw_ref, probs_ref, ctx_ref,
    w_ref, rows_in, sem,
):
    copies = Copies(sem)
    copies.add(rows_ref.at[:, 0], rows_in)
    load_first(meta_ref, copies, (own_q, own_k, own_v, own_rel), (p0, p1, p2, p3, p4, p5), w_ref)
    copies.start()
    copies.wait()
    tok = rows_in[...].reshape(ROWS, D)
    tok_ref[...] = tok
    rel = whole(w_ref, REL_AT, REL_HALF)
    pick = (bucket_ref[...] == iota((OFFS, OFFS), 1)).astype(LOW)
    relw = mm(pick, rel).astype(LOW)
    relw_ref[...] = relw
    w_query = whole(w_ref, 0, HALF)
    q_ref[...] = mm(tok, w_query).astype(LOW)
    pq_ref[...] = mm(relw, w_query).astype(LOW)
    w_key = whole(w_ref, HALF, HALF)
    k_ref[...] = mm(tok, w_key).astype(LOW)
    pk_ref[...] = mm(relw, w_key).astype(LOW)
    v_ref[...] = mm(tok, whole(w_ref, 2 * HALF, HALF)).astype(LOW)
    heads_forward(meta_ref, 0, (q_ref, k_ref, v_ref, pk_ref, pq_ref), probs_ref, ctx_ref)


def attend_forward_two_body(meta_ref, q_ref, k_ref, v_ref, pk_ref, pq_ref, probs_ref, ctx_ref):
    heads_forward(meta_ref, PAIRS // 2, (q_ref, k_ref, v_ref, pk_ref, pq_ref), probs_ref, ctx_ref)


def attend_forward(meta, bucket_column, rows, own, pieces):
    shape = jax.ShapeDtypeStruct
    full, anywhere = pl.BlockSpec(memory_space=pltpu.VMEM), pl.BlockSpec(memory_space=pltpu.HBM)
    return pl.pallas_call(
        attend_forward_body,
        out_shape=(
            *(shape((ROWS, D), LOW),) * 4,
            shape((OFFS, D), LOW), shape((OFFS, D), LOW), shape((OFFS, D), LOW),
            shape((HEADS // 2, ROWS, ROWS), LOW), shape((ROWS, D // 2), LOW),
        ),
        in_specs=[pl.BlockSpec(memory_space=pltpu.SMEM), full] + [anywhere] * 11,
        out_specs=(full,) * 9,
        scratch_shapes=[
            pltpu.VMEM((GROUP, 2, FIRST, D), LOW), pltpu.VMEM((GROUP, PART, D), LOW), pltpu.SemaphoreType.DMA((11,)),
        ],
        compiler_params=pltpu.CompilerParams(vmem_limit_bytes=28 * MIB),
        cost_estimate=pl.CostEstimate(flops=12_000_000_000, bytes_accessed=40_000_000, transcendentals=800_000),
        name="attend_forward",
    )(meta, bucket_column, rows, *own, *pieces)


def attend_forward_two(meta, saved):
    shape = jax.ShapeDtypeStruct
    full = pl.BlockSpec(memory_space=pltpu.VMEM)
    return pl.pallas_call(
        attend_forward_two_body,
        out_shape=(shape((HEADS // 2, ROWS, ROWS), LOW), shape((ROWS, D // 2), LOW)),
        in_specs=[pl.BlockSpec(memory_space=pltpu.SMEM)] + [full] * 5,
        out_specs=(full,) * 2,
        compiler_params=pltpu.CompilerParams(vmem_limit_bytes=24 * MIB),
        cost_estimate=pl.CostEstimate(flops=8_000_000_000, bytes_accessed=20_000_000, transcendentals=400_000),
        name="attend_forward_two",
    )(meta, *saved)


def heads_back(first_pair, count, refs, outs):
    q_ref, k_ref, v_ref, pk_ref, pq_ref, probs_ref, gctx_ref = refs
    gq_ref, gk_ref, gv_ref, gpk_ref, gpq_ref, qr_ref, kr_ref = outs
    flip = (iota((ROWS, ROWS), 0) + iota((ROWS, ROWS), 1) == ROWS - 1).astype(LOW)
    qr_ref[...] = mm(flip, q_ref[...]).astype(LOW)
    kr_ref[...] = mm(flip, k_ref[...]).astype(LOW)
    side = iota((ROWS, 2 * HEAD_DIM), 1) // HEAD_DIM
    side_off = iota((OFFS, 2 * HEAD_DIM), 1) // HEAD_DIM
    blank = jnp.zeros((ROWS, OFFS - ROWS), F32)

    def pair_step(pair, carry):
        cols = pl.ds(pl.multiple_of(pair * 2 * HEAD_DIM, 2 * HEAD_DIM), 2 * HEAD_DIM)
        q_pair, k_pair, v_pair = q_ref[:, cols], k_ref[:, cols], v_ref[:, cols]
        pk_pair, pq_pair, gctx_pair = pk_ref[:, cols], pq_ref[:, cols], gctx_ref[:, cols]
        qr_pair, kr_pair = qr_ref[:, cols], kr_ref[:, cols]
        zero = jnp.zeros_like(q_pair)
        parts = []
        for h in range(2):
            gctx_head = jnp.where(side == h, gctx_pair, zero)
            grad_probs = mm_nt(gctx_head, v_pair)
            probs_low = probs_ref[2 * (pair - first_pair) + h]
            probs = probs_low.astype(F32)
            inner = jnp.sum(probs * grad_probs, axis=1, keepdims=True)
            grad_scores = (probs * (grad_probs - inner)).astype(LOW)
            g_value = mm_tn(probs_low, gctx_pair)
            rows_back = mm(flip, grad_scores)
            cols_back = mm_nt(flip, grad_scores)
            to_off = pltpu.roll(jnp.concatenate([rows_back, blank], axis=1), 0, 1, stride=1, stride_axis=0).astype(LOW)
            from_off = pltpu.roll(jnp.concatenate([cols_back, blank], axis=1), 0, 1, stride=1, stride_axis=0).astype(LOW)
            g_query = mm(rows_back.astype(LOW), k_pair) + mm(to_off, pk_pair)
            g_key = mm(cols_back.astype(LOW), q_pair) + mm(from_off, pq_pair)
            g_pk = mm_tn(to_off, qr_pair)
            g_pq = mm_tn(from_off, kr_pair)
            parts.append((g_value, g_query, g_key, g_pk, g_pq))
        first, second = parts
        gv_ref[:, cols] = jnp.where(side == 0, first[0], second[0]).astype(LOW)
        gq_ref[:, cols] = (jnp.where(side == 0, first[1], second[1]) * SCALING).astype(LOW)
        gk_ref[:, cols] = (jnp.where(side == 0, first[2], second[2]) * SCALING).astype(LOW)
        gpk_ref[:, cols] = (jnp.where(side_off == 0, first[3], second[3]) * SCALING).astype(LOW)
        gpq_ref[:, cols] = (jnp.where(side_off == 0, first[4], second[4]) * SCALING).astype(LOW)
        return carry

    lax.fori_loop(first_pair, first_pair + count, pair_step, 0)
    return flip


def attend_back_one_body(
    q_ref, k_ref, v_ref, pk_ref, pq_ref, probs_ref, gctx_ref,
    gq_ref, gk_ref, gv_ref, gpk_ref, gpq_ref, qr_ref, kr_ref,
):
    heads_back(
        0, PAIRS // 2, (q_ref, k_ref, v_ref, pk_ref, pq_ref, probs_ref, gctx_ref),
        (gq_ref, gk_ref, gv_ref, gpk_ref, gpq_ref, qr_ref, kr_ref),
    )


def attend_back_two_body(
    meta_ref, q_ref, k_ref, v_ref, pk_ref, pq_ref, probs_ref, gctx_ref, hq, hk, hv, hpk, hpq,
    tok_ref, relw_ref, gres_ref, bucket_ref,
    own_q, own_k, own_v, own_rel, p0, p1, p2, p3, p4, p5,
    out_ref,
    home_ref, keep_ref, send_ref,
    grad_ref, gv_ref, pos_ref, qr_ref, kr_ref, gtok_ref, w_ref, sem,
):
    gq_ref, gk_ref, gpq_ref, gpk_ref = grad_ref.at[0], grad_ref.at[1], pos_ref.at[0], pos_ref.at[1]
    copies = Copies(sem)
    load_first(meta_ref, copies, (own_q, own_k, own_v, own_rel), (p0, p1, p2, p3, p4, p5), w_ref)
    copies.start()
    for target, done in ((gq_ref, hq), (gk_ref, hk), (gv_ref, hv), (gpk_ref, hpk), (gpq_ref, hpq)):
        target[:, : D // 2] = done[...]
    flip = heads_back(
        PAIRS // 2, PAIRS // 2, (q_ref, k_ref, v_ref, pk_ref, pq_ref, probs_ref, gctx_ref),
        (gq_ref, gk_ref, gv_ref, gpk_ref, gpq_ref, qr_ref, kr_ref),
    )
    copies.wait()
    tok, relw = tok_ref[...], relw_ref[...]
    x, core = meta_ref[X], meta_ref[CORE]

    def put(start, size, value):
        for shard in range(GROUP):
            keep, send = select_halves(meta_ref, value[shard * 2 * size : (shard + 1) * 2 * size])
            keep_ref[position(x ^ shard, near_of(core)), pl.ds(start, size)] = keep
            send_ref[position(x ^ shard, far_of(core)), pl.ds(start, size)] = send

    def weight_step(i, carry):
        g_tok, g_rel = carry
        start = pl.multiple_of(i * HALF, HALF)
        grads = mm(flip, grad_ref[i]).astype(LOW)
        weight = w_ref[:, :, pl.ds(start, HALF), :].reshape(D, D)
        put(start, HALF, mm_tn(tok, grads) + mm_tn(relw, pos_ref[i]))
        return g_tok + mm_nt(grads, weight), g_rel + mm_nt(pos_ref[i], weight)

    g_tok, g_rel = lax.fori_loop(0, 2, weight_step, (gres_ref[...], jnp.zeros((OFFS, D), F32)))
    g_value = gv_ref[...]
    gtok_ref[...] = (g_tok + mm_nt(g_value, whole(w_ref, 2 * HALF, HALF))).astype(LOW)
    put(2 * HALF, HALF, mm_tn(tok, g_value))
    pick = (bucket_ref[...] == iota((OFFS, OFFS), 1)).astype(LOW)
    put(REL_AT, REL_HALF, mm_tn(pick, g_rel.astype(LOW)))
    for member in range(GROUP):
        home_ref[member, 0] = out_ref[member * PART : (member + 1) * PART, :]
        home_ref[member, 1] = gtok_ref[member * PART : (member + 1) * PART, :]


def attend_back_one(saved, gctx):
    shape = jax.ShapeDtypeStruct
    full = pl.BlockSpec(memory_space=pltpu.VMEM)
    return pl.pallas_call(
        attend_back_one_body,
        out_shape=(*(shape((ROWS, D // 2), LOW),) * 3, *(shape((OFFS, D // 2), LOW),) * 2),
        in_specs=[full] * 7,
        out_specs=(full,) * 5,
        scratch_shapes=[pltpu.VMEM((ROWS, D), LOW), pltpu.VMEM((ROWS, D), LOW)],
        compiler_params=pltpu.CompilerParams(vmem_limit_bytes=24 * MIB),
        cost_estimate=pl.CostEstimate(flops=8_000_000_000, bytes_accessed=20_000_000, transcendentals=0),
        name="attend_back_one",
    )(*saved, gctx)


def attend_back_two(meta, saved, gctx, half_done, tok, relw, gres, bucket_column, own, pieces, out):
    shape = jax.ShapeDtypeStruct
    full, anywhere = pl.BlockSpec(memory_space=pltpu.VMEM), pl.BlockSpec(memory_space=pltpu.HBM)
    return pl.pallas_call(
        attend_back_two_body,
        out_shape=(shape((GROUP, 2, PART, D), LOW), shape((GROUP, FIRST, D), LOW), shape((GROUP, FIRST, D), LOW)),
        in_specs=[pl.BlockSpec(memory_space=pltpu.SMEM)] + [full] * 16 + [anywhere] * 10 + [full],
        out_specs=(full,) * 3,
        scratch_shapes=[
            pltpu.VMEM((2, ROWS, D), LOW), pltpu.VMEM((ROWS, D), LOW), pltpu.VMEM((2, OFFS, D), LOW),
            *(pltpu.VMEM((ROWS, D), LOW),) * 3,
            pltpu.VMEM((GROUP, 2, FIRST, D), LOW), pltpu.SemaphoreType.DMA((10,)),
        ],
        compiler_params=pltpu.CompilerParams(vmem_limit_bytes=22 * MIB),
        cost_estimate=pl.CostEstimate(flops=14_000_000_000, bytes_accessed=40_000_000, transcendentals=0),
        name="attend_back_two",
    )(meta, *saved, gctx, *half_done, tok, relw, gres, bucket_column, *own, *pieces, out)


def feed_body(
    meta_ref, tok_ref, ctx_one_ref, ctx_two_ref, rows_ref, own_outer, own_out, own_norm, own_inner, *rest,
):
    pieces, rest = rest[:10], rest[10:]
    out_ref, gctx_ref, gres_ref, keep_ref, send_ref, keep_in_ref, send_in_ref = rest[:7]
    up_ref, low_ref, act_ref, slope_ref, w_ref, in_ref, sem = rest[7:]
    copies = Copies(sem)
    copies.add(rows_ref.at[:, 1], up_ref)
    load_second(meta_ref, copies, (own_outer, own_out, own_norm, own_inner), pieces, w_ref, in_ref)
    copies.start()
    copies.wait()
    x, core = meta_ref[X], meta_ref[CORE]
    assist, assist_peer = assist_of(meta_ref, core), assist_of(meta_ref, 1 - core)

    def put_outer(shard, quarter, keep, send, start):
        rows = slice(start, start + keep.shape[0])
        keep_ref[position(assist ^ quarter, 1), position(x ^ shard, near_of(core)), rows] = keep
        send_ref[position(assist_peer ^ quarter, 1), position(x ^ shard, far_of(core)), rows] = send

    def put_inner(shard, quarter, keep, send):
        keep_in_ref[position(assist ^ quarter, 3), position(x ^ shard, near_of(core))] = keep
        send_in_ref[position(assist_peer ^ quarter, 3), position(x ^ shard, far_of(core))] = send

    length = meta_ref[LENGTH]
    mask = (iota((ROWS, 1), 0) < length).astype(F32)
    norm_rows = []
    for s in range(GROUP):
        side, place = second_block(meta_ref, s, 0)
        norm_rows.append(w_ref[side, place, NORM_AT : NORM_AT + QUARTER - HALF, :].astype(F32)[:1])
    gain_one, bias_one, gain_two, bias_two = (
        jnp.concatenate([row[:, i * PIECE : (i + 1) * PIECE] for row in norm_rows], axis=1) for i in range(4)
    )
    token = tok_ref[...].astype(F32)
    ctx = jnp.concatenate([ctx_one_ref[...], ctx_two_ref[...]], axis=1)
    blocks = [second_block(meta_ref, shard, half) for shard in range(GROUP) for half in range(2)]
    w_out = jnp.concatenate([w_ref[side, place, OUT_AT : OUT_AT + HALF, :] for side, place in blocks], axis=0)
    attn = mm(ctx, w_out)

    def norm(values):
        center = values - jnp.mean(values, axis=1, keepdims=True)
        inverse = lax.rsqrt(jnp.mean(center * center, axis=1, keepdims=True) + EPSILON)
        return center * inverse, inverse

    def norm_back(upstream, normed, inverse, gain):
        scaled = upstream * gain
        plain = jnp.mean(scaled, axis=1, keepdims=True)
        cross = jnp.mean(scaled * normed, axis=1, keepdims=True)
        return inverse * (scaled - plain - normed * cross)

    def total(values):
        return jnp.sum(values, axis=0, keepdims=True)

    normed_one, inverse_one = norm(token + attn)
    hidden_one = normed_one * gain_one + bias_one
    low_ref[...] = hidden_one.astype(LOW)

    def columns(c):
        return pl.ds(pl.multiple_of(c * D, D), D)

    def outer_rows(c):
        halves = [second_block(meta_ref, c, half) for half in range(2)]
        return jnp.concatenate([w_ref[side, place, 0 : D // 2, :] for side, place in halves], axis=0)

    def inner_columns(c):
        return jnp.concatenate([in_ref[side, place, :, columns(c)] for side, place in blocks], axis=0)

    def forward_step(c, ffn):
        inner = mm(low_ref[...], inner_columns(c))
        cumulative = 0.5 * (1.0 + lax.erf(inner * 0.5**0.5))
        density = jnp.exp(-0.5 * inner * inner) * 0.3989422804014327
        act = (inner * cumulative).astype(LOW)
        act_ref[c] = act
        slope_ref[c] = cumulative + inner * density
        return ffn + mm(act, outer_rows(c))

    ffn = lax.fori_loop(0, GROUP, forward_step, jnp.zeros((ROWS, D), F32))
    normed_two, inverse_two = norm(hidden_one + ffn)
    layer = (normed_two * gain_two + bias_two) * mask
    out_ref[...] = layer.astype(LOW)
    squares = [token * token * mask, attn * attn * mask, ffn * ffn * mask, layer * layer]
    sums = [jnp.sum(total(s), axis=1, keepdims=True) for s in squares]
    grad_y = up_ref[...].reshape(ROWS, D).astype(F32) * mask
    grad_gain_two = total(grad_y * normed_two)
    grad_bias_two = total(grad_y)
    grad_two = norm_back(grad_y, normed_two, inverse_two, gain_two)
    grad_ffn = grad_two.astype(LOW)

    def back_step(c, grad_hidden):
        grad_act = mm_nt(grad_ffn, outer_rows(c))
        grad_inner = (grad_act * slope_ref[c]).astype(LOW)
        keep, send = select_halves(meta_ref, mm_tn(act_ref[c], grad_ffn))
        for quarter in range(3):
            rows = slice(quarter * QUARTER, (quarter + 1) * QUARTER)
            put_outer(c, quarter, keep[rows], send[rows], 0)
        grad_w = mm_tn(low_ref[...], grad_inner)
        for s in range(GROUP):
            put_inner(s, c, *select_halves(meta_ref, grad_w[s * PIECE : (s + 1) * PIECE]))
        return grad_hidden + mm_nt(grad_inner, inner_columns(c))

    grad_hidden = lax.fori_loop(0, GROUP, back_step, grad_two)
    grad_gain_one = total(grad_hidden * normed_one)
    grad_bias_one = total(grad_hidden)
    grad_one = norm_back(grad_hidden, normed_one, inverse_one, gain_one)
    gres_ref[...] = grad_one
    grad_attn = grad_one.astype(LOW)
    grad_out = mm_tn(ctx, grad_attn)
    for s in range(GROUP):
        put_outer(s, 3, *select_halves(meta_ref, grad_out[s * PIECE : (s + 1) * PIECE]), 0)
    gctx_ref[...] = mm_nt(grad_attn, w_out).astype(LOW)
    lane = iota((1, D), 1)
    stats = jnp.zeros((1, D), F32)
    for i, value in enumerate(sums):
        stats = jnp.where(lane == i, value, stats)
    low = stats - stats.astype(LOW).astype(F32)
    zeros = jnp.zeros((1, D), F32)
    norm_rows = (grad_gain_one, grad_bias_one, grad_gain_two, grad_bias_two)
    for s in range(GROUP):
        row = jnp.concatenate([r[:, s * PIECE : (s + 1) * PIECE] for r in norm_rows], axis=1)
        block = jnp.concatenate([row] + [zeros] * 31 + [stats, low] + [zeros] * 30, axis=0)
        put_outer(s, 3, *select_halves(meta_ref, block), HALF)


def feed(meta, tok, ctx_one, ctx_two, rows, own, pieces):
    shape = jax.ShapeDtypeStruct
    full, anywhere = pl.BlockSpec(memory_space=pltpu.VMEM), pl.BlockSpec(memory_space=pltpu.HBM)
    block, wide = shape((GROUP, GROUP, QUARTER, D), LOW), shape((GROUP, GROUP, HALF, D), LOW)
    return pl.pallas_call(
        feed_body,
        out_shape=(
            shape((ROWS, D), LOW), shape((ROWS, D), LOW), shape((ROWS, D), F32), block, block, wide, wide
        ),
        in_specs=[pl.BlockSpec(memory_space=pltpu.SMEM)] + [full] * 3 + [anywhere] * 15,
        out_specs=(full,) * 7,
        scratch_shapes=[
            pltpu.VMEM((GROUP, PART, D), LOW), pltpu.VMEM((ROWS, D), LOW), pltpu.VMEM((GROUP, ROWS, D), LOW),
            pltpu.VMEM((GROUP, ROWS, D), F32), pltpu.VMEM((2, GROUP, SECOND, D), LOW),
            pltpu.VMEM((2, GROUP, HALF, WIDE), LOW), pltpu.SemaphoreType.DMA((24,)),
        ],
        compiler_params=pltpu.CompilerParams(vmem_limit_bytes=28 * MIB),
        cost_estimate=pl.CostEstimate(flops=16_000_000_000, bytes_accessed=60_000_000, transcendentals=1_600_000),
        name="feed",
    )(meta, tok, ctx_one, ctx_two, rows, *own, *pieces)


def finish_body(
    meta_ref, mine, other, rows_ref,
    q_ref, k_ref, v_ref, rel_ref, outer_ref, wout_ref, inner_ref, extra_ref, out_ref, gtok_ref,
):
    for piece, side in ((mine, 0), (other, 1)):
        core = meta_ref[CORE] if side == 0 else 1 - meta_ref[CORE]
        assist = assist_of(meta_ref, core)
        for i, ref in enumerate((q_ref, k_ref, v_ref, rel_ref)):
            size = REL_HALF if i == 3 else HALF
            ref[pl.ds(pl.multiple_of(core * size, size), size), :] = piece[i * HALF : i * HALF + size, :].astype(F32)

        def piece_step(distance, carry):
            quarter = assist ^ distance
            at = pl.multiple_of(FIRST + distance * SPAN, HALF // 3)
            block = piece[pl.ds(at, QUARTER), :].astype(F32)

            @pl.when(quarter < 3)
            def _():
                outer_ref[pl.ds(pl.multiple_of(core * 3 * QUARTER + quarter * QUARTER, QUARTER), QUARTER), :] = block

            @pl.when(quarter == 3)
            def _():
                wout_ref[pl.ds(pl.multiple_of(core * HALF, HALF), HALF), :] = block[:HALF]
                extra_ref[core] = block[HALF:]

            inner_ref[
                pl.ds(pl.multiple_of(core * HALF, HALF), HALF), pl.ds(pl.multiple_of(quarter * D, D), D)
            ] = piece[pl.ds(at + QUARTER, HALF), :].astype(F32)
            return carry

        lax.fori_loop(0, GROUP, piece_step, 0)
    for k in range(GROUP):
        member = meta_ref[X] ^ k
        out_ref[meta_ref[SEQ + k]] = rows_ref[member, 0]
        gtok_ref[meta_ref[SEQ + k]] = rows_ref[member, 1]


def finish(meta, mine, other, rows):
    shape = jax.ShapeDtypeStruct
    full = pl.BlockSpec(memory_space=pltpu.VMEM)
    return pl.pallas_call(
        finish_body,
        out_shape=(
            *(shape((PIECE, D), F32),) * 3, shape((OFFS // GROUP, D), F32),
            shape((D, D), F32), shape((PIECE, D), F32), shape((PIECE, WIDE), F32), shape((2, QUARTER - HALF, D), F32),
            *(shape((GROUP, PART, D), LOW),) * 2,
        ),
        in_specs=[pl.BlockSpec(memory_space=pltpu.SMEM)] + [full] * 3,
        out_specs=(full,) * 10,
        compiler_params=pltpu.CompilerParams(vmem_limit_bytes=24 * MIB),
        name="finish",
    )(meta, mine, other, rows)


NEAR, FAR = (1, 3), (3, 1)


def hop_x(value, flips):
    pairs = [(c * 4 + i, c * 4 + (i ^ flips[c])) for c in range(2) for i in range(4)]
    return lax.ppermute(value, ("core", "shard"), pairs)


def hop_yz(value, flip, swapped=False):
    pairs = []
    for y in range(4):
        for z in range(4):
            for c in range(2):
                along_y = (c == 0) != swapped
                ty, tz = (y ^ flip, z) if along_y else (y, z ^ flip)
                pairs.append(((y * 4 + z) * 2 + c, (ty * 4 + tz) * 2 + c))
    return lax.ppermute(value, ("y", "z", "core"), pairs)


def swap(value):
    return lax.ppermute(value, "core", [(0, 1), (1, 0)])


def after(value, *others):
    return lax.optimization_barrier((value, *others))[0]


def add(*values):
    total = values[0].astype(F32)
    for value in values[1:]:
        total = total + value.astype(F32)
    return total.astype(LOW)


def exchange_rows(rows):
    return lax.all_to_all(rows, "shard", split_axis=0, concat_axis=0, tiled=True)


def shards(
    hidden, grad_out, lengths, bucket, w_query, w_key, w_value, w_out, w_inner, w_outer, rel_table,
    ln1_gain, ln1_bias, ln2_gain, ln2_bias,
):
    coords = jnp.stack([lax.axis_index(name) for name in ("shard", "y", "z", "core")]).astype(jnp.int32)
    norm_block = jnp.concatenate(
        [jnp.concatenate([ln1_gain, ln1_bias, ln2_gain, ln2_bias])[None], jnp.zeros((31, D), LOW)], axis=0
    )
    bucket_column = jnp.concatenate([bucket[::-1], jnp.full((1,), -1, jnp.int32)])[:, None]
    own_first = (w_query, w_key, w_value, rel_table)
    own_halves = tuple(ref.reshape(2, ref.shape[0] // 2, D) for ref in own_first)
    meta, first, second, rows = pack(
        coords, lengths, hidden, grad_out, own_first, (w_outer, w_out, w_inner), norm_block
    )
    near_two, far_two = hop_x(second, NEAR), hop_x(second, FAR)
    near, far = hop_x(first, NEAR), hop_x(first, FAR)
    rows = exchange_rows(rows)
    across_two = hop_x(near_two, FAR)
    base = after(jnp.stack([near_two, far_two, across_two]), near, far)
    base_near, base_far = hop_yz(base, 1), hop_yz(base, 3)
    across = hop_x(near, FAR)
    pieces = (near, far, across, swap(near), swap(far), swap(across))
    part_outer, part_inner = base_near[:, :QUARTER], base_far[:, QUARTER:]
    rows = after(rows, part_outer, part_inner)
    across_outer, across_inner = hop_yz(part_outer, 3), hop_yz(part_inner, 1)
    tok, *saved, relw, probs, ctx = attend_forward(meta, bucket_column, rows, own_halves, pieces)
    across_outer, across_inner, base, base_near, base_far, _ = lax.optimization_barrier(
        (across_outer, across_inner, base, base_near, base_far, ctx)
    )
    arrived = (base, base_near, base_far, across_outer, across_inner)
    swapped = tuple(swap(piece) for piece in arrived)
    probs_two, ctx_two = attend_forward_two(meta, saved)
    swapped = after(swapped, ctx_two)
    out, gctx, gres, keep, send, keep_in, send_in = feed(
        meta, tok, ctx, ctx_two, rows, (w_outer, w_out, norm_block, w_inner), (*arrived, *swapped)
    )
    other, other_in = swap(send), swap(send_in)
    half_done = attend_back_one((*saved, probs), gctx)
    leave = add(keep[:2], other[:2])
    leave_in = add(keep_in[:2], other_in[:2])
    came, came_in = hop_yz(leave, 1), hop_yz(leave_in, 3)
    half_done = after(tuple(half_done), leave, leave_in)
    leaving, keep_one, send_one = attend_back_two(
        meta, (*saved, probs_two), gctx, half_done, tok, relw, gres, bucket_column, own_halves, pieces, out
    )
    other_one = swap(after(send_one, came, came_in))
    leave_one = add(keep_one[:2], other_one[:2])
    came, came_in = after((came, came_in), leave_one)
    last = hop_yz(add(keep[2], other[2], came[0]), 3)
    last_in = hop_yz(add(keep_in[2], other_in[2], came_in[0]), 1)
    came_one = hop_x(leave_one, NEAR)
    came_one = after(came_one, last, last_in)
    leave_two = add(keep_one[2], other_one[2], came_one[0])
    last_one = hop_x(leave_two, FAR)
    last, last_in, _ = lax.optimization_barrier((last, last_in, leave_two))
    mine = add(keep[3], other[3], came[1], last)
    mine_in = add(keep_in[3], other_in[3], came_in[1], last_in)
    both = jnp.concatenate([mine, mine_in], axis=1)
    came_x = hop_x(both[:2], NEAR)
    home = exchange_rows(leaving)
    last_one = after(last_one, came_x)
    mine_one = add(keep_one[3], other_one[3], came_one[1], last_one)
    come_one = hop_yz(mine_one, 1, swapped=True)
    last_x = hop_x(after(add(both[2], came_x[0]), mine_one), FAR)
    mine_one = add(mine_one, after(come_one, last_x))
    come_one = hop_yz(mine_one, 3, swapped=True)
    both = after(add(both[3], came_x[1], last_x), mine_one)
    step = hop_yz(both, 1, swapped=True)
    mine_one = add(mine_one, after(come_one, step))
    come_one = hop_yz(mine_one, 1)
    both = after(add(both, step), mine_one)
    step = hop_yz(both, 3, swapped=True)
    mine_one = add(mine_one, after(come_one, step))
    come_one = hop_yz(mine_one, 3)
    both = after(add(both, step), mine_one)
    both = [both, *(hop_yz(both, flip) for flip in (1, 3, 2))]
    both[1], both[2], both[3] = both[1], both[3], both[2]
    mine_one = add(mine_one, come_one)
    packed = after(jnp.concatenate([mine_one, *both], axis=0), home)
    q_grad, k_grad, v_grad, rel_grad, outer_grad, out_grad, inner_grad, extra, layer_output, grad_hidden = finish(
        meta, packed, swap(packed), home
    )
    norm_sums = extra[0, 0].reshape(GROUP, PIECE)
    stats = extra[1, 0, :GROUP] + extra[1, 1, :GROUP]
    return (
        layer_output, grad_hidden, q_grad, k_grad, v_grad, out_grad, inner_grad, outer_grad, rel_grad,
        norm_sums[0], norm_sums[1], norm_sums[2], norm_sums[3],
        jnp.sqrt(stats / (TOKENS * D)),
    )


def solution(mesh):
    split = Mesh(mesh.devices.reshape(4, 4, 2, 4), ("y", "z", "core", "shard"))
    rep = ("y", "z", "core")
    rows, vector = P("shard", None), P("shard")
    batch = P(rep, "shard", None)
    return jax.shard_map(
        shards,
        mesh=split,
        in_specs=(batch, batch, P(rep), P(), *(rows,) * 7, *(vector,) * 4),
        out_specs=(batch, batch, *(rows,) * 7, *(vector,) * 4, P()),
        check_vma=False,
    )
```

```python
import jax
import jax.numpy as jnp
from jax import lax
from jax.experimental import pallas as pl
from jax.experimental.pallas import tpu as pltpu
from jax.sharding import Mesh
from jax.sharding import PartitionSpec as P

D = 768
HEADS = 12
HEAD_DIM = 64
PAIRS = HEADS // 2
ROWS = 256
OFFS = 512
TOKENS = 20480
GROUP = 4
PIECE = D // GROUP
HALF = PIECE // 2
WIDE = GROUP * D
REL_HALF = OFFS // GROUP // 2
REL_AT = 3 * HALF
FIRST = 3 * HALF + REL_HALF
OUT_AT = D // 2
NORM_AT = D // 2 + HALF
QUARTER = 128
SECOND = GROUP * QUARTER
SPAN = QUARTER + HALF
PART = ROWS // GROUP
X, Y, Z, CORE, LENGTH, SEQ = 0, 1, 2, 3, 4, 5
META = 16
EPSILON = 1e-07
MASKED = -1e30
SCALING = (3.0 * HEAD_DIM) ** (-0.5)
F32 = jnp.float32
LOW = jnp.bfloat16
MIB = 1024 * 1024


def mm(a, b):
    return lax.dot_general(a, b, (((1,), (0,)), ((), ())), preferred_element_type=F32)


def mm_nt(a, b):
    return lax.dot_general(a, b, (((1,), (1,)), ((), ())), preferred_element_type=F32)


def mm_tn(a, b):
    return lax.dot_general(a, b, (((0,), (0,)), ((), ())), preferred_element_type=F32)


def iota(shape, dim):
    return lax.broadcasted_iota(jnp.int32, shape, dim)


def whole(ref, start, size):
    piece = ref[:, :, start : start + size, :]
    return piece.reshape(GROUP * 2 * size, piece.shape[3])


def run_copies(copies):
    for copy in copies:
        copy.start()
    for copy in copies:
        copy.wait()


class Copies:
    def __init__(self, sem):
        self.sem, self.made = sem, []

    def add(self, source, target):
        self.made.append(pltpu.make_async_copy(source, target, self.sem.at[len(self.made)]))

    def start(self):
        for copy in self.made:
            copy.start()

    def wait(self):
        for copy in self.made:
            copy.wait()


def near_of(core):
    return 1 + 2 * core


def far_of(core):
    return 3 - 2 * core


def assist_of(meta_ref, core):
    return jnp.where(core == 0, meta_ref[Y], meta_ref[Z])


def position(distance, near):
    far = 4 - near
    place = jnp.where(distance == near, 1, jnp.where(distance == far, 2, 0))
    return jnp.where(distance == 0, 3, place)


def pack_body(
    coord_ref, length_ref, hidden_ref, grad_ref, own_q, own_k, own_v, own_rel, own_outer, own_out, own_inner, norm_ref,
    meta_ref, first_ref, second_ref, *rest,
):
    rows_out, sem, tail_sem = rest
    x, y, z, core = (coord_ref[i] for i in range(4))
    for i in range(4):
        meta_ref[i] = coord_ref[i]
    lengths = [length_ref[i] for i in range(GROUP)]
    dealing = []
    for i in range(GROUP):
        rank = jnp.int32(0)
        for j in range(GROUP):
            if j != i:
                ahead = lengths[j] >= lengths[i] if j < i else lengths[j] > lengths[i]
                rank = rank + ahead.astype(jnp.int32)
        dealing.append(rank)
    length = jnp.int32(0)
    for i in range(GROUP):
        length = length + jnp.where(dealing[i] == x, lengths[i], 0)
    meta_ref[LENGTH] = length
    copies = Copies(sem)
    for k in range(GROUP):
        source = jnp.int32(0)
        for i in range(GROUP):
            source = source + jnp.where(dealing[i] == (x ^ k), i, 0)
        meta_ref[SEQ + k] = source
        copies.add(hidden_ref.at[source], rows_out.at[x ^ k, 0])
        copies.add(grad_ref.at[source], rows_out.at[x ^ k, 1])
    for i in range(SEQ + GROUP, META):
        meta_ref[i] = jnp.int32(0)
    for i, ref in enumerate((own_q, own_k, own_v, own_rel)):
        size = REL_HALF if i == 3 else HALF
        copies.add(ref.at[pl.ds(core * size, size)], first_ref.at[pl.ds(i * HALF, size)])
    quarter = jnp.where(core == 0, y, z)
    copies.add(
        own_inner.at[pl.ds(core * HALF, HALF), pl.ds(pl.multiple_of(quarter * D, D), D)],
        second_ref.at[pl.ds(QUARTER, HALF)],
    )
    copies.start()
    tail = Copies(tail_sem)

    @pl.when(quarter < 3)
    def _():
        copy = pltpu.make_async_copy(
            own_outer.at[pl.ds(core * 3 * QUARTER + quarter * QUARTER, QUARTER)], second_ref.at[pl.ds(0, QUARTER)],
            tail_sem.at[0],
        )
        copy.start()
        copy.wait()

    @pl.when(quarter == 3)
    def _():
        tail.add(own_out.at[pl.ds(core * HALF, HALF)], second_ref.at[pl.ds(0, HALF)])
        tail.add(norm_ref, second_ref.at[pl.ds(HALF, QUARTER - HALF)])
        tail.start()
        tail.wait()

    copies.wait()


def pack(coords, lengths, hidden, grad_out, own_first, own_second, norm_block):
    shape = jax.ShapeDtypeStruct
    scalars, anywhere = pl.BlockSpec(memory_space=pltpu.SMEM), pl.BlockSpec(memory_space=pltpu.HBM)
    full = pl.BlockSpec(memory_space=pltpu.VMEM)
    return pl.pallas_call(
        pack_body,
        out_shape=(
            shape((META,), jnp.int32), shape((FIRST, D), LOW), shape((SPAN, D), LOW), shape((GROUP, 2, PART, D), LOW),
        ),
        in_specs=[scalars, scalars] + [anywhere] * 10,
        out_specs=(scalars, full, full, full),
        scratch_shapes=[pltpu.SemaphoreType.DMA((13,)), pltpu.SemaphoreType.DMA((2,))],
        compiler_params=pltpu.CompilerParams(vmem_limit_bytes=60 * MIB),
        name="pack",
    )(coords, lengths, hidden, grad_out, *own_first, *own_second, norm_block)


def load_first(meta_ref, copies, own, pieces, w_ref):
    x, core = meta_ref[X], meta_ref[CORE]
    near, far = x ^ near_of(core), x ^ far_of(core)
    slots = ((near, core), (far, core), (x ^ 2, core), (far, 1 - core), (near, 1 - core), (x ^ 2, 1 - core))
    for piece, (slot, half) in zip(pieces, slots):
        copies.add(piece, w_ref.at[slot, half])
    for i, ref in enumerate(own):
        size = REL_HALF if i == 3 else HALF
        copies.add(ref, w_ref.at[x, :, pl.ds(i * HALF, size)])


def load_second(meta_ref, copies, own, pieces, w_ref, in_ref):
    own_outer, own_out, own_norm, own_inner = own
    for side in range(2):
        assist = assist_of(meta_ref, meta_ref[CORE] if side == 0 else 1 - meta_ref[CORE])
        base, near, far, across_outer, across_inner = pieces[5 * side : 5 * side + 5]
        for distance, outer, inner in (
            (0, base.at[:, pl.ds(0, QUARTER)], base.at[:, pl.ds(QUARTER, HALF)]),
            (1, near.at[:, pl.ds(0, QUARTER)], near.at[:, pl.ds(QUARTER, HALF)]),
            (3, far.at[:, pl.ds(0, QUARTER)], far.at[:, pl.ds(QUARTER, HALF)]),
            (2, across_outer, across_inner),
        ):
            quarter = assist ^ distance
            copies.add(outer, w_ref.at[side, pl.ds(0, 3), pl.ds(quarter * QUARTER, QUARTER)])
            copies.add(inner, in_ref.at[side, pl.ds(0, 3), :, pl.ds(pl.multiple_of(quarter * D, D), D)])
    for half in range(2):
        side = half ^ meta_ref[CORE]
        copies.add(own_outer.at[pl.ds(half * 3 * QUARTER, 3 * QUARTER)], w_ref.at[side, 3, pl.ds(0, 3 * QUARTER)])
        copies.add(own_out.at[pl.ds(half * HALF, HALF)], w_ref.at[side, 3, pl.ds(OUT_AT, HALF)])
        copies.add(own_inner.at[pl.ds(half * HALF, HALF)], in_ref.at[side, 3])
    copies.add(own_norm, w_ref.at[meta_ref[CORE], 3, pl.ds(NORM_AT, QUARTER - HALF)])


def second_block(meta_ref, shard, half):
    apart = meta_ref[X] ^ shard
    place = jnp.where(apart == near_of(half), 0, jnp.where(apart == far_of(half), 1, 2))
    return half ^ meta_ref[CORE], jnp.where(apart == 0, 3, place)


def select_halves(meta_ref, value):
    half = value.shape[0] // 2
    low, high = value[:half].astype(LOW), value[half:].astype(LOW)
    first_core = meta_ref[CORE] == 0
    return jnp.where(first_core, low, high), jnp.where(first_core, high, low)


def heads_forward(meta_ref, first_pair, refs, probs_ref, ctx_ref):
    q_ref, k_ref, v_ref, pk_ref, pq_ref = refs
    length = meta_ref[LENGTH]
    valid = iota((ROWS, ROWS), 1) < length
    side = iota((ROWS, 2 * HEAD_DIM), 1) // HEAD_DIM

    def pair_step(pair, carry):
        out_cols = pl.ds(pl.multiple_of((pair - first_pair) * 2 * HEAD_DIM, 2 * HEAD_DIM), 2 * HEAD_DIM)
        cols = pl.ds(pl.multiple_of(pair * 2 * HEAD_DIM, 2 * HEAD_DIM), 2 * HEAD_DIM)
        q_pair, k_pair, v_pair = q_ref[:, cols], k_ref[:, cols], v_ref[:, cols]
        pk_pair, pq_pair = pk_ref[:, cols], pq_ref[:, cols]
        zero = jnp.zeros_like(q_pair)
        contexts = []
        for h in range(2):
            mine = side == h
            q_head = jnp.where(mine, q_pair, zero)
            k_head = jnp.where(mine, k_pair, zero)
            content = mm_nt(q_head, k_pair)
            to_off = mm_nt(q_head, pk_pair)
            from_off = mm_nt(k_head, pq_pair)
            to_rel = pltpu.roll(to_off, ROWS + 1, 1, stride=1, stride_axis=0)[:, :ROWS]
            from_rel = pltpu.roll(from_off, ROWS + 1, 1, stride=1, stride_axis=0)[:, :ROWS]
            scores = (content + to_rel + from_rel.T) * SCALING
            scores = jnp.where(valid, scores, MASKED)
            top = jnp.max(scores, axis=1, keepdims=True)
            shifted = jnp.exp(scores - top)
            summed = jnp.sum(shifted, axis=1, keepdims=True)
            probs = (shifted * (1.0 / summed)).astype(LOW)
            probs_ref[2 * (pair - first_pair) + h] = probs
            contexts.append(mm(probs, v_pair))
        ctx_ref[:, out_cols] = jnp.where(side == 0, contexts[0], contexts[1]).astype(LOW)
        return carry

    lax.fori_loop(first_pair, first_pair + PAIRS // 2, pair_step, 0)


def attend_forward_body(
    meta_ref, bucket_ref, rows_ref, own_q, own_k, own_v, own_rel, p0, p1, p2, p3, p4, p5,
    tok_ref, q_ref, k_ref, v_ref, pk_ref, pq_ref, relw_ref, probs_ref, ctx_ref,
    w_ref, rows_in, sem,
):
    copies = Copies(sem)
    copies.add(rows_ref.at[:, 0], rows_in)
    load_first(meta_ref, copies, (own_q, own_k, own_v, own_rel), (p0, p1, p2, p3, p4, p5), w_ref)
    copies.start()
    copies.wait()
    tok = rows_in[...].reshape(ROWS, D)
    tok_ref[...] = tok
    rel = whole(w_ref, REL_AT, REL_HALF)
    pick = (bucket_ref[...] == iota((OFFS, OFFS), 1)).astype(LOW)
    relw = mm(pick, rel).astype(LOW)
    relw_ref[...] = relw
    w_query = whole(w_ref, 0, HALF)
    q_ref[...] = mm(tok, w_query).astype(LOW)
    pq_ref[...] = mm(relw, w_query).astype(LOW)
    w_key = whole(w_ref, HALF, HALF)
    k_ref[...] = mm(tok, w_key).astype(LOW)
    pk_ref[...] = mm(relw, w_key).astype(LOW)
    v_ref[...] = mm(tok, whole(w_ref, 2 * HALF, HALF)).astype(LOW)
    heads_forward(meta_ref, 0, (q_ref, k_ref, v_ref, pk_ref, pq_ref), probs_ref, ctx_ref)


def attend_forward_two_body(meta_ref, q_ref, k_ref, v_ref, pk_ref, pq_ref, probs_ref, ctx_ref):
    heads_forward(meta_ref, PAIRS // 2, (q_ref, k_ref, v_ref, pk_ref, pq_ref), probs_ref, ctx_ref)


def attend_forward(meta, bucket_column, rows, own, pieces):
    shape = jax.ShapeDtypeStruct
    full, anywhere = pl.BlockSpec(memory_space=pltpu.VMEM), pl.BlockSpec(memory_space=pltpu.HBM)
    return pl.pallas_call(
        attend_forward_body,
        out_shape=(
            *(shape((ROWS, D), LOW),) * 4,
            shape((OFFS, D), LOW), shape((OFFS, D), LOW), shape((OFFS, D), LOW),
            shape((HEADS // 2, ROWS, ROWS), LOW), shape((ROWS, D // 2), LOW),
        ),
        in_specs=[pl.BlockSpec(memory_space=pltpu.SMEM), full] + [anywhere] * 11,
        out_specs=(full,) * 9,
        scratch_shapes=[
            pltpu.VMEM((GROUP, 2, FIRST, D), LOW), pltpu.VMEM((GROUP, PART, D), LOW), pltpu.SemaphoreType.DMA((11,)),
        ],
        compiler_params=pltpu.CompilerParams(vmem_limit_bytes=28 * MIB),
        cost_estimate=pl.CostEstimate(flops=12_000_000_000, bytes_accessed=40_000_000, transcendentals=800_000),
        name="attend_forward",
    )(meta, bucket_column, rows, *own, *pieces)


def attend_forward_two(meta, saved):
    shape = jax.ShapeDtypeStruct
    full = pl.BlockSpec(memory_space=pltpu.VMEM)
    return pl.pallas_call(
        attend_forward_two_body,
        out_shape=(shape((HEADS // 2, ROWS, ROWS), LOW), shape((ROWS, D // 2), LOW)),
        in_specs=[pl.BlockSpec(memory_space=pltpu.SMEM)] + [full] * 5,
        out_specs=(full,) * 2,
        compiler_params=pltpu.CompilerParams(vmem_limit_bytes=24 * MIB),
        cost_estimate=pl.CostEstimate(flops=8_000_000_000, bytes_accessed=20_000_000, transcendentals=400_000),
        name="attend_forward_two",
    )(meta, *saved)


def both_heads(pair, side):
    zero = jnp.zeros_like(pair)
    return jnp.concatenate([jnp.where(side == h, pair, zero) for h in range(2)], axis=0)


def heads_back(first_pair, count, refs, outs):
    q_ref, k_ref, v_ref, pk_ref, pq_ref, probs_ref, gctx_ref = refs
    gq_ref, gk_ref, gv_ref, gpk_ref, gpq_ref, qr_ref, kr_ref = outs
    flip = (iota((ROWS, ROWS), 0) + iota((ROWS, ROWS), 1) == ROWS - 1).astype(LOW)
    qr_ref[...] = mm(flip, q_ref[...]).astype(LOW)
    kr_ref[...] = mm(flip, k_ref[...]).astype(LOW)
    side = iota((ROWS, 2 * HEAD_DIM), 1) // HEAD_DIM
    side_off = iota((OFFS, 2 * HEAD_DIM), 1) // HEAD_DIM
    blank = jnp.zeros((ROWS, OFFS - ROWS), F32)

    def pair_step(pair, carry):
        cols = pl.ds(pl.multiple_of(pair * 2 * HEAD_DIM, 2 * HEAD_DIM), 2 * HEAD_DIM)
        q_pair, k_pair, v_pair = q_ref[:, cols], k_ref[:, cols], v_ref[:, cols]
        pk_pair, pq_pair, gctx_pair = pk_ref[:, cols], pq_ref[:, cols], gctx_ref[:, cols]
        qr_pair, kr_pair = qr_ref[:, cols], kr_ref[:, cols]
        grad_probs_both = mm_nt(both_heads(gctx_pair, side), v_pair)
        scores_both, probs_both = [], []
        for h in range(2):
            grad_probs = grad_probs_both[h * ROWS : (h + 1) * ROWS]
            probs_low = probs_ref[2 * (pair - first_pair) + h]
            probs = probs_low.astype(F32)
            inner = jnp.sum(probs * grad_probs, axis=1, keepdims=True)
            scores_both.append((probs * (grad_probs - inner)).astype(LOW))
            probs_both.append(probs_low)
        g_value = mm_tn(jnp.concatenate(probs_both, axis=1), gctx_pair)
        rows_both = mm(flip, jnp.concatenate(scores_both, axis=1))
        cols_both = mm_nt(flip, jnp.concatenate(scores_both, axis=0))

        def spread_out(both):
            return [
                pltpu.roll(
                    jnp.concatenate([both[:, h * ROWS : (h + 1) * ROWS], blank], axis=1), 0, 1, stride=1, stride_axis=0
                ).astype(LOW)
                for h in range(2)
            ]

        def stacked(both):
            return jnp.concatenate([both[:, :ROWS], both[:, ROWS:]], axis=0).astype(LOW)

        to_off, from_off = spread_out(rows_both), spread_out(cols_both)
        g_query = mm(stacked(rows_both), k_pair) + mm(jnp.concatenate(to_off, axis=0), pk_pair)
        g_key = mm(stacked(cols_both), q_pair) + mm(jnp.concatenate(from_off, axis=0), pq_pair)
        g_pk = mm_tn(jnp.concatenate(to_off, axis=1), qr_pair)
        g_pq = mm_tn(jnp.concatenate(from_off, axis=1), kr_pair)
        first = [grad[: grad.shape[0] // 2] for grad in (g_value, g_query, g_key, g_pk, g_pq)]
        second = [grad[grad.shape[0] // 2 :] for grad in (g_value, g_query, g_key, g_pk, g_pq)]
        gv_ref[:, cols] = jnp.where(side == 0, first[0], second[0]).astype(LOW)
        gq_ref[:, cols] = (jnp.where(side == 0, first[1], second[1]) * SCALING).astype(LOW)
        gk_ref[:, cols] = (jnp.where(side == 0, first[2], second[2]) * SCALING).astype(LOW)
        gpk_ref[:, cols] = (jnp.where(side_off == 0, first[3], second[3]) * SCALING).astype(LOW)
        gpq_ref[:, cols] = (jnp.where(side_off == 0, first[4], second[4]) * SCALING).astype(LOW)
        return carry

    lax.fori_loop(first_pair, first_pair + count, pair_step, 0)
    return flip


def attend_back_one_body(
    q_ref, k_ref, v_ref, pk_ref, pq_ref, probs_ref, gctx_ref,
    gq_ref, gk_ref, gv_ref, gpk_ref, gpq_ref, qr_ref, kr_ref,
):
    heads_back(
        0, PAIRS // 2, (q_ref, k_ref, v_ref, pk_ref, pq_ref, probs_ref, gctx_ref),
        (gq_ref, gk_ref, gv_ref, gpk_ref, gpq_ref, qr_ref, kr_ref),
    )


def attend_back_two_body(
    meta_ref, q_ref, k_ref, v_ref, pk_ref, pq_ref, probs_ref, gctx_ref, hq, hk, hv, hpk, hpq,
    tok_ref, relw_ref, gres_ref, bucket_ref,
    own_q, own_k, own_v, own_rel, p0, p1, p2, p3, p4, p5,
    out_ref,
    home_ref, keep_ref, send_ref,
    grad_ref, gv_ref, pos_ref, qr_ref, kr_ref, gtok_ref, w_ref, sem,
):
    gq_ref, gk_ref, gpq_ref, gpk_ref = grad_ref.at[0], grad_ref.at[1], pos_ref.at[0], pos_ref.at[1]
    copies = Copies(sem)
    load_first(meta_ref, copies, (own_q, own_k, own_v, own_rel), (p0, p1, p2, p3, p4, p5), w_ref)
    copies.start()
    for target, done in ((gq_ref, hq), (gk_ref, hk), (gv_ref, hv), (gpk_ref, hpk), (gpq_ref, hpq)):
        target[:, : D // 2] = done[...]
    flip = heads_back(
        PAIRS // 2, PAIRS // 2, (q_ref, k_ref, v_ref, pk_ref, pq_ref, probs_ref, gctx_ref),
        (gq_ref, gk_ref, gv_ref, gpk_ref, gpq_ref, qr_ref, kr_ref),
    )
    copies.wait()
    tok, relw = tok_ref[...], relw_ref[...]
    x, core = meta_ref[X], meta_ref[CORE]

    def put(start, size, value):
        for shard in range(GROUP):
            keep, send = select_halves(meta_ref, value[shard * 2 * size : (shard + 1) * 2 * size])
            keep_ref[position(x ^ shard, near_of(core)), pl.ds(start, size)] = keep
            send_ref[position(x ^ shard, far_of(core)), pl.ds(start, size)] = send

    def weight_step(i, carry):
        g_tok, g_rel = carry
        start = pl.multiple_of(i * HALF, HALF)
        grads = mm(flip, grad_ref[i]).astype(LOW)
        weight = w_ref[:, :, pl.ds(start, HALF), :].reshape(D, D)
        put(start, HALF, mm_tn(tok, grads) + mm_tn(relw, pos_ref[i]))
        return g_tok + mm_nt(grads, weight), g_rel + mm_nt(pos_ref[i], weight)

    g_tok, g_rel = lax.fori_loop(0, 2, weight_step, (gres_ref[...], jnp.zeros((OFFS, D), F32)))
    g_value = gv_ref[...]
    gtok_ref[...] = (g_tok + mm_nt(g_value, whole(w_ref, 2 * HALF, HALF))).astype(LOW)
    put(2 * HALF, HALF, mm_tn(tok, g_value))
    pick = (bucket_ref[...] == iota((OFFS, OFFS), 1)).astype(LOW)
    put(REL_AT, REL_HALF, mm_tn(pick, g_rel.astype(LOW)))
    for member in range(GROUP):
        home_ref[member, 0] = out_ref[member * PART : (member + 1) * PART, :]
        home_ref[member, 1] = gtok_ref[member * PART : (member + 1) * PART, :]


def attend_back_one(saved, gctx):
    shape = jax.ShapeDtypeStruct
    full = pl.BlockSpec(memory_space=pltpu.VMEM)
    return pl.pallas_call(
        attend_back_one_body,
        out_shape=(*(shape((ROWS, D // 2), LOW),) * 3, *(shape((OFFS, D // 2), LOW),) * 2),
        in_specs=[full] * 7,
        out_specs=(full,) * 5,
        scratch_shapes=[pltpu.VMEM((ROWS, D), LOW), pltpu.VMEM((ROWS, D), LOW)],
        compiler_params=pltpu.CompilerParams(vmem_limit_bytes=24 * MIB),
        cost_estimate=pl.CostEstimate(flops=8_000_000_000, bytes_accessed=20_000_000, transcendentals=0),
        name="attend_back_one",
    )(*saved, gctx)


def attend_back_two(meta, saved, gctx, half_done, tok, relw, gres, bucket_column, own, pieces, out):
    shape = jax.ShapeDtypeStruct
    full, anywhere = pl.BlockSpec(memory_space=pltpu.VMEM), pl.BlockSpec(memory_space=pltpu.HBM)
    return pl.pallas_call(
        attend_back_two_body,
        out_shape=(shape((GROUP, 2, PART, D), LOW), shape((GROUP, FIRST, D), LOW), shape((GROUP, FIRST, D), LOW)),
        in_specs=[pl.BlockSpec(memory_space=pltpu.SMEM)] + [full] * 16 + [anywhere] * 10 + [full],
        out_specs=(full,) * 3,
        scratch_shapes=[
            pltpu.VMEM((2, ROWS, D), LOW), pltpu.VMEM((ROWS, D), LOW), pltpu.VMEM((2, OFFS, D), LOW),
            *(pltpu.VMEM((ROWS, D), LOW),) * 3,
            pltpu.VMEM((GROUP, 2, FIRST, D), LOW), pltpu.SemaphoreType.DMA((10,)),
        ],
        compiler_params=pltpu.CompilerParams(vmem_limit_bytes=22 * MIB),
        cost_estimate=pl.CostEstimate(flops=14_000_000_000, bytes_accessed=40_000_000, transcendentals=0),
        name="attend_back_two",
    )(meta, *saved, gctx, *half_done, tok, relw, gres, bucket_column, *own, *pieces, out)


def feed_body(
    meta_ref, tok_ref, ctx_one_ref, ctx_two_ref, rows_ref, own_outer, own_out, own_norm, own_inner, *rest,
):
    pieces, rest = rest[:10], rest[10:]
    out_ref, gctx_ref, gres_ref, keep_ref, send_ref, keep_in_ref, send_in_ref = rest[:7]
    up_ref, low_ref, act_ref, slope_ref, w_ref, in_ref, sem = rest[7:]
    copies = Copies(sem)
    copies.add(rows_ref.at[:, 1], up_ref)
    load_second(meta_ref, copies, (own_outer, own_out, own_norm, own_inner), pieces, w_ref, in_ref)
    copies.start()
    copies.wait()
    x, core = meta_ref[X], meta_ref[CORE]
    assist, assist_peer = assist_of(meta_ref, core), assist_of(meta_ref, 1 - core)

    def put_outer(shard, quarter, keep, send, start):
        rows = slice(start, start + keep.shape[0])
        keep_ref[position(assist ^ quarter, 1), position(x ^ shard, near_of(core)), rows] = keep
        send_ref[position(assist_peer ^ quarter, 1), position(x ^ shard, far_of(core)), rows] = send

    def put_inner(shard, quarter, keep, send):
        keep_in_ref[position(assist ^ quarter, 3), position(x ^ shard, near_of(core))] = keep
        send_in_ref[position(assist_peer ^ quarter, 3), position(x ^ shard, far_of(core))] = send

    length = meta_ref[LENGTH]
    mask = (iota((ROWS, 1), 0) < length).astype(F32)
    norm_rows = []
    for s in range(GROUP):
        side, place = second_block(meta_ref, s, 0)
        norm_rows.append(w_ref[side, place, NORM_AT : NORM_AT + QUARTER - HALF, :].astype(F32)[:1])
    gain_one, bias_one, gain_two, bias_two = (
        jnp.concatenate([row[:, i * PIECE : (i + 1) * PIECE] for row in norm_rows], axis=1) for i in range(4)
    )
    token = tok_ref[...].astype(F32)
    ctx = jnp.concatenate([ctx_one_ref[...], ctx_two_ref[...]], axis=1)
    blocks = [second_block(meta_ref, shard, half) for shard in range(GROUP) for half in range(2)]
    w_out = jnp.concatenate([w_ref[side, place, OUT_AT : OUT_AT + HALF, :] for side, place in blocks], axis=0)
    attn = mm(ctx, w_out)

    def norm(values):
        center = values - jnp.mean(values, axis=1, keepdims=True)
        inverse = lax.rsqrt(jnp.mean(center * center, axis=1, keepdims=True) + EPSILON)
        return center * inverse, inverse

    def norm_back(upstream, normed, inverse, gain):
        scaled = upstream * gain
        plain = jnp.mean(scaled, axis=1, keepdims=True)
        cross = jnp.mean(scaled * normed, axis=1, keepdims=True)
        return inverse * (scaled - plain - normed * cross)

    def total(values):
        return jnp.sum(values, axis=0, keepdims=True)

    normed_one, inverse_one = norm(token + attn)
    hidden_one = normed_one * gain_one + bias_one
    low_ref[...] = hidden_one.astype(LOW)

    def columns(c):
        return pl.ds(pl.multiple_of(c * D, D), D)

    def outer_rows(c):
        halves = [second_block(meta_ref, c, half) for half in range(2)]
        return jnp.concatenate([w_ref[side, place, 0 : D // 2, :] for side, place in halves], axis=0)

    def inner_columns(c):
        return jnp.concatenate([in_ref[side, place, :, columns(c)] for side, place in blocks], axis=0)

    def forward_step(c, ffn):
        inner = mm(low_ref[...], inner_columns(c))
        cumulative = 0.5 * (1.0 + lax.erf(inner * 0.5**0.5))
        density = jnp.exp(-0.5 * inner * inner) * 0.3989422804014327
        act = (inner * cumulative).astype(LOW)
        act_ref[c] = act
        slope_ref[c] = cumulative + inner * density
        return ffn + mm(act, outer_rows(c))

    ffn = lax.fori_loop(0, GROUP, forward_step, jnp.zeros((ROWS, D), F32))
    normed_two, inverse_two = norm(hidden_one + ffn)
    layer = (normed_two * gain_two + bias_two) * mask
    out_ref[...] = layer.astype(LOW)
    squares = [token * token * mask, attn * attn * mask, ffn * ffn * mask, layer * layer]
    sums = [jnp.sum(total(s), axis=1, keepdims=True) for s in squares]
    grad_y = up_ref[...].reshape(ROWS, D).astype(F32) * mask
    grad_gain_two = total(grad_y * normed_two)
    grad_bias_two = total(grad_y)
    grad_two = norm_back(grad_y, normed_two, inverse_two, gain_two)
    grad_ffn = grad_two.astype(LOW)

    def back_step(c, grad_hidden):
        grad_act = mm_nt(grad_ffn, outer_rows(c))
        grad_inner = (grad_act * slope_ref[c]).astype(LOW)
        keep, send = select_halves(meta_ref, mm_tn(act_ref[c], grad_ffn))
        for quarter in range(3):
            rows = slice(quarter * QUARTER, (quarter + 1) * QUARTER)
            put_outer(c, quarter, keep[rows], send[rows], 0)
        grad_w = mm_tn(low_ref[...], grad_inner)
        for s in range(GROUP):
            put_inner(s, c, *select_halves(meta_ref, grad_w[s * PIECE : (s + 1) * PIECE]))
        return grad_hidden + mm_nt(grad_inner, inner_columns(c))

    grad_hidden = lax.fori_loop(0, GROUP, back_step, grad_two)
    grad_gain_one = total(grad_hidden * normed_one)
    grad_bias_one = total(grad_hidden)
    grad_one = norm_back(grad_hidden, normed_one, inverse_one, gain_one)
    gres_ref[...] = grad_one
    grad_attn = grad_one.astype(LOW)
    grad_out = mm_tn(ctx, grad_attn)
    for s in range(GROUP):
        put_outer(s, 3, *select_halves(meta_ref, grad_out[s * PIECE : (s + 1) * PIECE]), 0)
    gctx_ref[...] = mm_nt(grad_attn, w_out).astype(LOW)
    lane = iota((1, D), 1)
    stats = jnp.zeros((1, D), F32)
    for i, value in enumerate(sums):
        stats = jnp.where(lane == i, value, stats)
    low = stats - stats.astype(LOW).astype(F32)
    zeros = jnp.zeros((1, D), F32)
    norm_rows = (grad_gain_one, grad_bias_one, grad_gain_two, grad_bias_two)
    for s in range(GROUP):
        row = jnp.concatenate([r[:, s * PIECE : (s + 1) * PIECE] for r in norm_rows], axis=1)
        block = jnp.concatenate([row] + [zeros] * 31 + [stats, low] + [zeros] * 30, axis=0)
        put_outer(s, 3, *select_halves(meta_ref, block), HALF)


def feed(meta, tok, ctx_one, ctx_two, rows, own, pieces):
    shape = jax.ShapeDtypeStruct
    full, anywhere = pl.BlockSpec(memory_space=pltpu.VMEM), pl.BlockSpec(memory_space=pltpu.HBM)
    block, wide = shape((GROUP, GROUP, QUARTER, D), LOW), shape((GROUP, GROUP, HALF, D), LOW)
    return pl.pallas_call(
        feed_body,
        out_shape=(
            shape((ROWS, D), LOW), shape((ROWS, D), LOW), shape((ROWS, D), F32), block, block, wide, wide
        ),
        in_specs=[pl.BlockSpec(memory_space=pltpu.SMEM)] + [full] * 3 + [anywhere] * 15,
        out_specs=(full,) * 7,
        scratch_shapes=[
            pltpu.VMEM((GROUP, PART, D), LOW), pltpu.VMEM((ROWS, D), LOW), pltpu.VMEM((GROUP, ROWS, D), LOW),
            pltpu.VMEM((GROUP, ROWS, D), F32), pltpu.VMEM((2, GROUP, SECOND, D), LOW),
            pltpu.VMEM((2, GROUP, HALF, WIDE), LOW), pltpu.SemaphoreType.DMA((24,)),
        ],
        compiler_params=pltpu.CompilerParams(vmem_limit_bytes=28 * MIB),
        cost_estimate=pl.CostEstimate(flops=16_000_000_000, bytes_accessed=60_000_000, transcendentals=1_600_000),
        name="feed",
    )(meta, tok, ctx_one, ctx_two, rows, *own, *pieces)


def finish_body(
    meta_ref, mine, other, rows_ref,
    q_ref, k_ref, v_ref, rel_ref, outer_ref, wout_ref, inner_ref, extra_ref, out_ref, gtok_ref,
):
    for piece, side in ((mine, 0), (other, 1)):
        core = meta_ref[CORE] if side == 0 else 1 - meta_ref[CORE]
        assist = assist_of(meta_ref, core)
        for i, ref in enumerate((q_ref, k_ref, v_ref, rel_ref)):
            size = REL_HALF if i == 3 else HALF
            ref[pl.ds(pl.multiple_of(core * size, size), size), :] = piece[i * HALF : i * HALF + size, :].astype(F32)

        def piece_step(distance, carry):
            quarter = assist ^ distance
            at = pl.multiple_of(FIRST + distance * SPAN, HALF // 3)
            block = piece[pl.ds(at, QUARTER), :].astype(F32)

            @pl.when(quarter < 3)
            def _():
                outer_ref[pl.ds(pl.multiple_of(core * 3 * QUARTER + quarter * QUARTER, QUARTER), QUARTER), :] = block

            @pl.when(quarter == 3)
            def _():
                wout_ref[pl.ds(pl.multiple_of(core * HALF, HALF), HALF), :] = block[:HALF]
                extra_ref[core] = block[HALF:]

            inner_ref[
                pl.ds(pl.multiple_of(core * HALF, HALF), HALF), pl.ds(pl.multiple_of(quarter * D, D), D)
            ] = piece[pl.ds(at + QUARTER, HALF), :].astype(F32)
            return carry

        lax.fori_loop(0, GROUP, piece_step, 0)
    for k in range(GROUP):
        member = meta_ref[X] ^ k
        out_ref[meta_ref[SEQ + k]] = rows_ref[member, 0]
        gtok_ref[meta_ref[SEQ + k]] = rows_ref[member, 1]


def finish(meta, mine, other, rows):
    shape = jax.ShapeDtypeStruct
    full = pl.BlockSpec(memory_space=pltpu.VMEM)
    return pl.pallas_call(
        finish_body,
        out_shape=(
            *(shape((PIECE, D), F32),) * 3, shape((OFFS // GROUP, D), F32),
            shape((D, D), F32), shape((PIECE, D), F32), shape((PIECE, WIDE), F32), shape((2, QUARTER - HALF, D), F32),
            *(shape((GROUP, PART, D), LOW),) * 2,
        ),
        in_specs=[pl.BlockSpec(memory_space=pltpu.SMEM)] + [full] * 3,
        out_specs=(full,) * 10,
        compiler_params=pltpu.CompilerParams(vmem_limit_bytes=24 * MIB),
        name="finish",
    )(meta, mine, other, rows)


NEAR, FAR = (1, 3), (3, 1)


def hop_x(value, flips):
    pairs = [(c * 4 + i, c * 4 + (i ^ flips[c])) for c in range(2) for i in range(4)]
    return lax.ppermute(value, ("core", "shard"), pairs)


def hop_yz(value, flip, swapped=False):
    pairs = []
    for y in range(4):
        for z in range(4):
            for c in range(2):
                along_y = (c == 0) != swapped
                ty, tz = (y ^ flip, z) if along_y else (y, z ^ flip)
                pairs.append(((y * 4 + z) * 2 + c, (ty * 4 + tz) * 2 + c))
    return lax.ppermute(value, ("y", "z", "core"), pairs)


def swap(value):
    return lax.ppermute(value, "core", [(0, 1), (1, 0)])


def after(value, *others):
    return lax.optimization_barrier((value, *others))[0]


def add(*values):
    total = values[0].astype(F32)
    for value in values[1:]:
        total = total + value.astype(F32)
    return total.astype(LOW)


def exchange_rows(rows):
    return lax.all_to_all(rows, "shard", split_axis=0, concat_axis=0, tiled=True)


def shards(
    hidden, grad_out, lengths, bucket, w_query, w_key, w_value, w_out, w_inner, w_outer, rel_table,
    ln1_gain, ln1_bias, ln2_gain, ln2_bias,
):
    coords = jnp.stack([lax.axis_index(name) for name in ("shard", "y", "z", "core")]).astype(jnp.int32)
    norm_block = jnp.concatenate(
        [jnp.concatenate([ln1_gain, ln1_bias, ln2_gain, ln2_bias])[None], jnp.zeros((31, D), LOW)], axis=0
    )
    bucket_column = jnp.concatenate([bucket[::-1], jnp.full((1,), -1, jnp.int32)])[:, None]
    own_first = (w_query, w_key, w_value, rel_table)
    own_halves = tuple(
        pltpu.with_memory_space_constraint(ref.reshape(2, ref.shape[0] // 2, D), pltpu.HBM) for ref in own_first
    )
    meta, first, second, rows = pack(
        coords, lengths, hidden, grad_out, own_first, (w_outer, w_out, w_inner), norm_block
    )
    near_two, far_two = hop_x(second, NEAR), hop_x(second, FAR)
    near, far = hop_x(first, NEAR), hop_x(first, FAR)
    rows = exchange_rows(rows)
    across_two = hop_x(near_two, FAR)
    base = after(jnp.stack([near_two, far_two, across_two]), near, far)
    base_near, base_far = hop_yz(base, 1), hop_yz(base, 3)
    across = hop_x(near, FAR)
    pieces = (near, far, across, swap(near), swap(far), swap(across))
    part_outer, part_inner = base_near[:, :QUARTER], base_far[:, QUARTER:]
    rows = after(rows, part_outer, part_inner)
    across_outer, across_inner = hop_yz(part_outer, 3), hop_yz(part_inner, 1)
    tok, *saved, relw, probs, ctx = attend_forward(meta, bucket_column, rows, own_halves, pieces)
    across_outer, across_inner, base, base_near, base_far, _ = lax.optimization_barrier(
        (across_outer, across_inner, base, base_near, base_far, ctx)
    )
    arrived = (base, base_near, base_far, across_outer, across_inner)
    swapped = tuple(swap(piece) for piece in arrived)
    probs_two, ctx_two = attend_forward_two(meta, saved)
    swapped = after(swapped, ctx_two)
    out, gctx, gres, keep, send, keep_in, send_in = feed(
        meta, tok, ctx, ctx_two, rows, (w_outer, w_out, norm_block, w_inner), (*arrived, *swapped)
    )
    other, other_in = swap(send), swap(send_in)
    half_done = attend_back_one((*saved, probs), gctx)
    leave = add(keep[:2], other[:2])
    leave_in = add(keep_in[:2], other_in[:2])
    came, came_in = hop_yz(leave, 1), hop_yz(leave_in, 3)
    half_done = after(tuple(half_done), leave, leave_in)
    leaving, keep_one, send_one = attend_back_two(
        meta, (*saved, probs_two), gctx, half_done, tok, relw, gres, bucket_column, own_halves, pieces, out
    )
    other_one = swap(after(send_one, came, came_in))
    leave_one = add(keep_one[:2], other_one[:2])
    came, came_in = after((came, came_in), leave_one)
    last = hop_yz(add(keep[2], other[2], came[0]), 3)
    last_in = hop_yz(add(keep_in[2], other_in[2], came_in[0]), 1)
    came_one = hop_x(leave_one, NEAR)
    came_one = after(came_one, last, last_in)
    leave_two = add(keep_one[2], other_one[2], came_one[0])
    last_one = hop_x(leave_two, FAR)
    last, last_in, _ = lax.optimization_barrier((last, last_in, leave_two))
    mine = add(keep[3], other[3], came[1], last)
    mine_in = add(keep_in[3], other_in[3], came_in[1], last_in)
    both = jnp.concatenate([mine, mine_in], axis=1)
    came_x = hop_x(both[:2], NEAR)
    home = exchange_rows(leaving)
    last_one = after(last_one, came_x)
    mine_one = add(keep_one[3], other_one[3], came_one[1], last_one)
    come_one = hop_yz(mine_one, 1, swapped=True)
    last_x = hop_x(after(add(both[2], came_x[0]), mine_one), FAR)
    mine_one = add(mine_one, after(come_one, last_x))
    come_one = hop_yz(mine_one, 3, swapped=True)
    both = after(add(both[3], came_x[1], last_x), mine_one)
    step = hop_yz(both, 1, swapped=True)
    mine_one = add(mine_one, after(come_one, step))
    come_one = hop_yz(mine_one, 1)
    both = after(add(both, step), mine_one)
    step = hop_yz(both, 3, swapped=True)
    mine_one = add(mine_one, after(come_one, step))
    come_one = hop_yz(mine_one, 3)
    both = after(add(both, step), mine_one)
    both = [both, *(hop_yz(both, flip) for flip in (1, 3, 2))]
    both[1], both[2], both[3] = both[1], both[3], both[2]
    mine_one = add(mine_one, come_one)
    packed = after(jnp.concatenate([mine_one, *both], axis=0), home)
    q_grad, k_grad, v_grad, rel_grad, outer_grad, out_grad, inner_grad, extra, layer_output, grad_hidden = finish(
        meta, packed, swap(packed), home
    )
    norm_sums = extra[0, 0].reshape(GROUP, PIECE)
    stats = extra[1, 0, :GROUP] + extra[1, 1, :GROUP]
    return (
        layer_output, grad_hidden, q_grad, k_grad, v_grad, out_grad, inner_grad, outer_grad, rel_grad,
        norm_sums[0], norm_sums[1], norm_sums[2], norm_sums[3],
        jnp.sqrt(stats / (TOKENS * D)),
    )


def solution(mesh):
    split = Mesh(mesh.devices.reshape(4, 4, 2, 4), ("y", "z", "core", "shard"))
    rep = ("y", "z", "core")
    rows, vector = P("shard", None), P("shard")
    batch = P(rep, "shard", None)
    return jax.shard_map(
        shards,
        mesh=split,
        in_specs=(batch, batch, P(rep), P(), *(rows,) * 7, *(vector,) * 4),
        out_specs=(batch, batch, *(rows,) * 7, *(vector,) * 4, P()),
        check_vma=False,
    )
```

```python
import jax
import jax.numpy as jnp
from jax import lax
from jax.experimental import pallas as pl
from jax.experimental.pallas import tpu as pltpu
from jax.sharding import Mesh
from jax.sharding import PartitionSpec as P

D = 768
HEADS = 12
HEAD_DIM = 64
PAIRS = HEADS // 2
ROWS = 256
OFFS = 512
TOKENS = 20480
GROUP = 4
PIECE = D // GROUP
HALF = PIECE // 2
WIDE = GROUP * D
REL_HALF = OFFS // GROUP // 2
REL_AT = 3 * HALF
FIRST = 3 * HALF + REL_HALF
OUT_AT = D // 2
NORM_AT = D // 2 + HALF
QUARTER = 128
SECOND = GROUP * QUARTER
SPAN = QUARTER + HALF
PART = ROWS // GROUP
X, Y, Z, CORE, LENGTH, SEQ = 0, 1, 2, 3, 4, 5
META = 16
EPSILON = 1e-07
MASKED = -1e30
SCALING = (3.0 * HEAD_DIM) ** (-0.5)
F32 = jnp.float32
LOW = jnp.bfloat16
MIB = 1024 * 1024


def mm(a, b):
    return lax.dot_general(a, b, (((1,), (0,)), ((), ())), preferred_element_type=F32)


def mm_nt(a, b):
    return lax.dot_general(a, b, (((1,), (1,)), ((), ())), preferred_element_type=F32)


def mm_tn(a, b):
    return lax.dot_general(a, b, (((0,), (0,)), ((), ())), preferred_element_type=F32)


def iota(shape, dim):
    return lax.broadcasted_iota(jnp.int32, shape, dim)


def whole(ref, start, size):
    piece = ref[:, :, start : start + size, :]
    return piece.reshape(GROUP * 2 * size, piece.shape[3])


def run_copies(copies):
    for copy in copies:
        copy.start()
    for copy in copies:
        copy.wait()


class Copies:
    def __init__(self, sem):
        self.sem, self.made = sem, []

    def add(self, source, target):
        self.made.append(pltpu.make_async_copy(source, target, self.sem.at[len(self.made)]))

    def start(self):
        for copy in self.made:
            copy.start()

    def wait(self):
        for copy in self.made:
            copy.wait()


def near_of(core):
    return 1 + 2 * core


def far_of(core):
    return 3 - 2 * core


def assist_of(meta_ref, core):
    return jnp.where(core == 0, meta_ref[Y], meta_ref[Z])


def position(distance, near):
    far = 4 - near
    place = jnp.where(distance == near, 1, jnp.where(distance == far, 2, 0))
    return jnp.where(distance == 0, 3, place)


def pack_body(
    coord_ref, length_ref, hidden_ref, grad_ref, own_q, own_k, own_v, own_rel, own_outer, own_out, own_inner, norm_ref,
    meta_ref, first_ref, second_ref, *rest,
):
    rows_out, sem, tail_sem = rest
    x, y, z, core = (coord_ref[i] for i in range(4))
    for i in range(4):
        meta_ref[i] = coord_ref[i]
    lengths = [length_ref[i] for i in range(GROUP)]
    dealing = []
    for i in range(GROUP):
        rank = jnp.int32(0)
        for j in range(GROUP):
            if j != i:
                ahead = lengths[j] >= lengths[i] if j < i else lengths[j] > lengths[i]
                rank = rank + ahead.astype(jnp.int32)
        dealing.append(rank)
    length = jnp.int32(0)
    for i in range(GROUP):
        length = length + jnp.where(dealing[i] == x, lengths[i], 0)
    meta_ref[LENGTH] = length
    copies = Copies(sem)
    for k in range(GROUP):
        source = jnp.int32(0)
        for i in range(GROUP):
            source = source + jnp.where(dealing[i] == (x ^ k), i, 0)
        meta_ref[SEQ + k] = source
        copies.add(hidden_ref.at[source], rows_out.at[x ^ k, 0])
        copies.add(grad_ref.at[source], rows_out.at[x ^ k, 1])
    for i in range(SEQ + GROUP, META):
        meta_ref[i] = jnp.int32(0)
    for i, ref in enumerate((own_q, own_k, own_v, own_rel)):
        size = REL_HALF if i == 3 else HALF
        copies.add(ref.at[pl.ds(core * size, size)], first_ref.at[pl.ds(i * HALF, size)])
    quarter = jnp.where(core == 0, y, z)
    copies.add(
        own_inner.at[pl.ds(core * HALF, HALF), pl.ds(pl.multiple_of(quarter * D, D), D)],
        second_ref.at[pl.ds(QUARTER, HALF)],
    )
    copies.start()
    tail = Copies(tail_sem)

    @pl.when(quarter < 3)
    def _():
        copy = pltpu.make_async_copy(
            own_outer.at[pl.ds(core * 3 * QUARTER + quarter * QUARTER, QUARTER)], second_ref.at[pl.ds(0, QUARTER)],
            tail_sem.at[0],
        )
        copy.start()
        copy.wait()

    @pl.when(quarter == 3)
    def _():
        tail.add(own_out.at[pl.ds(core * HALF, HALF)], second_ref.at[pl.ds(0, HALF)])
        tail.add(norm_ref, second_ref.at[pl.ds(HALF, QUARTER - HALF)])
        tail.start()
        tail.wait()

    copies.wait()


def pack(coords, lengths, hidden, grad_out, own_first, own_second, norm_block):
    shape = jax.ShapeDtypeStruct
    scalars, anywhere = pl.BlockSpec(memory_space=pltpu.SMEM), pl.BlockSpec(memory_space=pltpu.HBM)
    full = pl.BlockSpec(memory_space=pltpu.VMEM)
    return pl.pallas_call(
        pack_body,
        out_shape=(
            shape((META,), jnp.int32), shape((FIRST, D), LOW), shape((SPAN, D), LOW), shape((GROUP, 2, PART, D), LOW),
        ),
        in_specs=[scalars, scalars] + [anywhere] * 10,
        out_specs=(scalars, full, full, full),
        scratch_shapes=[pltpu.SemaphoreType.DMA((13,)), pltpu.SemaphoreType.DMA((2,))],
        compiler_params=pltpu.CompilerParams(vmem_limit_bytes=60 * MIB),
        name="pack",
    )(coords, lengths, hidden, grad_out, *own_first, *own_second, norm_block)


def load_first(meta_ref, copies, own, pieces, w_ref):
    x, core = meta_ref[X], meta_ref[CORE]
    near, far = x ^ near_of(core), x ^ far_of(core)
    slots = ((near, core), (far, core), (x ^ 2, core), (far, 1 - core), (near, 1 - core), (x ^ 2, 1 - core))
    for piece, (slot, half) in zip(pieces, slots):
        copies.add(piece, w_ref.at[slot, half])
    for i, ref in enumerate(own):
        size = REL_HALF if i == 3 else HALF
        copies.add(ref, w_ref.at[x, :, pl.ds(i * HALF, size)])


def load_second(meta_ref, copies, own, pieces, w_ref, in_ref):
    own_outer, own_out, own_norm, own_inner = own
    for side in range(2):
        assist = assist_of(meta_ref, meta_ref[CORE] if side == 0 else 1 - meta_ref[CORE])
        base, near, far, across_outer, across_inner = pieces[5 * side : 5 * side + 5]
        for distance, outer, inner in (
            (0, base.at[:, pl.ds(0, QUARTER)], base.at[:, pl.ds(QUARTER, HALF)]),
            (1, near.at[:, pl.ds(0, QUARTER)], near.at[:, pl.ds(QUARTER, HALF)]),
            (3, far.at[:, pl.ds(0, QUARTER)], far.at[:, pl.ds(QUARTER, HALF)]),
            (2, across_outer, across_inner),
        ):
            quarter = assist ^ distance
            copies.add(outer, w_ref.at[side, pl.ds(0, 3), pl.ds(quarter * QUARTER, QUARTER)])
            copies.add(inner, in_ref.at[side, pl.ds(0, 3), :, pl.ds(pl.multiple_of(quarter * D, D), D)])
    for half in range(2):
        side = half ^ meta_ref[CORE]
        copies.add(own_outer.at[pl.ds(half * 3 * QUARTER, 3 * QUARTER)], w_ref.at[side, 3, pl.ds(0, 3 * QUARTER)])
        copies.add(own_out.at[pl.ds(half * HALF, HALF)], w_ref.at[side, 3, pl.ds(OUT_AT, HALF)])
        copies.add(own_inner.at[pl.ds(half * HALF, HALF)], in_ref.at[side, 3])
    copies.add(own_norm, w_ref.at[meta_ref[CORE], 3, pl.ds(NORM_AT, QUARTER - HALF)])


def second_block(meta_ref, shard, half):
    apart = meta_ref[X] ^ shard
    place = jnp.where(apart == near_of(half), 0, jnp.where(apart == far_of(half), 1, 2))
    return half ^ meta_ref[CORE], jnp.where(apart == 0, 3, place)


def select_halves(meta_ref, value):
    half = value.shape[0] // 2
    low, high = value[:half].astype(LOW), value[half:].astype(LOW)
    first_core = meta_ref[CORE] == 0
    return jnp.where(first_core, low, high), jnp.where(first_core, high, low)


def heads_forward(meta_ref, first_pair, refs, probs_ref, ctx_ref):
    q_ref, k_ref, v_ref, pk_ref, pq_ref = refs
    length = meta_ref[LENGTH]
    valid = iota((ROWS, ROWS), 1) < length
    side = iota((ROWS, 2 * HEAD_DIM), 1) // HEAD_DIM

    def pair_step(pair, carry):
        out_cols = pl.ds(pl.multiple_of((pair - first_pair) * 2 * HEAD_DIM, 2 * HEAD_DIM), 2 * HEAD_DIM)
        cols = pl.ds(pl.multiple_of(pair * 2 * HEAD_DIM, 2 * HEAD_DIM), 2 * HEAD_DIM)
        q_pair, k_pair, v_pair = q_ref[:, cols], k_ref[:, cols], v_ref[:, cols]
        pk_pair, pq_pair = pk_ref[:, cols], pq_ref[:, cols]
        zero = jnp.zeros_like(q_pair)
        contexts = []
        for h in range(2):
            mine = side == h
            q_head = jnp.where(mine, q_pair, zero)
            k_head = jnp.where(mine, k_pair, zero)
            content = mm_nt(q_head, k_pair)
            to_off = mm_nt(q_head, pk_pair)
            from_off = mm_nt(k_head, pq_pair)
            to_rel = pltpu.roll(to_off, ROWS + 1, 1, stride=1, stride_axis=0)[:, :ROWS]
            from_rel = pltpu.roll(from_off, ROWS + 1, 1, stride=1, stride_axis=0)[:, :ROWS]
            scores = (content + to_rel + from_rel.T) * SCALING
            scores = jnp.where(valid, scores, MASKED)
            top = jnp.max(scores, axis=1, keepdims=True)
            shifted = jnp.exp(scores - top)
            summed = jnp.sum(shifted, axis=1, keepdims=True)
            probs = (shifted * (1.0 / summed)).astype(LOW)
            probs_ref[2 * (pair - first_pair) + h] = probs
            contexts.append(mm(probs, v_pair))
        ctx_ref[:, out_cols] = jnp.where(side == 0, contexts[0], contexts[1]).astype(LOW)
        return carry

    lax.fori_loop(first_pair, first_pair + PAIRS // 2, pair_step, 0)


def attend_forward_body(
    meta_ref, bucket_ref, rows_ref, own_q, own_k, own_v, own_rel, p0, p1, p2, p3, p4, p5,
    tok_ref, q_ref, k_ref, v_ref, pk_ref, pq_ref, relw_ref, probs_ref, ctx_ref,
    w_ref, rows_in, sem,
):
    copies = Copies(sem)
    copies.add(rows_ref.at[:, 0], rows_in)
    load_first(meta_ref, copies, (own_q, own_k, own_v, own_rel), (p0, p1, p2, p3, p4, p5), w_ref)
    copies.start()
    copies.wait()
    tok = rows_in[...].reshape(ROWS, D)
    tok_ref[...] = tok
    rel = whole(w_ref, REL_AT, REL_HALF)
    pick = (bucket_ref[...] == iota((OFFS, OFFS), 1)).astype(LOW)
    relw = mm(pick, rel).astype(LOW)
    relw_ref[...] = relw
    w_query = whole(w_ref, 0, HALF)
    q_ref[...] = mm(tok, w_query).astype(LOW)
    pq_ref[...] = mm(relw, w_query).astype(LOW)
    w_key = whole(w_ref, HALF, HALF)
    k_ref[...] = mm(tok, w_key).astype(LOW)
    pk_ref[...] = mm(relw, w_key).astype(LOW)
    v_ref[...] = mm(tok, whole(w_ref, 2 * HALF, HALF)).astype(LOW)
    heads_forward(meta_ref, 0, (q_ref, k_ref, v_ref, pk_ref, pq_ref), probs_ref, ctx_ref)


def attend_forward_two_body(meta_ref, q_ref, k_ref, v_ref, pk_ref, pq_ref, probs_ref, ctx_ref):
    heads_forward(meta_ref, PAIRS // 2, (q_ref, k_ref, v_ref, pk_ref, pq_ref), probs_ref, ctx_ref)


def attend_forward(meta, bucket_column, rows, own, pieces):
    shape = jax.ShapeDtypeStruct
    full, anywhere = pl.BlockSpec(memory_space=pltpu.VMEM), pl.BlockSpec(memory_space=pltpu.HBM)
    return pl.pallas_call(
        attend_forward_body,
        out_shape=(
            *(shape((ROWS, D), LOW),) * 4,
            shape((OFFS, D), LOW), shape((OFFS, D), LOW), shape((OFFS, D), LOW),
            shape((HEADS // 2, ROWS, ROWS), LOW), shape((ROWS, D // 2), LOW),
        ),
        in_specs=[pl.BlockSpec(memory_space=pltpu.SMEM), full] + [anywhere] * 11,
        out_specs=(full,) * 9,
        scratch_shapes=[
            pltpu.VMEM((GROUP, 2, FIRST, D), LOW), pltpu.VMEM((GROUP, PART, D), LOW), pltpu.SemaphoreType.DMA((11,)),
        ],
        compiler_params=pltpu.CompilerParams(vmem_limit_bytes=28 * MIB),
        cost_estimate=pl.CostEstimate(flops=12_000_000_000, bytes_accessed=40_000_000, transcendentals=800_000),
        name="attend_forward",
    )(meta, bucket_column, rows, *own, *pieces)


def attend_forward_two(meta, saved):
    shape = jax.ShapeDtypeStruct
    full = pl.BlockSpec(memory_space=pltpu.VMEM)
    return pl.pallas_call(
        attend_forward_two_body,
        out_shape=(shape((HEADS // 2, ROWS, ROWS), LOW), shape((ROWS, D // 2), LOW)),
        in_specs=[pl.BlockSpec(memory_space=pltpu.SMEM)] + [full] * 5,
        out_specs=(full,) * 2,
        compiler_params=pltpu.CompilerParams(vmem_limit_bytes=24 * MIB),
        cost_estimate=pl.CostEstimate(flops=8_000_000_000, bytes_accessed=20_000_000, transcendentals=400_000),
        name="attend_forward_two",
    )(meta, *saved)


def both_heads(pair, side):
    zero = jnp.zeros_like(pair)
    return jnp.concatenate([jnp.where(side == h, pair, zero) for h in range(2)], axis=0)


def heads_back(first_pair, count, refs, outs):
    q_ref, k_ref, v_ref, pk_ref, pq_ref, probs_ref, gctx_ref = refs
    gq_ref, gk_ref, gv_ref, gpk_ref, gpq_ref, qr_ref, kr_ref = outs
    flip = (iota((ROWS, ROWS), 0) + iota((ROWS, ROWS), 1) == ROWS - 1).astype(LOW)
    qr_ref[...] = mm(flip, q_ref[...]).astype(LOW)
    kr_ref[...] = mm(flip, k_ref[...]).astype(LOW)
    side = iota((ROWS, 2 * HEAD_DIM), 1) // HEAD_DIM
    side_off = iota((OFFS, 2 * HEAD_DIM), 1) // HEAD_DIM
    blank = jnp.zeros((ROWS, OFFS - ROWS), F32)

    def pair_step(pair, carry):
        cols = pl.ds(pl.multiple_of(pair * 2 * HEAD_DIM, 2 * HEAD_DIM), 2 * HEAD_DIM)
        q_pair, k_pair, v_pair = q_ref[:, cols], k_ref[:, cols], v_ref[:, cols]
        pk_pair, pq_pair, gctx_pair = pk_ref[:, cols], pq_ref[:, cols], gctx_ref[:, cols]
        qr_pair, kr_pair = qr_ref[:, cols], kr_ref[:, cols]
        grad_probs_both = mm_nt(both_heads(gctx_pair, side), v_pair)
        scores_both, probs_both = [], []
        for h in range(2):
            grad_probs = grad_probs_both[h * ROWS : (h + 1) * ROWS]
            probs_low = probs_ref[2 * (pair - first_pair) + h]
            probs = probs_low.astype(F32)
            inner = jnp.sum(probs * grad_probs, axis=1, keepdims=True)
            scores_both.append((probs * (grad_probs - inner)).astype(LOW))
            probs_both.append(probs_low)
        g_value = mm_tn(jnp.concatenate(probs_both, axis=1), gctx_pair)
        rows_both = mm(flip, jnp.concatenate(scores_both, axis=1))
        cols_both = mm_nt(flip, jnp.concatenate(scores_both, axis=0))

        def spread_out(both):
            return [
                pltpu.roll(
                    jnp.concatenate([both[:, h * ROWS : (h + 1) * ROWS], blank], axis=1), 0, 1, stride=1, stride_axis=0
                ).astype(LOW)
                for h in range(2)
            ]

        def stacked(both):
            return jnp.concatenate([both[:, :ROWS], both[:, ROWS:]], axis=0).astype(LOW)

        to_off, from_off = spread_out(rows_both), spread_out(cols_both)
        g_query = mm(stacked(rows_both), k_pair) + mm(jnp.concatenate(to_off, axis=0), pk_pair)
        g_key = mm(stacked(cols_both), q_pair) + mm(jnp.concatenate(from_off, axis=0), pq_pair)
        g_pk = mm_tn(jnp.concatenate(to_off, axis=1), qr_pair)
        g_pq = mm_tn(jnp.concatenate(from_off, axis=1), kr_pair)
        first = [grad[: grad.shape[0] // 2] for grad in (g_value, g_query, g_key, g_pk, g_pq)]
        second = [grad[grad.shape[0] // 2 :] for grad in (g_value, g_query, g_key, g_pk, g_pq)]
        gv_ref[:, cols] = jnp.where(side == 0, first[0], second[0]).astype(LOW)
        gq_ref[:, cols] = (jnp.where(side == 0, first[1], second[1]) * SCALING).astype(LOW)
        gk_ref[:, cols] = (jnp.where(side == 0, first[2], second[2]) * SCALING).astype(LOW)
        gpk_ref[:, cols] = (jnp.where(side_off == 0, first[3], second[3]) * SCALING).astype(LOW)
        gpq_ref[:, cols] = (jnp.where(side_off == 0, first[4], second[4]) * SCALING).astype(LOW)
        return carry

    lax.fori_loop(first_pair, first_pair + count, pair_step, 0)
    return flip


def attend_back_one_body(
    q_ref, k_ref, v_ref, pk_ref, pq_ref, probs_ref, gctx_ref,
    gq_ref, gk_ref, gv_ref, gpk_ref, gpq_ref, qr_ref, kr_ref,
):
    heads_back(
        0, PAIRS // 2, (q_ref, k_ref, v_ref, pk_ref, pq_ref, probs_ref, gctx_ref),
        (gq_ref, gk_ref, gv_ref, gpk_ref, gpq_ref, qr_ref, kr_ref),
    )


def attend_back_two_body(
    meta_ref, q_ref, k_ref, v_ref, pk_ref, pq_ref, probs_ref, gctx_ref, hq, hk, hv, hpk, hpq,
    tok_ref, relw_ref, gres_ref, bucket_ref,
    own_q, own_k, own_v, own_rel, p0, p1, p2, p3, p4, p5,
    out_ref,
    home_ref, keep_ref, send_ref,
    grad_ref, gv_ref, pos_ref, qr_ref, kr_ref, gtok_ref, w_ref, sem,
):
    gq_ref, gk_ref, gpq_ref, gpk_ref = grad_ref.at[0], grad_ref.at[1], pos_ref.at[0], pos_ref.at[1]
    copies = Copies(sem)
    load_first(meta_ref, copies, (own_q, own_k, own_v, own_rel), (p0, p1, p2, p3, p4, p5), w_ref)
    copies.start()
    for target, done in ((gq_ref, hq), (gk_ref, hk), (gv_ref, hv), (gpk_ref, hpk), (gpq_ref, hpq)):
        target[:, : D // 2] = done[...]
    flip = heads_back(
        PAIRS // 2, PAIRS // 2, (q_ref, k_ref, v_ref, pk_ref, pq_ref, probs_ref, gctx_ref),
        (gq_ref, gk_ref, gv_ref, gpk_ref, gpq_ref, qr_ref, kr_ref),
    )
    copies.wait()
    tok, relw = tok_ref[...], relw_ref[...]
    x, core = meta_ref[X], meta_ref[CORE]

    def put(start, size, value):
        for shard in range(GROUP):
            keep, send = select_halves(meta_ref, value[shard * 2 * size : (shard + 1) * 2 * size])
            keep_ref[position(x ^ shard, near_of(core)), pl.ds(start, size)] = keep
            send_ref[position(x ^ shard, far_of(core)), pl.ds(start, size)] = send

    def weight_step(i, carry):
        g_tok, g_rel = carry
        start = pl.multiple_of(i * HALF, HALF)
        grads = mm(flip, grad_ref[i]).astype(LOW)
        weight = w_ref[:, :, pl.ds(start, HALF), :].reshape(D, D)
        put(start, HALF, mm_tn(tok, grads) + mm_tn(relw, pos_ref[i]))
        return g_tok + mm_nt(grads, weight), g_rel + mm_nt(pos_ref[i], weight)

    g_tok, g_rel = lax.fori_loop(0, 2, weight_step, (gres_ref[...], jnp.zeros((OFFS, D), F32)))
    g_value = gv_ref[...]
    gtok_ref[...] = (g_tok + mm_nt(g_value, whole(w_ref, 2 * HALF, HALF))).astype(LOW)
    put(2 * HALF, HALF, mm_tn(tok, g_value))
    pick = (bucket_ref[...] == iota((OFFS, OFFS), 1)).astype(LOW)
    put(REL_AT, REL_HALF, mm_tn(pick, g_rel.astype(LOW)))
    for member in range(GROUP):
        home_ref[member, 0] = out_ref[member * PART : (member + 1) * PART, :]
        home_ref[member, 1] = gtok_ref[member * PART : (member + 1) * PART, :]


def attend_back_one(saved, gctx):
    shape = jax.ShapeDtypeStruct
    full = pl.BlockSpec(memory_space=pltpu.VMEM)
    return pl.pallas_call(
        attend_back_one_body,
        out_shape=(*(shape((ROWS, D // 2), LOW),) * 3, *(shape((OFFS, D // 2), LOW),) * 2),
        in_specs=[full] * 7,
        out_specs=(full,) * 5,
        scratch_shapes=[pltpu.VMEM((ROWS, D), LOW), pltpu.VMEM((ROWS, D), LOW)],
        compiler_params=pltpu.CompilerParams(vmem_limit_bytes=24 * MIB),
        cost_estimate=pl.CostEstimate(flops=8_000_000_000, bytes_accessed=20_000_000, transcendentals=0),
        name="attend_back_one",
    )(*saved, gctx)


def attend_back_two(meta, saved, gctx, half_done, tok, relw, gres, bucket_column, own, pieces, out):
    shape = jax.ShapeDtypeStruct
    full, anywhere = pl.BlockSpec(memory_space=pltpu.VMEM), pl.BlockSpec(memory_space=pltpu.HBM)
    return pl.pallas_call(
        attend_back_two_body,
        out_shape=(shape((GROUP, 2, PART, D), LOW), shape((GROUP, FIRST, D), LOW), shape((GROUP, FIRST, D), LOW)),
        in_specs=[pl.BlockSpec(memory_space=pltpu.SMEM)] + [full] * 16 + [anywhere] * 10 + [full],
        out_specs=(full,) * 3,
        scratch_shapes=[
            pltpu.VMEM((2, ROWS, D), LOW), pltpu.VMEM((ROWS, D), LOW), pltpu.VMEM((2, OFFS, D), LOW),
            *(pltpu.VMEM((ROWS, D), LOW),) * 3,
            pltpu.VMEM((GROUP, 2, FIRST, D), LOW), pltpu.SemaphoreType.DMA((10,)),
        ],
        compiler_params=pltpu.CompilerParams(vmem_limit_bytes=22 * MIB),
        cost_estimate=pl.CostEstimate(flops=14_000_000_000, bytes_accessed=40_000_000, transcendentals=0),
        name="attend_back_two",
    )(meta, *saved, gctx, *half_done, tok, relw, gres, bucket_column, *own, *pieces, out)


def feed_body(
    meta_ref, tok_ref, ctx_one_ref, ctx_two_ref, rows_ref, own_outer, own_out, own_norm, own_inner, *rest,
):
    pieces, rest = rest[:10], rest[10:]
    out_ref, gctx_ref, gres_ref, keep_ref, send_ref, keep_in_ref, send_in_ref = rest[:7]
    up_ref, low_ref, act_ref, slope_ref, w_ref, in_ref, sem = rest[7:]
    copies = Copies(sem)
    copies.add(rows_ref.at[:, 1], up_ref)
    load_second(meta_ref, copies, (own_outer, own_out, own_norm, own_inner), pieces, w_ref, in_ref)
    copies.start()
    copies.wait()
    x, core = meta_ref[X], meta_ref[CORE]
    assist, assist_peer = assist_of(meta_ref, core), assist_of(meta_ref, 1 - core)

    def put_outer(shard, quarter, keep, send, start):
        rows = slice(start, start + keep.shape[0])
        keep_ref[position(assist ^ quarter, 1), position(x ^ shard, near_of(core)), rows] = keep
        send_ref[position(assist_peer ^ quarter, 1), position(x ^ shard, far_of(core)), rows] = send

    def put_inner(shard, quarter, keep, send):
        keep_in_ref[position(assist ^ quarter, 3), position(x ^ shard, near_of(core))] = keep
        send_in_ref[position(assist_peer ^ quarter, 3), position(x ^ shard, far_of(core))] = send

    length = meta_ref[LENGTH]
    mask = (iota((ROWS, 1), 0) < length).astype(F32)
    norm_rows = []
    for s in range(GROUP):
        side, place = second_block(meta_ref, s, 0)
        norm_rows.append(w_ref[side, place, NORM_AT : NORM_AT + QUARTER - HALF, :].astype(F32)[:1])
    gain_one, bias_one, gain_two, bias_two = (
        jnp.concatenate([row[:, i * PIECE : (i + 1) * PIECE] for row in norm_rows], axis=1) for i in range(4)
    )
    token = tok_ref[...].astype(F32)
    ctx = jnp.concatenate([ctx_one_ref[...], ctx_two_ref[...]], axis=1)
    blocks = [second_block(meta_ref, shard, half) for shard in range(GROUP) for half in range(2)]
    w_out = jnp.concatenate([w_ref[side, place, OUT_AT : OUT_AT + HALF, :] for side, place in blocks], axis=0)
    attn = mm(ctx, w_out)

    def norm(values):
        center = values - jnp.mean(values, axis=1, keepdims=True)
        inverse = lax.rsqrt(jnp.mean(center * center, axis=1, keepdims=True) + EPSILON)
        return center * inverse, inverse

    def norm_back(upstream, normed, inverse, gain):
        scaled = upstream * gain
        plain = jnp.mean(scaled, axis=1, keepdims=True)
        cross = jnp.mean(scaled * normed, axis=1, keepdims=True)
        return inverse * (scaled - plain - normed * cross)

    def total(values):
        return jnp.sum(values, axis=0, keepdims=True)

    normed_one, inverse_one = norm(token + attn)
    hidden_one = normed_one * gain_one + bias_one
    low_ref[...] = hidden_one.astype(LOW)

    def columns(c):
        return pl.ds(pl.multiple_of(c * D, D), D)

    def outer_rows(c):
        halves = [second_block(meta_ref, c, half) for half in range(2)]
        return jnp.concatenate([w_ref[side, place, 0 : D // 2, :] for side, place in halves], axis=0)

    def inner_columns(c):
        return jnp.concatenate([in_ref[side, place, :, columns(c)] for side, place in blocks], axis=0)

    def forward_step(c, ffn):
        inner = mm(low_ref[...], inner_columns(c))
        cumulative = 0.5 * (1.0 + lax.erf(inner * 0.5**0.5))
        density = jnp.exp(-0.5 * inner * inner) * 0.3989422804014327
        act = (inner * cumulative).astype(LOW)
        act_ref[c] = act
        slope_ref[c] = cumulative + inner * density
        return ffn + mm(act, outer_rows(c))

    ffn = lax.fori_loop(0, GROUP, forward_step, jnp.zeros((ROWS, D), F32))
    normed_two, inverse_two = norm(hidden_one + ffn)
    layer = (normed_two * gain_two + bias_two) * mask
    out_ref[...] = layer.astype(LOW)
    squares = [token * token * mask, attn * attn * mask, ffn * ffn * mask, layer * layer]
    sums = [jnp.sum(total(s), axis=1, keepdims=True) for s in squares]
    grad_y = up_ref[...].reshape(ROWS, D).astype(F32) * mask
    grad_gain_two = total(grad_y * normed_two)
    grad_bias_two = total(grad_y)
    grad_two = norm_back(grad_y, normed_two, inverse_two, gain_two)
    grad_ffn = grad_two.astype(LOW)

    def back_step(c, grad_hidden):
        grad_act = mm_nt(grad_ffn, outer_rows(c))
        grad_inner = (grad_act * slope_ref[c]).astype(LOW)
        keep, send = select_halves(meta_ref, mm_tn(act_ref[c], grad_ffn))
        for quarter in range(3):
            rows = slice(quarter * QUARTER, (quarter + 1) * QUARTER)
            put_outer(c, quarter, keep[rows], send[rows], 0)
        grad_w = mm_tn(low_ref[...], grad_inner)
        for s in range(GROUP):
            put_inner(s, c, *select_halves(meta_ref, grad_w[s * PIECE : (s + 1) * PIECE]))
        return grad_hidden + mm_nt(grad_inner, inner_columns(c))

    grad_hidden = lax.fori_loop(0, GROUP, back_step, grad_two)
    grad_gain_one = total(grad_hidden * normed_one)
    grad_bias_one = total(grad_hidden)
    grad_one = norm_back(grad_hidden, normed_one, inverse_one, gain_one)
    gres_ref[...] = grad_one
    grad_attn = grad_one.astype(LOW)
    grad_out = mm_tn(ctx, grad_attn)
    for s in range(GROUP):
        put_outer(s, 3, *select_halves(meta_ref, grad_out[s * PIECE : (s + 1) * PIECE]), 0)
    gctx_ref[...] = mm_nt(grad_attn, w_out).astype(LOW)
    lane = iota((1, D), 1)
    stats = jnp.zeros((1, D), F32)
    for i, value in enumerate(sums):
        stats = jnp.where(lane == i, value, stats)
    low = stats - stats.astype(LOW).astype(F32)
    zeros = jnp.zeros((1, D), F32)
    norm_rows = (grad_gain_one, grad_bias_one, grad_gain_two, grad_bias_two)
    for s in range(GROUP):
        row = jnp.concatenate([r[:, s * PIECE : (s + 1) * PIECE] for r in norm_rows], axis=1)
        block = jnp.concatenate([row] + [zeros] * 31 + [stats, low] + [zeros] * 30, axis=0)
        put_outer(s, 3, *select_halves(meta_ref, block), HALF)


def feed(meta, tok, ctx_one, ctx_two, rows, own, pieces):
    shape = jax.ShapeDtypeStruct
    full, anywhere = pl.BlockSpec(memory_space=pltpu.VMEM), pl.BlockSpec(memory_space=pltpu.HBM)
    block, wide = shape((GROUP, GROUP, QUARTER, D), LOW), shape((GROUP, GROUP, HALF, D), LOW)
    return pl.pallas_call(
        feed_body,
        out_shape=(
            shape((ROWS, D), LOW), shape((ROWS, D), LOW), shape((ROWS, D), F32), block, block, wide, wide
        ),
        in_specs=[pl.BlockSpec(memory_space=pltpu.SMEM)] + [full] * 3 + [anywhere] * 15,
        out_specs=(full,) * 7,
        scratch_shapes=[
            pltpu.VMEM((GROUP, PART, D), LOW), pltpu.VMEM((ROWS, D), LOW), pltpu.VMEM((GROUP, ROWS, D), LOW),
            pltpu.VMEM((GROUP, ROWS, D), F32), pltpu.VMEM((2, GROUP, SECOND, D), LOW),
            pltpu.VMEM((2, GROUP, HALF, WIDE), LOW), pltpu.SemaphoreType.DMA((24,)),
        ],
        compiler_params=pltpu.CompilerParams(vmem_limit_bytes=28 * MIB),
        cost_estimate=pl.CostEstimate(flops=16_000_000_000, bytes_accessed=60_000_000, transcendentals=1_600_000),
        name="feed",
    )(meta, tok, ctx_one, ctx_two, rows, *own, *pieces)


def finish_body(
    meta_ref, mine, other, rows_ref,
    q_ref, k_ref, v_ref, rel_ref, outer_ref, wout_ref, inner_ref, g1_ref, b1_ref, g2_ref, b2_ref, rms_ref,
    out_ref, gtok_ref, extra_ref,
):
    for piece, side in ((mine, 0), (other, 1)):
        core = meta_ref[CORE] if side == 0 else 1 - meta_ref[CORE]
        assist = assist_of(meta_ref, core)
        for i, ref in enumerate((q_ref, k_ref, v_ref, rel_ref)):
            size = REL_HALF if i == 3 else HALF
            ref[pl.ds(pl.multiple_of(core * size, size), size), :] = piece[i * HALF : i * HALF + size, :].astype(F32)

        def piece_step(distance, carry):
            quarter = assist ^ distance
            at = pl.multiple_of(FIRST + distance * SPAN, HALF // 3)
            block = piece[pl.ds(at, QUARTER), :].astype(F32)

            @pl.when(quarter < 3)
            def _():
                outer_ref[pl.ds(pl.multiple_of(core * 3 * QUARTER + quarter * QUARTER, QUARTER), QUARTER), :] = block

            @pl.when(quarter == 3)
            def _():
                wout_ref[pl.ds(pl.multiple_of(core * HALF, HALF), HALF), :] = block[:HALF]
                extra_ref[core] = block[HALF:]

            inner_ref[
                pl.ds(pl.multiple_of(core * HALF, HALF), HALF), pl.ds(pl.multiple_of(quarter * D, D), D)
            ] = piece[pl.ds(at + QUARTER, HALF), :].astype(F32)
            return carry

        lax.fori_loop(0, GROUP, piece_step, 0)
    norms = extra_ref[0, 0:1, :]
    for i, ref in enumerate((g1_ref, b1_ref, g2_ref, b2_ref)):
        ref[...] = norms[:, i * PIECE : (i + 1) * PIECE]
    stats = extra_ref[1, 0:1, :] + extra_ref[1, 1:2, :]
    rms_ref[...] = jnp.sqrt(stats[:, :GROUP] * (1.0 / (TOKENS * D)))
    for k in range(GROUP):
        member = meta_ref[X] ^ k
        out_ref[meta_ref[SEQ + k]] = rows_ref[member, 0]
        gtok_ref[meta_ref[SEQ + k]] = rows_ref[member, 1]


def finish(meta, mine, other, rows):
    shape = jax.ShapeDtypeStruct
    full = pl.BlockSpec(memory_space=pltpu.VMEM)
    return pl.pallas_call(
        finish_body,
        out_shape=(
            *(shape((PIECE, D), F32),) * 3, shape((OFFS // GROUP, D), F32),
            shape((D, D), F32), shape((PIECE, D), F32), shape((PIECE, WIDE), F32),
            *(shape((1, PIECE), F32),) * 4, shape((1, GROUP), F32),
            *(shape((GROUP, PART, D), LOW),) * 2,
        ),
        in_specs=[pl.BlockSpec(memory_space=pltpu.SMEM)] + [full] * 3,
        out_specs=(full,) * 14,
        scratch_shapes=[pltpu.VMEM((2, QUARTER - HALF, D), F32)],
        compiler_params=pltpu.CompilerParams(vmem_limit_bytes=24 * MIB),
        name="finish",
    )(meta, mine, other, rows)


NEAR, FAR = (1, 3), (3, 1)


def hop_x(value, flips):
    pairs = [(c * 4 + i, c * 4 + (i ^ flips[c])) for c in range(2) for i in range(4)]
    return lax.ppermute(value, ("core", "shard"), pairs)


def hop_yz(value, flip, swapped=False):
    pairs = []
    for y in range(4):
        for z in range(4):
            for c in range(2):
                along_y = (c == 0) != swapped
                ty, tz = (y ^ flip, z) if along_y else (y, z ^ flip)
                pairs.append(((y * 4 + z) * 2 + c, (ty * 4 + tz) * 2 + c))
    return lax.ppermute(value, ("y", "z", "core"), pairs)


def swap(value):
    return lax.ppermute(value, "core", [(0, 1), (1, 0)])


def after(value, *others):
    return lax.optimization_barrier((value, *others))[0]


def add(*values):
    total = values[0].astype(F32)
    for value in values[1:]:
        total = total + value.astype(F32)
    return total.astype(LOW)


def exchange_rows(rows):
    return lax.all_to_all(rows, "shard", split_axis=0, concat_axis=0, tiled=True)


def shards(
    hidden, grad_out, lengths, bucket, w_query, w_key, w_value, w_out, w_inner, w_outer, rel_table,
    ln1_gain, ln1_bias, ln2_gain, ln2_bias,
):
    coords = jnp.stack([lax.axis_index(name) for name in ("shard", "y", "z", "core")]).astype(jnp.int32)
    norm_block = jnp.concatenate(
        [jnp.concatenate([ln1_gain, ln1_bias, ln2_gain, ln2_bias])[None], jnp.zeros((31, D), LOW)], axis=0
    )
    bucket_column = jnp.concatenate([bucket[::-1], jnp.full((1,), -1, jnp.int32)])[:, None]
    own_first = (w_query, w_key, w_value, rel_table)
    own_halves = tuple(
        pltpu.with_memory_space_constraint(ref.reshape(2, ref.shape[0] // 2, D), pltpu.HBM) for ref in own_first
    )
    meta, first, second, rows = pack(
        coords, lengths, hidden, grad_out, own_first, (w_outer, w_out, w_inner), norm_block
    )
    near_two, far_two = hop_x(second, NEAR), hop_x(second, FAR)
    near, far = hop_x(first, NEAR), hop_x(first, FAR)
    rows = exchange_rows(rows)
    across_two = hop_x(near_two, FAR)
    base = after(jnp.stack([near_two, far_two, across_two]), near, far)
    base_near, base_far = hop_yz(base, 1), hop_yz(base, 3)
    across = hop_x(near, FAR)
    pieces = (near, far, across, swap(near), swap(far), swap(across))
    part_outer, part_inner = base_near[:, :QUARTER], base_far[:, QUARTER:]
    rows = after(rows, part_outer, part_inner)
    across_outer, across_inner = hop_yz(part_outer, 3), hop_yz(part_inner, 1)
    tok, *saved, relw, probs, ctx = attend_forward(meta, bucket_column, rows, own_halves, pieces)
    across_outer, across_inner, base, base_near, base_far, _ = lax.optimization_barrier(
        (across_outer, across_inner, base, base_near, base_far, ctx)
    )
    arrived = (base, base_near, base_far, across_outer, across_inner)
    swapped = tuple(swap(piece) for piece in arrived)
    probs_two, ctx_two = attend_forward_two(meta, saved)
    swapped = after(swapped, ctx_two)
    out, gctx, gres, keep, send, keep_in, send_in = feed(
        meta, tok, ctx, ctx_two, rows, (w_outer, w_out, norm_block, w_inner), (*arrived, *swapped)
    )
    other, other_in = swap(send), swap(send_in)
    half_done = attend_back_one((*saved, probs), gctx)
    leave = add(keep[:2], other[:2])
    leave_in = add(keep_in[:2], other_in[:2])
    came, came_in = hop_yz(leave, 1), hop_yz(leave_in, 3)
    half_done = after(tuple(half_done), leave, leave_in)
    leaving, keep_one, send_one = attend_back_two(
        meta, (*saved, probs_two), gctx, half_done, tok, relw, gres, bucket_column, own_halves, pieces, out
    )
    other_one = swap(after(send_one, came, came_in))
    leave_one = add(keep_one[:2], other_one[:2])
    came, came_in = after((came, came_in), leave_one)
    last = hop_yz(add(keep[2], other[2], came[0]), 3)
    last_in = hop_yz(add(keep_in[2], other_in[2], came_in[0]), 1)
    came_one = hop_x(leave_one, NEAR)
    came_one = after(came_one, last, last_in)
    leave_two = add(keep_one[2], other_one[2], came_one[0])
    last_one = hop_x(leave_two, FAR)
    last, last_in, _ = lax.optimization_barrier((last, last_in, leave_two))
    mine = add(keep[3], other[3], came[1], last)
    mine_in = add(keep_in[3], other_in[3], came_in[1], last_in)
    both = jnp.concatenate([mine, mine_in], axis=1)
    came_x = hop_x(both[:2], NEAR)
    home = exchange_rows(leaving)
    mine_one = add(keep_one[3], other_one[3], came_one[1], last_one)
    come_one = hop_yz(mine_one, 1, swapped=True)
    last_x = hop_x(after(add(both[2], came_x[0]), mine_one), FAR)
    mine_one = add(mine_one, after(come_one, last_x))
    come_one = hop_yz(mine_one, 3, swapped=True)
    both = after(add(both[3], came_x[1], last_x), mine_one)
    step = hop_yz(both, 1, swapped=True)
    mine_one = add(mine_one, after(come_one, step))
    come_one = hop_yz(mine_one, 1)
    both = after(add(both, step), mine_one)
    step = hop_yz(both, 3, swapped=True)
    mine_one = add(mine_one, after(come_one, step))
    come_one = hop_yz(mine_one, 3)
    both = after(add(both, step), mine_one)
    both = [both, *(hop_yz(both, flip) for flip in (1, 3, 2))]
    both[1], both[2], both[3] = both[1], both[3], both[2]
    mine_one = add(mine_one, come_one)
    packed = after(jnp.concatenate([mine_one, *both], axis=0), home)
    q_grad, k_grad, v_grad, rel_grad, outer_grad, out_grad, inner_grad, *small, layer_output, grad_hidden = finish(
        meta, packed, swap(packed), home
    )
    return (
        layer_output, grad_hidden, q_grad, k_grad, v_grad, out_grad, inner_grad, outer_grad, rel_grad,
        *(row[0] for row in small),
    )


def solution(mesh):
    split = Mesh(mesh.devices.reshape(4, 4, 2, 4), ("y", "z", "core", "shard"))
    rep = ("y", "z", "core")
    rows, vector = P("shard", None), P("shard")
    batch = P(rep, "shard", None)
    return jax.shard_map(
        shards,
        mesh=split,
        in_specs=(batch, batch, P(rep), P(), *(rows,) * 7, *(vector,) * 4),
        out_specs=(batch, batch, *(rows,) * 7, *(vector,) * 4, P()),
        check_vma=False,
    )
```

```python
import jax
import jax.numpy as jnp
from jax import lax
from jax.experimental import pallas as pl
from jax.experimental.pallas import tpu as pltpu
from jax.sharding import Mesh
from jax.sharding import PartitionSpec as P

D = 768
HEADS = 12
HEAD_DIM = 64
PAIRS = HEADS // 2
ROWS = 256
OFFS = 512
TOKENS = 20480
GROUP = 4
PIECE = D // GROUP
HALF = PIECE // 2
WIDE = GROUP * D
REL_HALF = OFFS // GROUP // 2
REL_AT = 3 * HALF
FIRST = 3 * HALF + REL_HALF
OUT_AT = D // 2
NORM_AT = D // 2 + HALF
QUARTER = 128
SECOND = GROUP * QUARTER
SPAN = QUARTER + HALF
PART = ROWS // GROUP
X, Y, Z, CORE, LENGTH, SEQ = 0, 1, 2, 3, 4, 5
META = 16
EPSILON = 1e-07
MASKED = -1e30
SCALING = (3.0 * HEAD_DIM) ** (-0.5)
F32 = jnp.float32
LOW = jnp.bfloat16
MIB = 1024 * 1024


def mm(a, b):
    return lax.dot_general(a, b, (((1,), (0,)), ((), ())), preferred_element_type=F32)


def mm_nt(a, b):
    return lax.dot_general(a, b, (((1,), (1,)), ((), ())), preferred_element_type=F32)


def mm_tn(a, b):
    return lax.dot_general(a, b, (((0,), (0,)), ((), ())), preferred_element_type=F32)


def iota(shape, dim):
    return lax.broadcasted_iota(jnp.int32, shape, dim)


def whole(ref, start, size):
    piece = ref[:, :, start : start + size, :]
    return piece.reshape(GROUP * 2 * size, piece.shape[3])


def run_copies(copies):
    for copy in copies:
        copy.start()
    for copy in copies:
        copy.wait()


class Copies:
    def __init__(self, sem):
        self.sem, self.made = sem, []

    def add(self, source, target):
        self.made.append(pltpu.make_async_copy(source, target, self.sem.at[len(self.made)]))

    def start(self):
        for copy in self.made:
            copy.start()

    def wait(self):
        for copy in self.made:
            copy.wait()


def near_of(core):
    return 1 + 2 * core


def far_of(core):
    return 3 - 2 * core


def assist_of(meta_ref, core):
    return jnp.where(core == 0, meta_ref[Y], meta_ref[Z])


def position(distance, near):
    far = 4 - near
    place = jnp.where(distance == near, 1, jnp.where(distance == far, 2, 0))
    return jnp.where(distance == 0, 3, place)


def pack_body(
    coord_ref, length_ref, hidden_ref, grad_ref, own_q, own_k, own_v, own_rel, own_outer, own_out, own_inner, norm_ref,
    meta_ref, first_ref, second_ref, *rest,
):
    rows_out, sem, tail_sem = rest
    x, y, z, core = (coord_ref[i] for i in range(4))
    for i in range(4):
        meta_ref[i] = coord_ref[i]
    lengths = [length_ref[i] for i in range(GROUP)]
    dealing = []
    for i in range(GROUP):
        rank = jnp.int32(0)
        for j in range(GROUP):
            if j != i:
                ahead = lengths[j] >= lengths[i] if j < i else lengths[j] > lengths[i]
                rank = rank + ahead.astype(jnp.int32)
        dealing.append(rank)
    length = jnp.int32(0)
    for i in range(GROUP):
        length = length + jnp.where(dealing[i] == x, lengths[i], 0)
    meta_ref[LENGTH] = length
    copies = Copies(sem)
    for k in range(GROUP):
        source = jnp.int32(0)
        for i in range(GROUP):
            source = source + jnp.where(dealing[i] == (x ^ k), i, 0)
        meta_ref[SEQ + k] = source
        copies.add(hidden_ref.at[source], rows_out.at[x ^ k, 0])
        copies.add(grad_ref.at[source], rows_out.at[x ^ k, 1])
    for i in range(SEQ + GROUP, META):
        meta_ref[i] = jnp.int32(0)
    for i, ref in enumerate((own_q, own_k, own_v, own_rel)):
        size = REL_HALF if i == 3 else HALF
        copies.add(ref.at[pl.ds(core * size, size)], first_ref.at[pl.ds(i * HALF, size)])
    quarter = jnp.where(core == 0, y, z)
    copies.add(
        own_inner.at[pl.ds(core * HALF, HALF), pl.ds(pl.multiple_of(quarter * D, D), D)],
        second_ref.at[pl.ds(QUARTER, HALF)],
    )
    copies.start()
    tail = Copies(tail_sem)

    @pl.when(quarter < 3)
    def _():
        copy = pltpu.make_async_copy(
            own_outer.at[pl.ds(core * 3 * QUARTER + quarter * QUARTER, QUARTER)], second_ref.at[pl.ds(0, QUARTER)],
            tail_sem.at[0],
        )
        copy.start()
        copy.wait()

    @pl.when(quarter == 3)
    def _():
        tail.add(own_out.at[pl.ds(core * HALF, HALF)], second_ref.at[pl.ds(0, HALF)])
        tail.add(norm_ref, second_ref.at[pl.ds(HALF, QUARTER - HALF)])
        tail.start()
        tail.wait()

    copies.wait()


def pack(coords, lengths, hidden, grad_out, own_first, own_second, norm_block):
    shape = jax.ShapeDtypeStruct
    scalars, anywhere = pl.BlockSpec(memory_space=pltpu.SMEM), pl.BlockSpec(memory_space=pltpu.HBM)
    full = pl.BlockSpec(memory_space=pltpu.VMEM)
    return pl.pallas_call(
        pack_body,
        out_shape=(
            shape((META,), jnp.int32), shape((FIRST, D), LOW), shape((SPAN, D), LOW), shape((GROUP, 2, PART, D), LOW),
        ),
        in_specs=[scalars, scalars] + [anywhere] * 10,
        out_specs=(scalars, full, full, full),
        scratch_shapes=[pltpu.SemaphoreType.DMA((13,)), pltpu.SemaphoreType.DMA((2,))],
        compiler_params=pltpu.CompilerParams(vmem_limit_bytes=60 * MIB),
        name="pack",
    )(coords, lengths, hidden, grad_out, *own_first, *own_second, norm_block)


def cut_body(near_ref, far_ref, outer_ref, inner_ref, sem):
    copies = Copies(sem)
    copies.add(near_ref.at[:, pl.ds(0, QUARTER)], outer_ref)
    copies.add(far_ref.at[:, pl.ds(QUARTER, HALF)], inner_ref)
    copies.start()
    copies.wait()


def cut(near, far):
    shape = jax.ShapeDtypeStruct
    full, anywhere = pl.BlockSpec(memory_space=pltpu.VMEM), pl.BlockSpec(memory_space=pl.ANY)
    return pl.pallas_call(
        cut_body,
        out_shape=(shape((3, QUARTER, D), LOW), shape((3, HALF, D), LOW)),
        in_specs=[anywhere] * 2,
        out_specs=(full, full),
        scratch_shapes=[pltpu.SemaphoreType.DMA((2,))],
        compiler_params=pltpu.CompilerParams(vmem_limit_bytes=4 * MIB),
        name="cut",
    )(near, far)


def load_first(meta_ref, copies, own, pieces, w_ref):
    x, core = meta_ref[X], meta_ref[CORE]
    near, far = x ^ near_of(core), x ^ far_of(core)
    slots = ((near, core), (far, core), (x ^ 2, core), (far, 1 - core), (near, 1 - core), (x ^ 2, 1 - core))
    for piece, (slot, half) in zip(pieces, slots):
        copies.add(piece, w_ref.at[slot, half])
    for i, ref in enumerate(own):
        size = REL_HALF if i == 3 else HALF
        copies.add(ref, w_ref.at[x, :, pl.ds(i * HALF, size)])


def load_second(meta_ref, copies, own, pieces, w_ref, in_ref):
    own_outer, own_out, own_norm, own_inner = own
    for side in range(2):
        assist = assist_of(meta_ref, meta_ref[CORE] if side == 0 else 1 - meta_ref[CORE])
        base, near, far, across_outer, across_inner = pieces[5 * side : 5 * side + 5]
        for distance, outer, inner in (
            (0, base.at[:, pl.ds(0, QUARTER)], base.at[:, pl.ds(QUARTER, HALF)]),
            (1, near.at[:, pl.ds(0, QUARTER)], near.at[:, pl.ds(QUARTER, HALF)]),
            (3, far.at[:, pl.ds(0, QUARTER)], far.at[:, pl.ds(QUARTER, HALF)]),
            (2, across_outer, across_inner),
        ):
            quarter = assist ^ distance
            copies.add(outer, w_ref.at[side, pl.ds(0, 3), pl.ds(quarter * QUARTER, QUARTER)])
            copies.add(inner, in_ref.at[side, pl.ds(0, 3), :, pl.ds(pl.multiple_of(quarter * D, D), D)])
    for half in range(2):
        side = half ^ meta_ref[CORE]
        copies.add(own_outer.at[pl.ds(half * 3 * QUARTER, 3 * QUARTER)], w_ref.at[side, 3, pl.ds(0, 3 * QUARTER)])
        copies.add(own_out.at[pl.ds(half * HALF, HALF)], w_ref.at[side, 3, pl.ds(OUT_AT, HALF)])
        copies.add(own_inner.at[pl.ds(half * HALF, HALF)], in_ref.at[side, 3])
    copies.add(own_norm, w_ref.at[meta_ref[CORE], 3, pl.ds(NORM_AT, QUARTER - HALF)])


def second_block(meta_ref, shard, half):
    apart = meta_ref[X] ^ shard
    place = jnp.where(apart == near_of(half), 0, jnp.where(apart == far_of(half), 1, 2))
    return half ^ meta_ref[CORE], jnp.where(apart == 0, 3, place)


def select_halves(meta_ref, value):
    half = value.shape[0] // 2
    low, high = value[:half].astype(LOW), value[half:].astype(LOW)
    first_core = meta_ref[CORE] == 0
    return jnp.where(first_core, low, high), jnp.where(first_core, high, low)


def heads_forward(meta_ref, first_pair, refs, probs_ref, ctx_ref):
    q_ref, k_ref, v_ref, pk_ref, pq_ref = refs
    length = meta_ref[LENGTH]
    valid = iota((ROWS, ROWS), 1) < length
    side = iota((ROWS, 2 * HEAD_DIM), 1) // HEAD_DIM

    def pair_step(pair, carry):
        out_cols = pl.ds(pl.multiple_of((pair - first_pair) * 2 * HEAD_DIM, 2 * HEAD_DIM), 2 * HEAD_DIM)
        cols = pl.ds(pl.multiple_of(pair * 2 * HEAD_DIM, 2 * HEAD_DIM), 2 * HEAD_DIM)
        q_pair, k_pair, v_pair = q_ref[:, cols], k_ref[:, cols], v_ref[:, cols]
        pk_pair, pq_pair = pk_ref[:, cols], pq_ref[:, cols]
        zero = jnp.zeros_like(q_pair)
        contexts = []
        for h in range(2):
            mine = side == h
            q_head = jnp.where(mine, q_pair, zero)
            k_head = jnp.where(mine, k_pair, zero)
            content = mm_nt(q_head, k_pair)
            to_off = mm_nt(q_head, pk_pair)
            from_off = mm_nt(k_head, pq_pair)
            to_rel = pltpu.roll(to_off, ROWS + 1, 1, stride=1, stride_axis=0)[:, :ROWS]
            from_rel = pltpu.roll(from_off, ROWS + 1, 1, stride=1, stride_axis=0)[:, :ROWS]
            scores = (content + to_rel + from_rel.T) * SCALING
            scores = jnp.where(valid, scores, MASKED)
            top = jnp.max(scores, axis=1, keepdims=True)
            shifted = jnp.exp(scores - top)
            summed = jnp.sum(shifted, axis=1, keepdims=True)
            probs = (shifted * (1.0 / summed)).astype(LOW)
            probs_ref[2 * (pair - first_pair) + h] = probs
            contexts.append(mm(probs, v_pair))
        ctx_ref[:, out_cols] = jnp.where(side == 0, contexts[0], contexts[1]).astype(LOW)
        return carry

    lax.fori_loop(first_pair, first_pair + PAIRS // 2, pair_step, 0)


def attend_forward_body(
    meta_ref, bucket_ref, rows_ref, own_q, own_k, own_v, own_rel, p0, p1, p2, p3, p4, p5,
    tok_ref, q_ref, k_ref, v_ref, pk_ref, pq_ref, relw_ref, probs_ref, ctx_ref,
    w_ref, rows_in, sem,
):
    copies = Copies(sem)
    copies.add(rows_ref.at[:, 0], rows_in)
    load_first(meta_ref, copies, (own_q, own_k, own_v, own_rel), (p0, p1, p2, p3, p4, p5), w_ref)
    copies.start()
    copies.wait()
    tok = rows_in[...].reshape(ROWS, D)
    tok_ref[...] = tok
    rel = whole(w_ref, REL_AT, REL_HALF)
    pick = (bucket_ref[...] == iota((OFFS, OFFS), 1)).astype(LOW)
    relw = mm(pick, rel).astype(LOW)
    relw_ref[...] = relw
    w_query = whole(w_ref, 0, HALF)
    q_ref[...] = mm(tok, w_query).astype(LOW)
    pq_ref[...] = mm(relw, w_query).astype(LOW)
    w_key = whole(w_ref, HALF, HALF)
    k_ref[...] = mm(tok, w_key).astype(LOW)
    pk_ref[...] = mm(relw, w_key).astype(LOW)
    v_ref[...] = mm(tok, whole(w_ref, 2 * HALF, HALF)).astype(LOW)
    heads_forward(meta_ref, 0, (q_ref, k_ref, v_ref, pk_ref, pq_ref), probs_ref, ctx_ref)


def attend_forward_two_body(meta_ref, q_ref, k_ref, v_ref, pk_ref, pq_ref, probs_ref, ctx_ref):
    heads_forward(meta_ref, PAIRS // 2, (q_ref, k_ref, v_ref, pk_ref, pq_ref), probs_ref, ctx_ref)


def attend_forward(meta, bucket_column, rows, own, pieces):
    shape = jax.ShapeDtypeStruct
    full, anywhere = pl.BlockSpec(memory_space=pltpu.VMEM), pl.BlockSpec(memory_space=pltpu.HBM)
    return pl.pallas_call(
        attend_forward_body,
        out_shape=(
            *(shape((ROWS, D), LOW),) * 4,
            shape((OFFS, D), LOW), shape((OFFS, D), LOW), shape((OFFS, D), LOW),
            shape((HEADS // 2, ROWS, ROWS), LOW), shape((ROWS, D // 2), LOW),
        ),
        in_specs=[pl.BlockSpec(memory_space=pltpu.SMEM), full] + [anywhere] * 11,
        out_specs=(full,) * 9,
        scratch_shapes=[
            pltpu.VMEM((GROUP, 2, FIRST, D), LOW), pltpu.VMEM((GROUP, PART, D), LOW), pltpu.SemaphoreType.DMA((11,)),
        ],
        compiler_params=pltpu.CompilerParams(vmem_limit_bytes=28 * MIB),
        cost_estimate=pl.CostEstimate(flops=12_000_000_000, bytes_accessed=40_000_000, transcendentals=800_000),
        name="attend_forward",
    )(meta, bucket_column, rows, *own, *pieces)


def attend_forward_two(meta, saved):
    shape = jax.ShapeDtypeStruct
    full = pl.BlockSpec(memory_space=pltpu.VMEM)
    return pl.pallas_call(
        attend_forward_two_body,
        out_shape=(shape((HEADS // 2, ROWS, ROWS), LOW), shape((ROWS, D // 2), LOW)),
        in_specs=[pl.BlockSpec(memory_space=pltpu.SMEM)] + [full] * 5,
        out_specs=(full,) * 2,
        compiler_params=pltpu.CompilerParams(vmem_limit_bytes=24 * MIB),
        cost_estimate=pl.CostEstimate(flops=8_000_000_000, bytes_accessed=20_000_000, transcendentals=400_000),
        name="attend_forward_two",
    )(meta, *saved)


def both_heads(pair, side):
    zero = jnp.zeros_like(pair)
    return jnp.concatenate([jnp.where(side == h, pair, zero) for h in range(2)], axis=0)


def heads_back(first_pair, count, refs, outs):
    q_ref, k_ref, v_ref, pk_ref, pq_ref, probs_ref, gctx_ref = refs
    gq_ref, gk_ref, gv_ref, gpk_ref, gpq_ref, qr_ref, kr_ref = outs
    flip = (iota((ROWS, ROWS), 0) + iota((ROWS, ROWS), 1) == ROWS - 1).astype(LOW)
    qr_ref[...] = mm(flip, q_ref[...]).astype(LOW)
    kr_ref[...] = mm(flip, k_ref[...]).astype(LOW)
    side = iota((ROWS, 2 * HEAD_DIM), 1) // HEAD_DIM
    side_off = iota((OFFS, 2 * HEAD_DIM), 1) // HEAD_DIM
    blank = jnp.zeros((ROWS, OFFS - ROWS), F32)

    def pair_step(pair, carry):
        cols = pl.ds(pl.multiple_of(pair * 2 * HEAD_DIM, 2 * HEAD_DIM), 2 * HEAD_DIM)
        q_pair, k_pair, v_pair = q_ref[:, cols], k_ref[:, cols], v_ref[:, cols]
        pk_pair, pq_pair, gctx_pair = pk_ref[:, cols], pq_ref[:, cols], gctx_ref[:, cols]
        qr_pair, kr_pair = qr_ref[:, cols], kr_ref[:, cols]
        grad_probs_both = mm_nt(both_heads(gctx_pair, side), v_pair)
        scores_both, probs_both = [], []
        for h in range(2):
            grad_probs = grad_probs_both[h * ROWS : (h + 1) * ROWS]
            probs_low = probs_ref[2 * (pair - first_pair) + h]
            probs = probs_low.astype(F32)
            inner = jnp.sum(probs * grad_probs, axis=1, keepdims=True)
            scores_both.append((probs * (grad_probs - inner)).astype(LOW))
            probs_both.append(probs_low)
        g_value = mm_tn(jnp.concatenate(probs_both, axis=1), gctx_pair)
        rows_both = mm(flip, jnp.concatenate(scores_both, axis=1))
        cols_both = mm_nt(flip, jnp.concatenate(scores_both, axis=0))

        def spread_out(both):
            return [
                pltpu.roll(
                    jnp.concatenate([both[:, h * ROWS : (h + 1) * ROWS], blank], axis=1), 0, 1, stride=1, stride_axis=0
                ).astype(LOW)
                for h in range(2)
            ]

        def stacked(both):
            return jnp.concatenate([both[:, :ROWS], both[:, ROWS:]], axis=0).astype(LOW)

        to_off, from_off = spread_out(rows_both), spread_out(cols_both)
        g_query = mm(stacked(rows_both), k_pair) + mm(jnp.concatenate(to_off, axis=0), pk_pair)
        g_key = mm(stacked(cols_both), q_pair) + mm(jnp.concatenate(from_off, axis=0), pq_pair)
        g_pk = mm_tn(jnp.concatenate(to_off, axis=1), qr_pair)
        g_pq = mm_tn(jnp.concatenate(from_off, axis=1), kr_pair)
        first = [grad[: grad.shape[0] // 2] for grad in (g_value, g_query, g_key, g_pk, g_pq)]
        second = [grad[grad.shape[0] // 2 :] for grad in (g_value, g_query, g_key, g_pk, g_pq)]
        gv_ref[:, cols] = jnp.where(side == 0, first[0], second[0]).astype(LOW)
        gq_ref[:, cols] = (jnp.where(side == 0, first[1], second[1]) * SCALING).astype(LOW)
        gk_ref[:, cols] = (jnp.where(side == 0, first[2], second[2]) * SCALING).astype(LOW)
        gpk_ref[:, cols] = (jnp.where(side_off == 0, first[3], second[3]) * SCALING).astype(LOW)
        gpq_ref[:, cols] = (jnp.where(side_off == 0, first[4], second[4]) * SCALING).astype(LOW)
        return carry

    lax.fori_loop(first_pair, first_pair + count, pair_step, 0)
    return flip


def attend_back_one_body(
    q_ref, k_ref, v_ref, pk_ref, pq_ref, probs_ref, gctx_ref,
    gq_ref, gk_ref, gv_ref, gpk_ref, gpq_ref, qr_ref, kr_ref,
):
    heads_back(
        0, PAIRS // 2, (q_ref, k_ref, v_ref, pk_ref, pq_ref, probs_ref, gctx_ref),
        (gq_ref, gk_ref, gv_ref, gpk_ref, gpq_ref, qr_ref, kr_ref),
    )


def attend_back_two_body(
    meta_ref, q_ref, k_ref, v_ref, pk_ref, pq_ref, probs_ref, gctx_ref, hq, hk, hv, hpk, hpq,
    tok_ref, relw_ref, gres_ref, bucket_ref,
    own_q, own_k, own_v, own_rel, p0, p1, p2, p3, p4, p5,
    out_ref,
    home_ref, keep_ref, send_ref,
    grad_ref, gv_ref, pos_ref, qr_ref, kr_ref, gtok_ref, w_ref, sem,
):
    gq_ref, gk_ref, gpq_ref, gpk_ref = grad_ref.at[0], grad_ref.at[1], pos_ref.at[0], pos_ref.at[1]
    copies = Copies(sem)
    load_first(meta_ref, copies, (own_q, own_k, own_v, own_rel), (p0, p1, p2, p3, p4, p5), w_ref)
    copies.start()
    for target, done in ((gq_ref, hq), (gk_ref, hk), (gv_ref, hv), (gpk_ref, hpk), (gpq_ref, hpq)):
        target[:, : D // 2] = done[...]
    flip = heads_back(
        PAIRS // 2, PAIRS // 2, (q_ref, k_ref, v_ref, pk_ref, pq_ref, probs_ref, gctx_ref),
        (gq_ref, gk_ref, gv_ref, gpk_ref, gpq_ref, qr_ref, kr_ref),
    )
    copies.wait()
    tok, relw = tok_ref[...], relw_ref[...]
    x, core = meta_ref[X], meta_ref[CORE]

    def put(start, size, value):
        for shard in range(GROUP):
            keep, send = select_halves(meta_ref, value[shard * 2 * size : (shard + 1) * 2 * size])
            keep_ref[position(x ^ shard, near_of(core)), pl.ds(start, size)] = keep
            send_ref[position(x ^ shard, far_of(core)), pl.ds(start, size)] = send

    def weight_step(i, carry):
        g_tok, g_rel = carry
        start = pl.multiple_of(i * HALF, HALF)
        grads = mm(flip, grad_ref[i]).astype(LOW)
        weight = w_ref[:, :, pl.ds(start, HALF), :].reshape(D, D)
        put(start, HALF, mm_tn(tok, grads) + mm_tn(relw, pos_ref[i]))
        return g_tok + mm_nt(grads, weight), g_rel + mm_nt(pos_ref[i], weight)

    g_tok, g_rel = lax.fori_loop(0, 2, weight_step, (gres_ref[...], jnp.zeros((OFFS, D), F32)))
    g_value = gv_ref[...]
    gtok_ref[...] = (g_tok + mm_nt(g_value, whole(w_ref, 2 * HALF, HALF))).astype(LOW)
    put(2 * HALF, HALF, mm_tn(tok, g_value))
    pick = (bucket_ref[...] == iota((OFFS, OFFS), 1)).astype(LOW)
    put(REL_AT, REL_HALF, mm_tn(pick, g_rel.astype(LOW)))
    for member in range(GROUP):
        home_ref[member, 0] = out_ref[member * PART : (member + 1) * PART, :]
        home_ref[member, 1] = gtok_ref[member * PART : (member + 1) * PART, :]


def attend_back_one(saved, gctx):
    shape = jax.ShapeDtypeStruct
    full = pl.BlockSpec(memory_space=pltpu.VMEM)
    return pl.pallas_call(
        attend_back_one_body,
        out_shape=(*(shape((ROWS, D // 2), LOW),) * 3, *(shape((OFFS, D // 2), LOW),) * 2),
        in_specs=[full] * 7,
        out_specs=(full,) * 5,
        scratch_shapes=[pltpu.VMEM((ROWS, D), LOW), pltpu.VMEM((ROWS, D), LOW)],
        compiler_params=pltpu.CompilerParams(vmem_limit_bytes=24 * MIB),
        cost_estimate=pl.CostEstimate(flops=8_000_000_000, bytes_accessed=20_000_000, transcendentals=0),
        name="attend_back_one",
    )(*saved, gctx)


def attend_back_two(meta, saved, gctx, half_done, tok, relw, gres, bucket_column, own, pieces, out):
    shape = jax.ShapeDtypeStruct
    full, anywhere = pl.BlockSpec(memory_space=pltpu.VMEM), pl.BlockSpec(memory_space=pltpu.HBM)
    return pl.pallas_call(
        attend_back_two_body,
        out_shape=(shape((GROUP, 2, PART, D), LOW), shape((GROUP, FIRST, D), LOW), shape((GROUP, FIRST, D), LOW)),
        in_specs=[pl.BlockSpec(memory_space=pltpu.SMEM)] + [full] * 16 + [anywhere] * 10 + [full],
        out_specs=(full,) * 3,
        scratch_shapes=[
            pltpu.VMEM((2, ROWS, D), LOW), pltpu.VMEM((ROWS, D), LOW), pltpu.VMEM((2, OFFS, D), LOW),
            *(pltpu.VMEM((ROWS, D), LOW),) * 3,
            pltpu.VMEM((GROUP, 2, FIRST, D), LOW), pltpu.SemaphoreType.DMA((10,)),
        ],
        compiler_params=pltpu.CompilerParams(vmem_limit_bytes=22 * MIB),
        cost_estimate=pl.CostEstimate(flops=14_000_000_000, bytes_accessed=40_000_000, transcendentals=0),
        name="attend_back_two",
    )(meta, *saved, gctx, *half_done, tok, relw, gres, bucket_column, *own, *pieces, out)


def feed_body(
    meta_ref, tok_ref, ctx_one_ref, ctx_two_ref, rows_ref, own_outer, own_out, own_norm, own_inner, *rest,
):
    pieces, rest = rest[:10], rest[10:]
    out_ref, gctx_ref, gres_ref, keep_ref, send_ref, keep_in_ref, send_in_ref = rest[:7]
    up_ref, low_ref, act_ref, slope_ref, w_ref, in_ref, sem = rest[7:]
    copies = Copies(sem)
    copies.add(rows_ref.at[:, 1], up_ref)
    load_second(meta_ref, copies, (own_outer, own_out, own_norm, own_inner), pieces, w_ref, in_ref)
    copies.start()
    copies.wait()
    x, core = meta_ref[X], meta_ref[CORE]
    assist, assist_peer = assist_of(meta_ref, core), assist_of(meta_ref, 1 - core)

    def put_outer(shard, quarter, keep, send, start):
        rows = slice(start, start + keep.shape[0])
        keep_ref[position(assist ^ quarter, 1), position(x ^ shard, near_of(core)), rows] = keep
        send_ref[position(assist_peer ^ quarter, 1), position(x ^ shard, far_of(core)), rows] = send

    def put_inner(shard, quarter, keep, send):
        keep_in_ref[position(assist ^ quarter, 3), position(x ^ shard, near_of(core))] = keep
        send_in_ref[position(assist_peer ^ quarter, 3), position(x ^ shard, far_of(core))] = send

    length = meta_ref[LENGTH]
    mask = (iota((ROWS, 1), 0) < length).astype(F32)
    norm_rows = []
    for s in range(GROUP):
        side, place = second_block(meta_ref, s, 0)
        norm_rows.append(w_ref[side, place, NORM_AT : NORM_AT + QUARTER - HALF, :].astype(F32)[:1])
    gain_one, bias_one, gain_two, bias_two = (
        jnp.concatenate([row[:, i * PIECE : (i + 1) * PIECE] for row in norm_rows], axis=1) for i in range(4)
    )
    token = tok_ref[...].astype(F32)
    ctx = jnp.concatenate([ctx_one_ref[...], ctx_two_ref[...]], axis=1)
    blocks = [second_block(meta_ref, shard, half) for shard in range(GROUP) for half in range(2)]
    w_out = jnp.concatenate([w_ref[side, place, OUT_AT : OUT_AT + HALF, :] for side, place in blocks], axis=0)
    attn = mm(ctx, w_out)

    def norm(values):
        center = values - jnp.mean(values, axis=1, keepdims=True)
        inverse = lax.rsqrt(jnp.mean(center * center, axis=1, keepdims=True) + EPSILON)
        return center * inverse, inverse

    def norm_back(upstream, normed, inverse, gain):
        scaled = upstream * gain
        plain = jnp.mean(scaled, axis=1, keepdims=True)
        cross = jnp.mean(scaled * normed, axis=1, keepdims=True)
        return inverse * (scaled - plain - normed * cross)

    def total(values):
        return jnp.sum(values, axis=0, keepdims=True)

    normed_one, inverse_one = norm(token + attn)
    hidden_one = normed_one * gain_one + bias_one
    low_ref[...] = hidden_one.astype(LOW)

    def columns(c):
        return pl.ds(pl.multiple_of(c * D, D), D)

    def outer_rows(c):
        halves = [second_block(meta_ref, c, half) for half in range(2)]
        return jnp.concatenate([w_ref[side, place, 0 : D // 2, :] for side, place in halves], axis=0)

    def inner_columns(c):
        return jnp.concatenate([in_ref[side, place, :, columns(c)] for side, place in blocks], axis=0)

    def forward_step(c, ffn):
        inner = mm(low_ref[...], inner_columns(c))
        cumulative = 0.5 * (1.0 + lax.erf(inner * 0.5**0.5))
        density = jnp.exp(-0.5 * inner * inner) * 0.3989422804014327
        act = (inner * cumulative).astype(LOW)
        act_ref[c] = act
        slope_ref[c] = cumulative + inner * density
        return ffn + mm(act, outer_rows(c))

    ffn = lax.fori_loop(0, GROUP, forward_step, jnp.zeros((ROWS, D), F32))
    normed_two, inverse_two = norm(hidden_one + ffn)
    layer = (normed_two * gain_two + bias_two) * mask
    out_ref[...] = layer.astype(LOW)
    squares = [token * token * mask, attn * attn * mask, ffn * ffn * mask, layer * layer]
    sums = [jnp.sum(total(s), axis=1, keepdims=True) for s in squares]
    grad_y = up_ref[...].reshape(ROWS, D).astype(F32) * mask
    grad_gain_two = total(grad_y * normed_two)
    grad_bias_two = total(grad_y)
    grad_two = norm_back(grad_y, normed_two, inverse_two, gain_two)
    grad_ffn = grad_two.astype(LOW)

    def back_step(c, grad_hidden):
        grad_act = mm_nt(grad_ffn, outer_rows(c))
        grad_inner = (grad_act * slope_ref[c]).astype(LOW)
        keep, send = select_halves(meta_ref, mm_tn(act_ref[c], grad_ffn))
        for quarter in range(3):
            rows = slice(quarter * QUARTER, (quarter + 1) * QUARTER)
            put_outer(c, quarter, keep[rows], send[rows], 0)
        grad_w = mm_tn(low_ref[...], grad_inner)
        for s in range(GROUP):
            put_inner(s, c, *select_halves(meta_ref, grad_w[s * PIECE : (s + 1) * PIECE]))
        return grad_hidden + mm_nt(grad_inner, inner_columns(c))

    grad_hidden = lax.fori_loop(0, GROUP, back_step, grad_two)
    grad_gain_one = total(grad_hidden * normed_one)
    grad_bias_one = total(grad_hidden)
    grad_one = norm_back(grad_hidden, normed_one, inverse_one, gain_one)
    gres_ref[...] = grad_one
    grad_attn = grad_one.astype(LOW)
    grad_out = mm_tn(ctx, grad_attn)
    for s in range(GROUP):
        put_outer(s, 3, *select_halves(meta_ref, grad_out[s * PIECE : (s + 1) * PIECE]), 0)
    gctx_ref[...] = mm_nt(grad_attn, w_out).astype(LOW)
    lane = iota((1, D), 1)
    stats = jnp.zeros((1, D), F32)
    for i, value in enumerate(sums):
        stats = jnp.where(lane == i, value, stats)
    low = stats - stats.astype(LOW).astype(F32)
    zeros = jnp.zeros((1, D), F32)
    norm_rows = (grad_gain_one, grad_bias_one, grad_gain_two, grad_bias_two)
    for s in range(GROUP):
        row = jnp.concatenate([r[:, s * PIECE : (s + 1) * PIECE] for r in norm_rows], axis=1)
        block = jnp.concatenate([row] + [zeros] * 31 + [stats, low] + [zeros] * 30, axis=0)
        put_outer(s, 3, *select_halves(meta_ref, block), HALF)


def feed(meta, tok, ctx_one, ctx_two, rows, own, pieces):
    shape = jax.ShapeDtypeStruct
    full, anywhere = pl.BlockSpec(memory_space=pltpu.VMEM), pl.BlockSpec(memory_space=pltpu.HBM)
    block, wide = shape((GROUP, GROUP, QUARTER, D), LOW), shape((GROUP, GROUP, HALF, D), LOW)
    return pl.pallas_call(
        feed_body,
        out_shape=(
            shape((ROWS, D), LOW), shape((ROWS, D), LOW), shape((ROWS, D), F32), block, block, wide, wide
        ),
        in_specs=[pl.BlockSpec(memory_space=pltpu.SMEM)] + [full] * 3 + [anywhere] * 15,
        out_specs=(full,) * 7,
        scratch_shapes=[
            pltpu.VMEM((GROUP, PART, D), LOW), pltpu.VMEM((ROWS, D), LOW), pltpu.VMEM((GROUP, ROWS, D), LOW),
            pltpu.VMEM((GROUP, ROWS, D), F32), pltpu.VMEM((2, GROUP, SECOND, D), LOW),
            pltpu.VMEM((2, GROUP, HALF, WIDE), LOW), pltpu.SemaphoreType.DMA((24,)),
        ],
        compiler_params=pltpu.CompilerParams(vmem_limit_bytes=28 * MIB),
        cost_estimate=pl.CostEstimate(flops=16_000_000_000, bytes_accessed=60_000_000, transcendentals=1_600_000),
        name="feed",
    )(meta, tok, ctx_one, ctx_two, rows, *own, *pieces)


def finish_body(
    meta_ref, mine, other, rows_ref,
    q_ref, k_ref, v_ref, rel_ref, outer_ref, wout_ref, inner_ref, g1_ref, b1_ref, g2_ref, b2_ref, rms_ref,
    out_ref, gtok_ref, extra_ref,
):
    for piece, side in ((mine, 0), (other, 1)):
        core = meta_ref[CORE] if side == 0 else 1 - meta_ref[CORE]
        assist = assist_of(meta_ref, core)
        for i, ref in enumerate((q_ref, k_ref, v_ref, rel_ref)):
            size = REL_HALF if i == 3 else HALF
            ref[pl.ds(pl.multiple_of(core * size, size), size), :] = piece[i * HALF : i * HALF + size, :].astype(F32)

        def piece_step(distance, carry):
            quarter = assist ^ distance
            at = pl.multiple_of(FIRST + distance * SPAN, HALF // 3)
            block = piece[pl.ds(at, QUARTER), :].astype(F32)

            @pl.when(quarter < 3)
            def _():
                outer_ref[pl.ds(pl.multiple_of(core * 3 * QUARTER + quarter * QUARTER, QUARTER), QUARTER), :] = block

            @pl.when(quarter == 3)
            def _():
                wout_ref[pl.ds(pl.multiple_of(core * HALF, HALF), HALF), :] = block[:HALF]
                extra_ref[core] = block[HALF:]

            inner_ref[
                pl.ds(pl.multiple_of(core * HALF, HALF), HALF), pl.ds(pl.multiple_of(quarter * D, D), D)
            ] = piece[pl.ds(at + QUARTER, HALF), :].astype(F32)
            return carry

        lax.fori_loop(0, GROUP, piece_step, 0)
    norms = extra_ref[0, 0:1, :]
    for i, ref in enumerate((g1_ref, b1_ref, g2_ref, b2_ref)):
        ref[...] = norms[:, i * PIECE : (i + 1) * PIECE]
    stats = extra_ref[1, 0:1, :] + extra_ref[1, 1:2, :]
    rms_ref[...] = jnp.sqrt(stats[:, :GROUP] * (1.0 / (TOKENS * D)))
    for k in range(GROUP):
        member = meta_ref[X] ^ k
        out_ref[meta_ref[SEQ + k]] = rows_ref[member, 0]
        gtok_ref[meta_ref[SEQ + k]] = rows_ref[member, 1]


def finish(meta, mine, other, rows):
    shape = jax.ShapeDtypeStruct
    full = pl.BlockSpec(memory_space=pltpu.VMEM)
    return pl.pallas_call(
        finish_body,
        out_shape=(
            *(shape((PIECE, D), F32),) * 3, shape((OFFS // GROUP, D), F32),
            shape((D, D), F32), shape((PIECE, D), F32), shape((PIECE, WIDE), F32),
            *(shape((1, PIECE), F32),) * 4, shape((1, GROUP), F32),
            *(shape((GROUP, PART, D), LOW),) * 2,
        ),
        in_specs=[pl.BlockSpec(memory_space=pltpu.SMEM)] + [full] * 3,
        out_specs=(full,) * 14,
        scratch_shapes=[pltpu.VMEM((2, QUARTER - HALF, D), F32)],
        compiler_params=pltpu.CompilerParams(vmem_limit_bytes=24 * MIB),
        name="finish",
    )(meta, mine, other, rows)


NEAR, FAR = (1, 3), (3, 1)


def hop_x(value, flips):
    pairs = [(c * 4 + i, c * 4 + (i ^ flips[c])) for c in range(2) for i in range(4)]
    return lax.ppermute(value, ("core", "shard"), pairs)


def hop_yz(value, flip, swapped=False):
    pairs = []
    for y in range(4):
        for z in range(4):
            for c in range(2):
                along_y = (c == 0) != swapped
                ty, tz = (y ^ flip, z) if along_y else (y, z ^ flip)
                pairs.append(((y * 4 + z) * 2 + c, (ty * 4 + tz) * 2 + c))
    return lax.ppermute(value, ("y", "z", "core"), pairs)


def swap(value):
    return lax.ppermute(value, "core", [(0, 1), (1, 0)])


def after(value, *others):
    return lax.optimization_barrier((value, *others))[0]


def add(*values):
    total = values[0].astype(F32)
    for value in values[1:]:
        total = total + value.astype(F32)
    return total.astype(LOW)


def exchange_rows(rows):
    return lax.all_to_all(rows, "shard", split_axis=0, concat_axis=0, tiled=True)


def shards(
    hidden, grad_out, lengths, bucket, w_query, w_key, w_value, w_out, w_inner, w_outer, rel_table,
    ln1_gain, ln1_bias, ln2_gain, ln2_bias,
):
    coords = jnp.stack([lax.axis_index(name) for name in ("shard", "y", "z", "core")]).astype(jnp.int32)
    norm_block = jnp.concatenate(
        [jnp.concatenate([ln1_gain, ln1_bias, ln2_gain, ln2_bias])[None], jnp.zeros((31, D), LOW)], axis=0
    )
    bucket_column = jnp.concatenate([bucket[::-1], jnp.full((1,), -1, jnp.int32)])[:, None]
    own_first = (w_query, w_key, w_value, rel_table)
    own_halves = tuple(
        pltpu.with_memory_space_constraint(ref.reshape(2, ref.shape[0] // 2, D), pltpu.HBM) for ref in own_first
    )
    meta, first, second, rows = pack(
        coords, lengths, hidden, grad_out, own_first, (w_outer, w_out, w_inner), norm_block
    )
    near_two, far_two = hop_x(second, NEAR), hop_x(second, FAR)
    near, far = hop_x(first, NEAR), hop_x(first, FAR)
    rows = exchange_rows(rows)
    across_two = hop_x(near_two, FAR)
    base = after(jnp.stack([near_two, far_two, across_two]), near, far)
    base_near, base_far = hop_yz(base, 1), hop_yz(base, 3)
    across = hop_x(near, FAR)
    pieces = (near, far, across, swap(near), swap(far), swap(across))
    part_outer, part_inner = cut(base_near, base_far)
    rows = after(rows, part_outer, part_inner)
    across_outer, across_inner = hop_yz(part_outer, 3), hop_yz(part_inner, 1)
    tok, *saved, relw, probs, ctx = attend_forward(meta, bucket_column, rows, own_halves, pieces)
    across_outer, across_inner, base, base_near, base_far, _ = lax.optimization_barrier(
        (across_outer, across_inner, base, base_near, base_far, ctx)
    )
    arrived = (base, base_near, base_far, across_outer, across_inner)
    swapped = tuple(swap(piece) for piece in arrived)
    probs_two, ctx_two = attend_forward_two(meta, saved)
    swapped = after(swapped, ctx_two)
    out, gctx, gres, keep, send, keep_in, send_in = feed(
        meta, tok, ctx, ctx_two, rows, (w_outer, w_out, norm_block, w_inner), (*arrived, *swapped)
    )
    other, other_in = swap(send), swap(send_in)
    half_done = attend_back_one((*saved, probs), gctx)
    leave = add(keep[:2], other[:2])
    leave_in = add(keep_in[:2], other_in[:2])
    came, came_in = hop_yz(leave, 1), hop_yz(leave_in, 3)
    half_done = after(tuple(half_done), leave, leave_in)
    leaving, keep_one, send_one = attend_back_two(
        meta, (*saved, probs_two), gctx, half_done, tok, relw, gres, bucket_column, own_halves, pieces, out
    )
    other_one = swap(after(send_one, came, came_in))
    leave_one = add(keep_one[:2], other_one[:2])
    came, came_in = after((came, came_in), leave_one)
    last = hop_yz(add(keep[2], other[2], came[0]), 3)
    last_in = hop_yz(add(keep_in[2], other_in[2], came_in[0]), 1)
    came_one = hop_x(leave_one, NEAR)
    came_one = after(came_one, last, last_in)
    leave_two = add(keep_one[2], other_one[2], came_one[0])
    last_one = hop_x(leave_two, FAR)
    last, last_in, _ = lax.optimization_barrier((last, last_in, leave_two))
    mine = add(keep[3], other[3], came[1], last)
    mine_in = add(keep_in[3], other_in[3], came_in[1], last_in)
    both = jnp.concatenate([mine, mine_in], axis=1)
    came_x = hop_x(both[:2], NEAR)
    home = exchange_rows(leaving)
    mine_one = add(keep_one[3], other_one[3], came_one[1], last_one)
    come_one = hop_yz(mine_one, 1, swapped=True)
    last_x = hop_x(after(add(both[2], came_x[0]), mine_one), FAR)
    mine_one = add(mine_one, after(come_one, last_x))
    come_one = hop_yz(mine_one, 3, swapped=True)
    both = after(add(both[3], came_x[1], last_x), mine_one)
    step = hop_yz(both, 1, swapped=True)
    mine_one = add(mine_one, after(come_one, step))
    come_one = hop_yz(mine_one, 1)
    both = after(add(both, step), mine_one)
    step = hop_yz(both, 3, swapped=True)
    mine_one = add(mine_one, after(come_one, step))
    come_one = hop_yz(mine_one, 3)
    both = after(add(both, step), mine_one)
    both = [both, *(hop_yz(both, flip) for flip in (1, 3, 2))]
    both[1], both[2], both[3] = both[1], both[3], both[2]
    mine_one = add(mine_one, come_one)
    packed = after(jnp.concatenate([mine_one, *both], axis=0), home)
    q_grad, k_grad, v_grad, rel_grad, outer_grad, out_grad, inner_grad, *small, layer_output, grad_hidden = finish(
        meta, packed, swap(packed), home
    )
    return (
        layer_output, grad_hidden, q_grad, k_grad, v_grad, out_grad, inner_grad, outer_grad, rel_grad,
        *(row[0] for row in small),
    )


def solution(mesh):
    split = Mesh(mesh.devices.reshape(4, 4, 2, 4), ("y", "z", "core", "shard"))
    rep = ("y", "z", "core")
    rows, vector = P("shard", None), P("shard")
    batch = P(rep, "shard", None)
    return jax.shard_map(
        shards,
        mesh=split,
        in_specs=(batch, batch, P(rep), P(), *(rows,) * 7, *(vector,) * 4),
        out_specs=(batch, batch, *(rows,) * 7, *(vector,) * 4, P()),
        check_vma=False,
    )
```
